32 devices in a mesh: member: 4 (over x, core), space: 8 (over z, y).
Axes of the slice: x: 2, y: 2, z: 4, core: 2. Of those that a mesh axis runs over, the one named last changes fastest.
Arguments:
- spectra: float32 [16, 12, 320, 641], P('member', None, 'space'), may hold values from -6 to 6
- legendre: bfloat16 [320, 641, 384], P('space'), as said below
- sin_lat: float32 [384], replicated, may hold values from 0 to 1, as said below
- gravity: float32 [2, 2], replicated, may hold values from 0.1 to 2, as said below
- stability: float32 [2, 2], replicated, may hold values from 0.1 to 2, as said below
- clones: int32 [2, 2], replicated, may hold values from 0 to 15, as said below
Outputs:
- new_state: float32 [16, 12, 320, 641], P('member', None, 'space')
The draws below stay inside these ranges and needn't reach their ends.
Inputs may be any that keep to these rules, and one draw needn't show every extreme that they name: `clones`: column 0 holds 2 distinct killed trajectories, column 1 for each a survivor; no survivor is killed, and a survivor may be copied onto several killed trajectories. legendre[p, j, l] is the associated Legendre function of the (m, n) of position (p, j), normalized so that its square integrates to one over -1 to 1, at mu = sin_lat[l]. `sin_lat`: decreasing from the pole towards the equator. `gravity`: diagonal entries 1 to 2, off-diagonal entries 0.1 to 0.6. `stability`: diagonal entries 1 to 2, off-diagonal entries 0.1 to 0.6.
All inputs are finite; a program needn't handle non-finite values.
Results may differ from the reference program's by a relative error of at most 0.0016.
Values may be sent and summed in bfloat16 or wider, within the bound.
No kernel may reach another device: no remote copies, remote signals or barrier semaphores. Data moves between devices by JAX's collectives and lax.ppermute only.
A program may use at most 192 MiB of HBM per device.

```python
import math
import jax
import jax.numpy as jnp
from jax import lax

NW = 640
NLAT = 768
NLON = 1280
TRAJ_DEV = 4
PAIRS = 320
NHALF = 384
MEMBERS = 16
KILLED = 2


def latitude_sines(key):
    jitter = jax.random.uniform(jax.random.fold_in(key, 11), (NHALF,), jnp.float32, -0.35, 0.35)
    colatitude = math.pi * (jnp.arange(NHALF, dtype=jnp.float32) + 0.5 + jitter) / NLAT
    return jnp.cos(colatitude)


def draw_sin_lat(key, part):
    return latitude_sines(key)


def draw_legendre(key, part):
    cosine = latitude_sines(key)[None, :]
    sine_theta = jnp.sqrt(1.0 - cosine * cosine)
    factor_index = jnp.arange(1, NW, dtype=jnp.float32)
    log_factor = jnp.concatenate([jnp.zeros((1,), jnp.float32), jnp.cumsum(jnp.log((2.0 * factor_index + 1.0) / (2.0 * factor_index)))])
    pair_index = jnp.arange(PAIRS, dtype=jnp.int32)[:, None]

    def advance_row(carry, column):
        latest, before = carry
        leading = column < NW - pair_index
        wave_order = jnp.where(leading, pair_index, NW - 1 - pair_index)
        offset = jnp.where(leading, column, column - (NW - pair_index))
        order_real = wave_order.astype(jnp.float32)
        degree = (wave_order + offset).astype(jnp.float32)
        diagonal = jnp.exp(0.5 * jnp.log(0.5) + 0.5 * log_factor[wave_order] + order_real * jnp.log(sine_theta))
        second = jnp.sqrt(2.0 * order_real + 3.0) * cosine * latest
        prior = degree - 1.0
        span_now = jnp.where(offset >= 2, degree * degree - order_real * order_real, 1.0)
        span_prior = jnp.where(offset >= 2, prior * prior - order_real * order_real, 1.0)
        ahead = jnp.sqrt(jnp.maximum(4.0 * degree * degree - 1.0, 1.0) / span_now)
        behind = jnp.sqrt(jnp.maximum(4.0 * prior * prior - 1.0, 1.0) / span_prior)
        general = ahead * (cosine * latest - before / behind)
        value = jnp.where(offset == 0, diagonal, jnp.where(offset == 1, second, general))
        return ((value, latest), value)
    zero_initial_state = jnp.zeros((PAIRS, NHALF), jnp.float32)
    final_carry, stacked = lax.scan(advance_row, (zero_initial_state, zero_initial_state), jnp.arange(NW + 1, dtype=jnp.int32))
    return jnp.transpose(stacked, (1, 0, 2)).astype(jnp.bfloat16)


def coupling_matrix(key):
    diagonal = jax.random.uniform(jax.random.fold_in(key, 1), (2,), jnp.float32, 1.0, 2.0)
    crossed = jax.random.uniform(jax.random.fold_in(key, 2), (2,), jnp.float32, 0.1, 0.6)
    return jnp.stack([jnp.stack([diagonal[0], crossed[0]]), jnp.stack([crossed[1], diagonal[1]])])


def draw_gravity(key, part):
    return coupling_matrix(jax.random.fold_in(key, 21))


def draw_stability(key, part):
    return coupling_matrix(jax.random.fold_in(key, 22))


def draw_clones(key, part):
    groups = MEMBERS // TRAJ_DEV
    base = jax.random.randint(jax.random.fold_in(key, 7), (), 0, groups).astype(jnp.int32)
    order = jax.random.permutation(jax.random.fold_in(key, 3), MEMBERS).astype(jnp.int32)
    index_all = jnp.arange(MEMBERS, dtype=jnp.int32)
    group_of = index_all // TRAJ_DEV
    near_row = (base + 1) % groups * TRAJ_DEV + jax.random.randint(jax.random.fold_in(key, 8), (), 0, TRAJ_DEV).astype(jnp.int32)
    far_row = (base + groups // 2) % groups * TRAJ_DEV + jax.random.randint(jax.random.fold_in(key, 9), (), 0, TRAJ_DEV).astype(jnp.int32)
    scores = jnp.where(group_of == base, order + MEMBERS, order)
    scores = jnp.where(index_all == near_row, -2, jnp.where(index_all == far_row, -1, scores))
    ranked = jnp.argsort(scores, stable=True).astype(jnp.int32)
    removed_members = ranked[:KILLED]
    alive_members = ranked[KILLED:]
    count_alive = MEMBERS - KILLED
    pick_one = jax.random.randint(jax.random.fold_in(key, 4), (KILLED,), 0, count_alive)
    pick_two = jax.random.randint(jax.random.fold_in(key, 5), (KILLED,), 0, count_alive)
    pick_three = jax.random.randint(jax.random.fold_in(key, 6), (KILLED,), 0, count_alive)
    selected_members = jnp.minimum(jnp.minimum(pick_one, pick_two), pick_three)
    remaining_members = alive_members[selected_members].astype(jnp.int32)
    owned_rows_list = base * TRAJ_DEV + jax.random.randint(jax.random.fold_in(key, 10), (2,), 0, TRAJ_DEV).astype(jnp.int32)
    remaining_members = jnp.concatenate([owned_rows_list, remaining_members[2:]])
    return jnp.stack([removed_members, remaining_members], axis=1).astype(jnp.int32)


def level_of(key, dims, shards, smallest, top_value):
    def one(dim, parts):
        draws = jax.random.uniform(jax.random.fold_in(jax.random.fold_in(key, 6), dim), (parts,), jnp.float32, smallest / len(shards), top_value / len(shards))
        return jnp.repeat(jnp.exp(draws), dims[dim] // parts).reshape((-1,) + (1,) * (len(dims) - dim - 1))

    factor_of = one(*shards[0])
    for cut in shards[1:]:
        factor_of = factor_of * one(*cut)
    return factor_of


def gaussian(rng, dims, scale, most, cuts=(), held_as=jnp.bfloat16):
    loudness = level_of(rng, dims, cuts, -0.22, 0.18) if cuts else 1.0
    entries = jax.random.normal(rng, dims, jnp.float32) * scale * loudness
    return jnp.minimum(jnp.maximum(entries, -most), most).astype(held_as)


def setup_inputs(seed: int = 0) -> dict:
    streams_of = jax.random.split(jax.random.key(seed), 7)
    spectra = gaussian(streams_of[0], (MEMBERS, 12, PAIRS, NW + 1), 1.0, 6.0, ((0, 4), (2, 8)), jnp.float32)
    legendre = draw_legendre(jax.random.fold_in(streams_of[6], 71), 0)
    sin_lat = draw_sin_lat(jax.random.fold_in(streams_of[6], 71), 0)
    gravity = draw_gravity(jax.random.fold_in(streams_of[6], 71), 0)
    stability = draw_stability(jax.random.fold_in(streams_of[6], 71), 0)
    clones = draw_clones(jax.random.fold_in(streams_of[6], 71), 0)
    return {"spectra": spectra, "legendre": legendre, "sin_lat": sin_lat, "gravity": gravity, "stability": stability, "clones": clones}


time_step = 0.25
wave_scale = 16.0
diffusion = 0.02

def pair_layout(pair_index, row_length, truncation):
    column = jnp.arange(row_length, dtype=jnp.int32)[None, :]
    lower_pair = pair_index[:, None]
    leading = column < truncation - lower_pair
    wave_order = jnp.where(leading, lower_pair, truncation - 1 - lower_pair)
    offset = jnp.where(leading, column, column - (truncation - lower_pair))
    parity = (1 - 2 * (offset % 2)).astype(jnp.float32)
    return (leading.astype(jnp.float32), parity, wave_order + offset)

def fourier_table(pair_count, truncation, longitudes):
    halves = jnp.arange(2, dtype=jnp.int32)[:, None]
    pair_all = jnp.arange(pair_count, dtype=jnp.int32)[None, :]
    wave_order = jnp.where(halves == 0, pair_all, truncation - 1 - pair_all)
    column = jnp.arange(longitudes, dtype=jnp.int32)
    phase = wave_order[:, :, None] * column[None, None, :] % longitudes
    angle = phase.astype(jnp.float32) * (2.0 * math.pi / longitudes)
    return jnp.stack([jnp.cos(angle), -jnp.sin(angle)]).astype(jnp.bfloat16)

def legendre_input(spectra, leading, parity):
    rounded = spectra.astype(jnp.bfloat16)
    halves = jnp.stack([leading, 1.0 - leading])
    mirror_sign = jnp.stack([jnp.ones_like(parity), parity])
    factor = (halves[:, None] * mirror_sign[None, :]).astype(jnp.bfloat16)
    return rounded[:, :, None, None] * factor[None, None]

def combine_halves(projected, leading, parity):
    first_part = projected[:, :, 0, 0] + parity * projected[:, :, 0, 1]
    second_part = projected[:, :, 1, 0] + parity * projected[:, :, 1, 1]
    return leading * first_part + (1.0 - leading) * second_part

def latitude_terms(sin_lat, first_row, count):
    mirrored = jnp.concatenate([sin_lat, -sin_lat])
    local_sine = lax.dynamic_slice_in_dim(mirrored, first_row, count)
    weights = math.pi * jnp.sqrt(1.0 - local_sine * local_sine) / mirrored.shape[0]
    return (2.0 * local_sine, weights)

def tendencies(physical_grid_samples, coriolis):
    local_spin_spectrum = physical_grid_samples[:, 0:2]
    spreading_rate_spectrum = physical_grid_samples[:, 2:4]
    thermal_spectrum = physical_grid_samples[:, 4:6]
    planetary_spin_spectrum = local_spin_spectrum + coriolis[:, None]
    average_heat_level = 0.5 * (thermal_spectrum[:, 0:1] + thermal_spectrum[:, 1:2])
    return jnp.concatenate([-planetary_spin_spectrum * spreading_rate_spectrum, planetary_spin_spectrum * local_spin_spectrum - 0.5 * spreading_rate_spectrum * spreading_rate_spectrum, -(thermal_spectrum + average_heat_level) * spreading_rate_spectrum], axis=1)

def semi_implicit(spectra, tendency, degree, gravity, stability):
    trajectory_count, comp_count, pair_count, row_length = spectra.shape
    truncation = row_length - 1
    shaped = spectra.reshape(trajectory_count, comp_count // 2, 2, pair_count, row_length)
    forcing = tendency.reshape(trajectory_count, comp_count // 2, 2, pair_count, row_length)
    eigen_value = wave_scale * (degree * (degree + 1)).astype(jnp.float32) / float(truncation * truncation)
    damping = 1.0 / (1.0 + diffusion * eigen_value * eigen_value)
    coupling = time_step * time_step * eigen_value
    product = jnp.dot(gravity, stability, precision=lax.Precision.HIGHEST)
    new_zeta = damping * (shaped[:, 0:2] + time_step * forcing[:, 0:2])
    t_star = shaped[:, 4:6] + time_step * forcing[:, 4:6]
    d_star = shaped[:, 2:4] + time_step * forcing[:, 2:4]
    right_one = d_star[:, 0] + time_step * eigen_value * (gravity[0, 0] * t_star[:, 0] + gravity[0, 1] * t_star[:, 1])
    right_two = d_star[:, 1] + time_step * eigen_value * (gravity[1, 0] * t_star[:, 0] + gravity[1, 1] * t_star[:, 1])
    diag_one = 1.0 + coupling * product[0, 0]
    diag_two = 1.0 + coupling * product[1, 1]
    cross_one = coupling * product[0, 1]
    cross_two = coupling * product[1, 0]
    determ = diag_one * diag_two - cross_one * cross_two
    div_one = (diag_two * right_one - cross_one * right_two) / determ
    div_two = (diag_one * right_two - cross_two * right_one) / determ
    temp_one = damping * (t_star[:, 0] - time_step * (stability[0, 0] * div_one + stability[0, 1] * div_two))
    temp_two = damping * (t_star[:, 1] - time_step * (stability[1, 0] * div_one + stability[1, 1] * div_two))
    new_div = damping * jnp.stack([div_one, div_two], axis=1)
    new_temp = jnp.stack([temp_one, temp_two], axis=1)
    result = jnp.concatenate([new_zeta, new_div, new_temp], axis=1)
    return result.reshape(spectra.shape)

def reference(spectra, legendre, sin_lat, gravity, stability, clones):
    leading, parity, degree = pair_layout(jnp.arange(PAIRS, dtype=jnp.int32), NW + 1, NW)
    zonal_table = fourier_table(PAIRS, NW, NLON).astype(jnp.float32)
    coriolis, weights = latitude_terms(sin_lat, 0, NLAT)
    legendre_wide = legendre.astype(jnp.float32)

    def advance_one(spectrum):
        spectrum = spectrum[None]
        inputs_wide = legendre_input(spectrum, leading, parity).astype(jnp.float32)
        fourier = jnp.einsum('tchqpj,pjl->tchpql', inputs_wide, legendre_wide)
        fourier = fourier.reshape(1, 12, 2, PAIRS, NLAT).astype(jnp.bfloat16)
        banded = fourier.astype(jnp.float32).reshape(1, 6, 2, 2, PAIRS, NLAT)
        physical_grid_samples = jnp.einsum('tfrhpl,rhpk->tflk', banded, zonal_table) * (1.0 / NW)
        forcing = tendencies(physical_grid_samples, coriolis).astype(jnp.bfloat16)
        weighted = jnp.einsum('tflk,rhpk->tfrhpl', forcing.astype(jnp.float32), zonal_table) * weights
        weighted = weighted.astype(jnp.bfloat16).astype(jnp.float32)
        returned = weighted.reshape(1, 12, 2, PAIRS, 2, NHALF)
        projected = jnp.einsum('tchpql,pjl->tchqpj', returned, legendre_wide)
        tendency = combine_halves(projected, leading, parity)
        return semi_implicit(spectrum, tendency, degree, gravity, stability)[0]
    advanced_states = lax.map(advance_one, spectra)
    return advanced_states.at[clones[:, 0]].set(advanced_states[clones[:, 1]])
```

```python
import functools
import math

import jax
import jax.numpy as jnp
from jax import lax
from jax.experimental import pallas as pl
from jax.experimental.pallas import tpu as pltpu
from jax.sharding import PartitionSpec as P

LANES = 128
SUB = 8
LONGITUDES_PER_WAVE = 2

time_step = 0.25
wave_scale = 16.0
diffusion = 0.02


def layout_terms(first_pair, count, lane0, lanes, truncation):
    pair = first_pair + lax.broadcasted_iota(jnp.int32, (count, lanes), 0)
    column = lane0 + lax.broadcasted_iota(jnp.int32, (count, lanes), 1)
    leading = column < truncation - pair
    offset = jnp.where(leading, column, column - (truncation - pair))
    order = jnp.where(leading, pair, truncation - 1 - pair)
    return leading, (offset & 1) == 1, order + offset


def load_legendre(leg_ref, wide, row_length):
    block = leg_ref.shape[1]
    tiles = leg_ref.shape[2] // LANES
    for k in range(tiles):
        wide[k, : row_length * block, :] = (
            leg_ref[:, :, k * LANES : (k + 1) * LANES]
            .astype(jnp.float32)
            .reshape(row_length * block, LANES)
        )


def clear_tail(wide, row_length, block):
    for k in range(wide.shape[0]):
        wide[k, row_length * block :, :] = jnp.zeros(
            (wide.shape[1] - row_length * block, LANES), jnp.float32
        )


def forward_kernel(where_ref, spec_ref, leg_ref, out_ref, wide, xs, res, *, truncation, pairs):
    step = pl.program_id(0)
    row_length = truncation + 1
    trajectories, comps, block, _ = spec_ref.shape
    rows = trajectories * comps
    tiles = xs.shape[0]
    padded = tiles * LANES

    @pl.when(step == 0)
    def _():
        clear_tail(wide, row_length, block)

    load_legendre(leg_ref, wide, row_length)
    for k in range(tiles):
        width = min(LANES, row_length - k * LANES)
        piece = spec_ref[:, :, :, k * LANES : k * LANES + width].reshape(rows * block, width)
        if width < LANES:
            xs[k] = jnp.zeros((rows * block, LANES), jnp.float32)
            xs[k, :, :width] = piece
        else:
            xs[k] = piece

    first_pair = where_ref[0] + step * block

    def one(q, carry):
        x = jnp.concatenate(
            [xs[k, pl.ds(q, rows, stride=block), :] for k in range(tiles)], axis=1
        )
        leading, odd, _ = layout_terms(first_pair + q, 1, 0, padded, truncation)
        lead = jnp.where(leading, x, 0.0)
        trail = jnp.where(leading, 0.0, x)
        lhs = jnp.concatenate(
            [lead, trail, jnp.where(odd, -lead, lead), jnp.where(odd, -trail, trail)], axis=0
        ).astype(jnp.bfloat16)
        rhs = wide[0, pl.ds(q, padded, stride=block), :].astype(jnp.bfloat16)
        got = jnp.dot(lhs, rhs, preferred_element_type=jnp.float32)
        res[pl.ds(step * block + q, 4 * rows, stride=pairs), :] = got
        return carry

    lax.fori_loop(0, block, one, 0)

    @pl.when(step == pl.num_programs(0) - 1)
    def _():
        for t in range(trajectories):
            for s in range(2):
                for f in range(comps // 2):
                    parts = []
                    for r in range(2):
                        for h in range(2):
                            row = ((s * 2 + h) * rows + t * comps + 2 * f + r) * pairs
                            parts.append(res[row : row + pairs, :])
                    out_ref[t * 2 + s, f] = jnp.concatenate(parts, axis=0).astype(jnp.bfloat16)


def grid_kernel(cor_ref, weight_ref, in_ref, syn_ref, ana_ref, out_ref, modes, force, *, scale):
    sources, fields, rows, lanes = in_ref.shape
    longitudes = syn_ref.shape[0]
    for d in range(sources):
        for f in range(fields):
            modes[d * rows : (d + 1) * rows, f * lanes : (f + 1) * lanes] = in_ref[d, f]
    cor = cor_ref[...]
    weight = weight_ref[...]
    span = 128

    def synth(b, carry):
        at = pl.multiple_of(b * span, span)
        g = (
            jnp.dot(syn_ref[pl.ds(at, span), :], modes[...], preferred_element_type=jnp.float32)
            * scale
        )
        field = [g[:, f * lanes : (f + 1) * lanes] for f in range(fields)]
        mean = 0.5 * (field[4] + field[5])
        out = [None] * fields
        for a in range(2):
            spin = field[a] + cor
            div = field[2 + a]
            out[a] = -spin * div
            out[2 + a] = spin * field[a] - 0.5 * div * div
            out[4 + a] = -(field[4 + a] + mean) * div
        for f in range(fields):
            force[pl.ds(at, span), f * lanes : (f + 1) * lanes] = out[f].astype(jnp.bfloat16)
        return carry

    lax.fori_loop(0, longitudes // span, synth, 0)

    def analyse(d, carry):
        at = pl.multiple_of(d * rows, 16)
        w = jnp.dot(ana_ref[pl.ds(at, rows), :], force[...], preferred_element_type=jnp.float32)
        for f in range(fields):
            out_ref[d, f] = (w[:, f * lanes : (f + 1) * lanes] * weight).astype(jnp.bfloat16)
        return carry

    lax.fori_loop(0, sources, analyse, 0)


def semi_implicit_slabs(old, tend, degree, gm, hm, truncation):
    eig = wave_scale * (degree * (degree + 1)).astype(jnp.float32) / float(truncation * truncation)
    damping = 1.0 / (1.0 + diffusion * eig * eig)
    coupling = time_step * time_step * eig
    pm = [[gm[a][0] * hm[0][b] + gm[a][1] * hm[1][b] for b in range(2)] for a in range(2)]
    diag_one = 1.0 + coupling * pm[0][0]
    diag_two = 1.0 + coupling * pm[1][1]
    cross_one = coupling * pm[0][1]
    cross_two = coupling * pm[1][0]
    inverse = 1.0 / (diag_one * diag_two - cross_one * cross_two)
    out = [None] * 12
    for r in range(2):
        star = [old[c * 2 + r] + time_step * tend[c * 2 + r] for c in range(6)]
        right = [
            star[2 + a] + time_step * eig * (gm[a][0] * star[4] + gm[a][1] * star[5])
            for a in range(2)
        ]
        div = [
            (diag_two * right[0] - cross_one * right[1]) * inverse,
            (diag_one * right[1] - cross_two * right[0]) * inverse,
        ]
        for a in range(2):
            out[a * 2 + r] = damping * star[a]
            out[(2 + a) * 2 + r] = damping * div[a]
            out[(4 + a) * 2 + r] = damping * (
                star[4 + a] - time_step * (hm[a][0] * div[0] + hm[a][1] * div[1])
            )
    return out


def inverse_kernel(where_ref, gravity_ref, stability_ref, *refs, truncation, pairs, chunks, last):
    w_refs, refs = refs[:chunks], refs[chunks:]
    leg_refs, refs = refs[:chunks], refs[chunks:]
    if last:
        part_ref, spec_ref, out_ref, wide, ws, ten = refs
    else:
        out_ref, wide, ws, ten = refs
    step = pl.program_id(0)
    row_length = truncation + 1
    trajectories, comps, block, _ = out_ref.shape
    rows = trajectories * comps
    tiles = ten.shape[0]
    padded = tiles * LANES

    @pl.when(step == 0)
    def _():
        clear_tail(wide, row_length, block)
        for k in range(chunks):
            for t in range(trajectories):
                for s in range(2):
                    for f in range(comps // 2):
                        got = w_refs[k][t * 2 + s, f].astype(jnp.float32)
                        for r in range(2):
                            for h in range(2):
                                row = ((s * 2 + h) * rows + t * comps + 2 * f + r) * pairs
                                at = (r * 2 + h) * pairs
                                ws[k, row : row + pairs, :] = got[at : at + pairs, :]

    for k in range(chunks):
        wide[k, : row_length * block, :] = (
            leg_refs[k][...].astype(jnp.float32).reshape(row_length * block, LANES)
        )
    first_pair = where_ref[0] + step * block

    def one(q, carry):
        got = None
        for k in range(chunks):
            lhs = ws[k, pl.ds(step * block + q, 4 * rows, stride=pairs), :].astype(jnp.bfloat16)
            rhs = wide[k, pl.ds(q, padded, stride=block), :].astype(jnp.bfloat16)
            term = lax.dot_general(
                lhs, rhs, (((1,), (1,)), ((), ())), preferred_element_type=jnp.float32
            )
            got = term if got is None else got + term
        leading, odd, _ = layout_terms(first_pair + q, 1, 0, padded, truncation)
        north = jnp.where(leading, got[:rows], got[rows : 2 * rows])
        south = jnp.where(leading, got[2 * rows : 3 * rows], got[3 * rows :])
        total = north + jnp.where(odd, -south, south)
        for k in range(tiles):
            ten[k, pl.ds(q, rows, stride=block), :] = total[:, k * LANES : (k + 1) * LANES]
        return carry

    lax.fori_loop(0, block, one, 0)

    if last:
        gm = [[gravity_ref[a, b] for b in range(2)] for a in range(2)]
        hm = [[stability_ref[a, b] for b in range(2)] for a in range(2)]
    for k in range(tiles):
        width = min(LANES, row_length - k * LANES)
        lanes = slice(k * LANES, k * LANES + width)
        if last:
            _, _, degree = layout_terms(first_pair, block, k * LANES, width, truncation)

        def body(t, carry):
            tend = []
            for c in range(comps):
                at = pl.multiple_of((t * comps + c) * block, SUB)
                value = ten[k, pl.ds(at, block), :][:, :width]
                tend.append(value)
            if last:
                tend = [tend[c] + part_ref[t, c, :, lanes] for c in range(comps)]
                old = [spec_ref[t, c, :, lanes] for c in range(comps)]
                tend = semi_implicit_slabs(old, tend, degree, gm, hm, truncation)
            for c in range(comps):
                out_ref[t, c, :, lanes] = tend[c]
            return carry

        lax.fori_loop(0, trajectories, body, 0)


def fourier_tables(pair_count, groups, truncation, longitudes):
    index = jnp.arange(pair_count * 4, dtype=jnp.int32)
    local = pair_count // groups
    group = index // (4 * local)
    part = index // (2 * local) % 2
    half = index // local % 2
    pair = group * local + index % local
    order = jnp.where(half == 0, pair, truncation - 1 - pair)
    phase = order[:, None] * jnp.arange(longitudes, dtype=jnp.int32)[None, :] % longitudes
    angle = phase.astype(jnp.float32) * (2.0 * math.pi / longitudes)
    return jnp.where(part[:, None] == 0, jnp.cos(angle), -jnp.sin(angle)).astype(jnp.bfloat16)


def cloned_rows(spectra, clones):
    local = spectra.shape[0]
    members = lax.axis_size("member")
    got = []
    for i in range(clones.shape[0]):
        source = clones[i, 1] // local
        target = clones[i, 0] // local
        row = lax.dynamic_index_in_dim(spectra, clones[i, 1] % local, 0, keepdims=False)

        def move(a, b):
            if a == b:
                return lambda v: v
            return lambda v: lax.ppermute(v, "member", [(a, b)])

        branches = [move(a, b) for a in range(members) for b in range(members)]
        got.append(lax.switch(source * members + target, branches, row))
    return got


def replace_rows(spectra, rows, clones):
    local = spectra.shape[0]
    me = lax.axis_index("member")
    index = jnp.arange(local, dtype=jnp.int32)
    for i, row in enumerate(rows):
        mine = jnp.logical_and(clones[i, 0] // local == me, index == clones[i, 0] % local)
        spectra = jnp.where(mine[:, None, None, None], row[None], spectra)
    return spectra


def shards(spectra, legendre, sin_lat, gravity, stability, clones):
    trajectories, comps, pairs, row_length = spectra.shape
    truncation = row_length - 1
    half_lat = legendre.shape[2]
    longitudes = LONGITUDES_PER_WAVE * truncation
    space = lax.axis_size("space")
    position = lax.axis_index("space")
    fields = comps // 2
    split = space // (2 * trajectories)
    lane_count = LANES // split
    chunk_count = half_lat // LANES
    padded_pairs = -(-pairs // SUB) * SUB
    steps = padded_pairs // SUB
    tiles = -(-row_length // LANES)
    extra = padded_pairs - pairs
    rows = trajectories * comps

    state = replace_rows(spectra, cloned_rows(spectra, clones), clones)
    columns = jnp.transpose(legendre, (1, 0, 2))
    if extra:
        state = jnp.pad(state, ((0, 0), (0, 0), (0, extra), (0, 0)))
        columns = jnp.pad(columns, ((0, 0), (0, extra), (0, 0)))
    where = (position * pairs).astype(jnp.int32).reshape(1)

    smem = pl.BlockSpec(memory_space=pltpu.SMEM)
    state_spec = pl.BlockSpec((trajectories, comps, SUB, row_length), lambda i: (0, 0, i, 0))
    wire_shape = (2 * trajectories, fields, 4 * padded_pairs, LANES)
    wire_spec = pl.BlockSpec(wire_shape, lambda i: (0, 0, 0, 0))

    def leg_spec(k):
        return pl.BlockSpec((row_length, SUB, LANES), lambda i: (0, i, k))

    limit = 60 * 1024 * 1024

    def forward(k):
        return pl.pallas_call(
            functools.partial(forward_kernel, truncation=truncation, pairs=padded_pairs),
            out_shape=jax.ShapeDtypeStruct(wire_shape, jnp.bfloat16),
            grid=(steps,),
            in_specs=[smem, state_spec, leg_spec(k)],
            out_specs=wire_spec,
            scratch_shapes=[
                pltpu.VMEM((1, tiles * LANES * SUB, LANES), jnp.float32),
                pltpu.VMEM((tiles, rows * SUB, LANES), jnp.float32),
                pltpu.VMEM((4 * rows * padded_pairs, LANES), jnp.float32),
            ],
            compiler_params=pltpu.CompilerParams(vmem_limit_bytes=limit),
            cost_estimate=pl.CostEstimate(
                flops=8 * rows * padded_pairs * row_length * LANES,
                bytes_accessed=16 * 1024 * 1024,
                transcendentals=0,
            ),
            name="forward",
        )(where, state, columns)

    def to_wire(x):
        if extra:
            x = x.reshape(2 * trajectories, fields, 4, padded_pairs, LANES)[:, :, :, :pairs]
            x = x.reshape(2 * trajectories, fields, 4 * pairs, LANES)
        if split > 1:
            x = x.reshape(2 * trajectories, fields, 4 * pairs, split, lane_count)
            x = jnp.transpose(x, (0, 3, 1, 2, 4)).reshape(space, fields, 4 * pairs, lane_count)
        return x

    def from_wire(x):
        if split > 1:
            x = x.reshape(2 * trajectories, split, fields, 4 * pairs, lane_count)
            x = jnp.transpose(x, (0, 2, 3, 1, 4))
            x = x.reshape(2 * trajectories, fields, 4 * pairs, LANES)
        if extra:
            x = x.reshape(2 * trajectories, fields, 4, pairs, LANES)
            x = jnp.pad(x, ((0, 0), (0, 0), (0, 0), (0, extra), (0, 0)))
            x = x.reshape(wire_shape)
        return x

    def exchange(x):
        return lax.all_to_all(x, "space", split_axis=0, concat_axis=0, tiled=True)

    analysis = fourier_tables(pairs * space, space, truncation, longitudes)
    synthesis = analysis.T
    south = position // split % 2
    hemisphere = jnp.where(south == 0, sin_lat, -sin_lat)
    weights_all = math.pi * jnp.sqrt(1.0 - hemisphere * hemisphere) / (2 * half_lat)
    vmem = pl.BlockSpec(memory_space=pltpu.VMEM)
    modes = 4 * pairs * space

    def grid(k, x):
        first = k * LANES + position % split * lane_count
        mu = lax.dynamic_slice_in_dim(hemisphere, first, lane_count)
        weight = lax.dynamic_slice_in_dim(weights_all, first, lane_count)
        if split > 1:
            short = LANES - lane_count
            mu = jnp.pad(mu, (0, short))
            weight = jnp.pad(weight, (0, short))
            x = jnp.pad(x, ((0, 0), (0, 0), (0, 0), (0, short)))
        out = pl.pallas_call(
            functools.partial(grid_kernel, scale=1.0 / truncation),
            out_shape=jax.ShapeDtypeStruct(x.shape, jnp.bfloat16),
            in_specs=[vmem] * 5,
            out_specs=vmem,
            scratch_shapes=[
                pltpu.VMEM((modes, fields * LANES), jnp.bfloat16),
                pltpu.VMEM((longitudes, fields * LANES), jnp.bfloat16),
            ],
            compiler_params=pltpu.CompilerParams(vmem_limit_bytes=limit),
            cost_estimate=pl.CostEstimate(
                flops=4 * modes * longitudes * fields * LANES,
                bytes_accessed=12 * 1024 * 1024,
                transcendentals=0,
            ),
            name="grid",
        )((2.0 * mu)[None], weight[None], x, synthesis, analysis)
        return out[..., :lane_count] if split > 1 else out

    def inverse(ws, first, last, part):
        chunks = len(ws)
        extra_in = [part, state] if last else []
        return pl.pallas_call(
            functools.partial(
                inverse_kernel, truncation=truncation, pairs=padded_pairs, chunks=chunks, last=last
            ),
            out_shape=jax.ShapeDtypeStruct(state.shape, jnp.float32),
            grid=(steps,),
            in_specs=[smem] * 3
            + [wire_spec] * chunks
            + [leg_spec(first + k) for k in range(chunks)]
            + [state_spec] * len(extra_in),
            out_specs=state_spec,
            scratch_shapes=[
                pltpu.VMEM((chunks, tiles * LANES * SUB, LANES), jnp.float32),
                pltpu.VMEM((chunks, 4 * rows * padded_pairs, LANES), jnp.float32),
                pltpu.VMEM((tiles, rows * SUB, LANES), jnp.float32),
            ],
            compiler_params=pltpu.CompilerParams(vmem_limit_bytes=limit),
            cost_estimate=pl.CostEstimate(
                flops=8 * rows * padded_pairs * row_length * LANES * chunks,
                bytes_accessed=20 * 1024 * 1024,
                transcendentals=0,
            ),
            name="inverse",
        )(where, gravity, stability, *ws, *([columns] * chunks), *extra_in)

    sent = [exchange(to_wire(forward(k))) for k in range(chunk_count)]
    back = [from_wire(exchange(grid(k, x))) for k, x in enumerate(sent)]
    part = inverse(back[:-1], 0, False, None)
    out = inverse(back[-1:], chunk_count - 1, True, part)
    return out[:, :, :pairs] if extra else out


def solution(mesh):
    placed = (P("member", None, "space", None), P("space", None, None), P(), P(), P(), P())
    return jax.shard_map(
        shards,
        mesh=mesh,
        in_specs=placed,
        out_specs=P("member", None, "space", None),
        check_vma=False,
    )
```

```python
import functools
import math

import jax
import jax.numpy as jnp
from jax import lax
from jax.experimental import pallas as pl
from jax.experimental.pallas import tpu as pltpu
from jax.sharding import PartitionSpec as P

LANES = 128
SUB = 8
LONGITUDES_PER_WAVE = 2

time_step = 0.25
wave_scale = 16.0
diffusion = 0.02


def layout_terms(first_pair, count, lane0, lanes, truncation):
    pair = first_pair + lax.broadcasted_iota(jnp.int32, (count, lanes), 0)
    column = lane0 + lax.broadcasted_iota(jnp.int32, (count, lanes), 1)
    leading = column < truncation - pair
    offset = jnp.where(leading, column, column - (truncation - pair))
    order = jnp.where(leading, pair, truncation - 1 - pair)
    return leading, (offset & 1) == 1, order + offset


def forward_kernel(where_ref, spec_ref, fresh_ref, leg_ref, out_ref, xs, res, *, truncation, pairs):
    step = pl.program_id(0)
    row_length = truncation + 1
    trajectories, comps, block, _ = spec_ref.shape
    rows = trajectories * comps
    tiles = xs.shape[0]
    padded = tiles * LANES

    for k in range(tiles):
        width = min(LANES, row_length - k * LANES)
        lanes = slice(k * LANES, k * LANES + width)
        if width < LANES:
            xs[k] = jnp.zeros((rows * block, LANES), jnp.float32)
        xs[k, :, :width] = spec_ref[:, :, :, lanes].reshape(rows * block, width)

    for i in range(fresh_ref.shape[0]):
        slot = where_ref[1 + i]

        @pl.when(slot >= 0)
        def _():
            at = pl.multiple_of(slot * comps * block, SUB)
            for k in range(tiles):
                width = min(LANES, row_length - k * LANES)
                fresh = fresh_ref[i, :, :, k * LANES : k * LANES + width].astype(jnp.float32)
                xs[k, pl.ds(at, comps * block), :width] = fresh.reshape(comps * block, width)

    first_pair = where_ref[0] + step * block

    def one(q, carry):
        x = jnp.concatenate(
            [xs[k, pl.ds(q, rows, stride=block), :] for k in range(tiles)], axis=1
        )
        leading, odd, _ = layout_terms(first_pair + q, 1, 0, padded, truncation)
        lead = jnp.where(leading, x, 0.0)
        trail = jnp.where(leading, 0.0, x)
        lhs = jnp.concatenate(
            [lead, trail, jnp.where(odd, -lead, lead), jnp.where(odd, -trail, trail)], axis=0
        ).astype(jnp.bfloat16)
        got = jnp.dot(lhs, leg_ref[q], preferred_element_type=jnp.float32)
        res[pl.ds(step * block + q, 4 * rows, stride=pairs), :] = got
        return carry

    lax.fori_loop(0, block, one, 0)

    @pl.when(step == pl.num_programs(0) - 1)
    def _():
        for t in range(trajectories):
            for s in range(2):
                for f in range(comps // 2):
                    parts = []
                    for r in range(2):
                        for h in range(2):
                            row = ((s * 2 + h) * rows + t * comps + 2 * f + r) * pairs
                            parts.append(res[row : row + pairs, :])
                    out_ref[t * 2 + s, f] = jnp.concatenate(parts, axis=0).astype(jnp.bfloat16)


def grid_kernel(cor_ref, weight_ref, in_ref, syn_ref, ana_ref, out_ref, modes, force, *, scale):
    sources, fields, rows, lanes = in_ref.shape
    longitudes = syn_ref.shape[0]
    for d in range(sources):
        for f in range(fields):
            modes[d * rows : (d + 1) * rows, f * lanes : (f + 1) * lanes] = in_ref[d, f]
    cor = cor_ref[...]
    weight = weight_ref[...]
    span = 128

    def synth(b, carry):
        at = pl.multiple_of(b * span, span)
        g = (
            jnp.dot(syn_ref[pl.ds(at, span), :], modes[...], preferred_element_type=jnp.float32)
            * scale
        )
        field = [g[:, f * lanes : (f + 1) * lanes] for f in range(fields)]
        mean = 0.5 * (field[4] + field[5])
        out = [None] * fields
        for a in range(2):
            spin = field[a] + cor
            div = field[2 + a]
            out[a] = -spin * div
            out[2 + a] = spin * field[a] - 0.5 * div * div
            out[4 + a] = -(field[4 + a] + mean) * div
        for f in range(fields):
            force[pl.ds(at, span), f * lanes : (f + 1) * lanes] = out[f].astype(jnp.bfloat16)
        return carry

    lax.fori_loop(0, longitudes // span, synth, 0)

    def analyse(d, carry):
        at = pl.multiple_of(d * rows, 16)
        w = jnp.dot(ana_ref[pl.ds(at, rows), :], force[...], preferred_element_type=jnp.float32)
        for f in range(fields):
            out_ref[d, f] = (w[:, f * lanes : (f + 1) * lanes] * weight).astype(jnp.bfloat16)
        return carry

    lax.fori_loop(0, sources, analyse, 0)


def semi_implicit_slabs(old, tend, degree, gm, hm, truncation):
    eig = wave_scale * (degree * (degree + 1)).astype(jnp.float32) / float(truncation * truncation)
    damping = 1.0 / (1.0 + diffusion * eig * eig)
    coupling = time_step * time_step * eig
    pm = [[gm[a][0] * hm[0][b] + gm[a][1] * hm[1][b] for b in range(2)] for a in range(2)]
    diag_one = 1.0 + coupling * pm[0][0]
    diag_two = 1.0 + coupling * pm[1][1]
    cross_one = coupling * pm[0][1]
    cross_two = coupling * pm[1][0]
    inverse = 1.0 / (diag_one * diag_two - cross_one * cross_two)
    out = [None] * 12
    for r in range(2):
        star = [old[c * 2 + r] + time_step * tend[c * 2 + r] for c in range(6)]
        right = [
            star[2 + a] + time_step * eig * (gm[a][0] * star[4] + gm[a][1] * star[5])
            for a in range(2)
        ]
        div = [
            (diag_two * right[0] - cross_one * right[1]) * inverse,
            (diag_one * right[1] - cross_two * right[0]) * inverse,
        ]
        for a in range(2):
            out[a * 2 + r] = damping * star[a]
            out[(2 + a) * 2 + r] = damping * div[a]
            out[(4 + a) * 2 + r] = damping * (
                star[4 + a] - time_step * (hm[a][0] * div[0] + hm[a][1] * div[1])
            )
    return out


def inverse_kernel(where_ref, gravity_ref, stability_ref, *refs, truncation, pairs, chunks, last):
    w_refs, refs = refs[:chunks], refs[chunks:]
    leg_refs, refs = refs[:chunks], refs[chunks:]
    if last:
        part_ref, spec_ref, fresh_ref, out_ref, ws, ten = refs
    else:
        out_ref, ws, ten = refs
    step = pl.program_id(0)
    row_length = truncation + 1
    trajectories, comps, block, _ = out_ref.shape
    rows = trajectories * comps
    tiles = ten.shape[0]
    padded = tiles * LANES

    @pl.when(step == 0)
    def _():
        for k in range(chunks):
            for t in range(trajectories):
                for s in range(2):
                    for f in range(comps // 2):
                        got = w_refs[k][t * 2 + s, f].astype(jnp.float32)
                        for r in range(2):
                            for h in range(2):
                                row = ((s * 2 + h) * rows + t * comps + 2 * f + r) * pairs
                                at = (r * 2 + h) * pairs
                                ws[k, row : row + pairs, :] = got[at : at + pairs, :]

    first_pair = where_ref[0] + step * block

    def one(q, carry):
        got = None
        for k in range(chunks):
            lhs = ws[k, pl.ds(step * block + q, 4 * rows, stride=pairs), :].astype(jnp.bfloat16)
            term = lax.dot_general(
                lhs, leg_refs[k][q], (((1,), (1,)), ((), ())), preferred_element_type=jnp.float32
            )
            got = term if got is None else got + term
        leading, odd, _ = layout_terms(first_pair + q, 1, 0, padded, truncation)
        north = jnp.where(leading, got[:rows], got[rows : 2 * rows])
        south = jnp.where(leading, got[2 * rows : 3 * rows], got[3 * rows :])
        total = north + jnp.where(odd, -south, south)
        for k in range(tiles):
            ten[k, pl.ds(q, rows, stride=block), :] = total[:, k * LANES : (k + 1) * LANES]
        return carry

    lax.fori_loop(0, block, one, 0)

    if last:
        gm = [[gravity_ref[a, b] for b in range(2)] for a in range(2)]
        hm = [[stability_ref[a, b] for b in range(2)] for a in range(2)]
    for k in range(tiles):
        width = min(LANES, row_length - k * LANES)
        lanes = slice(k * LANES, k * LANES + width)
        if last:
            _, _, degree = layout_terms(first_pair, block, k * LANES, width, truncation)

        def body(t, carry):
            tend = []
            for c in range(comps):
                at = pl.multiple_of((t * comps + c) * block, SUB)
                value = ten[k, pl.ds(at, block), :][:, :width]
                tend.append(value)
            if last:
                tend = [tend[c] + part_ref[t, c, :, lanes] for c in range(comps)]
                old = [spec_ref[t, c, :, lanes] for c in range(comps)]
                for i in range(fresh_ref.shape[0]):
                    mine = where_ref[1 + i] == t
                    old = [jnp.where(mine, fresh_ref[i, c, :, lanes], old[c]) for c in range(comps)]
                tend = semi_implicit_slabs(old, tend, degree, gm, hm, truncation)
            for c in range(comps):
                out_ref[t, c, :, lanes] = tend[c]
            return carry

        lax.fori_loop(0, trajectories, body, 0)


def fourier_tables(pair_count, groups, truncation, longitudes):
    index = jnp.arange(pair_count * 4, dtype=jnp.int32)
    local = pair_count // groups
    group = index // (4 * local)
    part = index // (2 * local) % 2
    half = index // local % 2
    pair = group * local + index % local
    order = jnp.where(half == 0, pair, truncation - 1 - pair)
    quarter = part * (longitudes // 4)
    column = jnp.arange(longitudes, dtype=jnp.int32)[None, :]
    phase = (order[:, None] * column + quarter[:, None]) % longitudes
    angle = phase.astype(jnp.float32) * (2.0 * math.pi / longitudes)
    return jnp.cos(angle).astype(jnp.bfloat16)


def clone_routes(clones, local):
    members = lax.axis_size("member")
    me = lax.axis_index("member").astype(jnp.int32)
    owner = lax.div(clones, jnp.full_like(clones, local))
    index = clones - owner * local
    route = owner[:, 1] * members + owner[:, 0]
    slot = jnp.where(owner[:, 0] == me, index[:, 0], -1)
    return index[:, 1], route, slot


def send_clone(row, route):
    members = lax.axis_size("member")

    def move(a, b):
        if a == b:
            return lambda v: v
        return lambda v: lax.ppermute(v, "member", [(a, b)])

    branches = [move(a, b) for a in range(members) for b in range(members)]
    return lax.switch(route, branches, row)


def shards(spectra, legendre, sin_lat, gravity, stability, clones):
    trajectories, comps, pairs, row_length = spectra.shape
    truncation = row_length - 1
    half_lat = legendre.shape[2]
    longitudes = LONGITUDES_PER_WAVE * truncation
    space = lax.axis_size("space")
    position = lax.axis_index("space")
    fields = comps // 2
    split = space // (2 * trajectories)
    lane_count = LANES // split
    chunk_count = half_lat // LANES
    padded_pairs = -(-pairs // SUB) * SUB
    steps = padded_pairs // SUB
    tiles = -(-row_length // LANES)
    extra = padded_pairs - pairs
    rows = trajectories * comps

    survivor, route, slot = clone_routes(clones, trajectories)
    count = clones.shape[0]
    living = [
        lax.dynamic_index_in_dim(spectra, survivor[i], 0, keepdims=False) for i in range(count)
    ]
    fresh_narrow = jnp.stack(
        [send_clone(living[i].astype(jnp.bfloat16), route[i]) for i in range(count)]
    )
    state = spectra
    if extra:
        state = jnp.pad(state, ((0, 0), (0, 0), (0, extra), (0, 0)))
        fresh_narrow = jnp.pad(fresh_narrow, ((0, 0), (0, 0), (0, extra), (0, 0)))
    where = jnp.concatenate([(position * pairs).astype(jnp.int32).reshape(1), slot])
    columns = [
        jnp.pad(
            legendre[:, :, k * LANES : (k + 1) * LANES],
            ((0, extra), (0, tiles * LANES - row_length), (0, 0)),
        )
        for k in range(chunk_count)
    ]

    smem = pl.BlockSpec(memory_space=pltpu.SMEM)
    state_spec = pl.BlockSpec((trajectories, comps, SUB, row_length), lambda i: (0, 0, i, 0))
    wire_shape = (2 * trajectories, fields, 4 * padded_pairs, LANES)
    wire_spec = pl.BlockSpec(wire_shape, lambda i: (0, 0, 0, 0))

    fresh_spec = pl.BlockSpec((count, comps, SUB, row_length), lambda i: (0, 0, i, 0))
    leg_spec = pl.BlockSpec((SUB, tiles * LANES, LANES), lambda i: (i, 0, 0))

    limit = 60 * 1024 * 1024

    def forward(k):
        return pl.pallas_call(
            functools.partial(forward_kernel, truncation=truncation, pairs=padded_pairs),
            out_shape=jax.ShapeDtypeStruct(wire_shape, jnp.bfloat16),
            grid=(steps,),
            in_specs=[smem, state_spec, fresh_spec, leg_spec],
            out_specs=wire_spec,
            scratch_shapes=[
                pltpu.VMEM((tiles, rows * SUB, LANES), jnp.float32),
                pltpu.VMEM((4 * rows * padded_pairs, LANES), jnp.float32),
            ],
            compiler_params=pltpu.CompilerParams(vmem_limit_bytes=limit),
            cost_estimate=pl.CostEstimate(
                flops=8 * rows * padded_pairs * row_length * LANES,
                bytes_accessed=16 * 1024 * 1024,
                transcendentals=0,
            ),
            name="forward",
        )(where, state, fresh_narrow, columns[k])

    def to_wire(x):
        if extra:
            x = x.reshape(2 * trajectories, fields, 4, padded_pairs, LANES)[:, :, :, :pairs]
            x = x.reshape(2 * trajectories, fields, 4 * pairs, LANES)
        if split > 1:
            x = x.reshape(2 * trajectories, fields, 4 * pairs, split, lane_count)
            x = jnp.transpose(x, (0, 3, 1, 2, 4)).reshape(space, fields, 4 * pairs, lane_count)
        return x

    def from_wire(x):
        if split > 1:
            x = x.reshape(2 * trajectories, split, fields, 4 * pairs, lane_count)
            x = jnp.transpose(x, (0, 2, 3, 1, 4))
            x = x.reshape(2 * trajectories, fields, 4 * pairs, LANES)
        if extra:
            x = x.reshape(2 * trajectories, fields, 4, pairs, LANES)
            x = jnp.pad(x, ((0, 0), (0, 0), (0, 0), (0, extra), (0, 0)))
            x = x.reshape(wire_shape)
        return x

    def exchange(x):
        return lax.all_to_all(x, "space", split_axis=0, concat_axis=0, tiled=True)

    analysis = lax.optimization_barrier(
        fourier_tables(pairs * space, space, truncation, longitudes)
    )
    synthesis = analysis.T
    south = position // split % 2
    hemisphere = jnp.where(south == 0, sin_lat, -sin_lat)
    weights_all = math.pi * jnp.sqrt(1.0 - hemisphere * hemisphere) / (2 * half_lat)
    vmem = pl.BlockSpec(memory_space=pltpu.VMEM)
    modes = 4 * pairs * space

    def grid(k, x):
        first = k * LANES + position % split * lane_count
        mu = lax.dynamic_slice_in_dim(hemisphere, first, lane_count)
        weight = lax.dynamic_slice_in_dim(weights_all, first, lane_count)
        if split > 1:
            short = LANES - lane_count
            mu = jnp.pad(mu, (0, short))
            weight = jnp.pad(weight, (0, short))
            x = jnp.pad(x, ((0, 0), (0, 0), (0, 0), (0, short)))
        out = pl.pallas_call(
            functools.partial(grid_kernel, scale=1.0 / truncation),
            out_shape=jax.ShapeDtypeStruct(x.shape, jnp.bfloat16),
            in_specs=[vmem] * 5,
            out_specs=vmem,
            scratch_shapes=[
                pltpu.VMEM((modes, fields * LANES), jnp.bfloat16),
                pltpu.VMEM((longitudes, fields * LANES), jnp.bfloat16),
            ],
            compiler_params=pltpu.CompilerParams(vmem_limit_bytes=limit),
            cost_estimate=pl.CostEstimate(
                flops=4 * modes * longitudes * fields * LANES,
                bytes_accessed=12 * 1024 * 1024,
                transcendentals=0,
            ),
            name="grid",
        )((2.0 * mu)[None], weight[None], x, synthesis, analysis)
        return out[..., :lane_count] if split > 1 else out

    def inverse(ws, first, last, part):
        chunks = len(ws)
        extra_in = [part, state, fresh] if last else []
        return pl.pallas_call(
            functools.partial(
                inverse_kernel, truncation=truncation, pairs=padded_pairs, chunks=chunks, last=last
            ),
            out_shape=jax.ShapeDtypeStruct(state.shape, jnp.float32),
            grid=(steps,),
            in_specs=[smem] * 3
            + [wire_spec] * chunks
            + [leg_spec] * chunks
            + [state_spec, state_spec, fresh_spec][: len(extra_in)],
            out_specs=state_spec,
            scratch_shapes=[
                pltpu.VMEM((chunks, 4 * rows * padded_pairs, LANES), jnp.float32),
                pltpu.VMEM((tiles, rows * SUB, LANES), jnp.float32),
            ],
            compiler_params=pltpu.CompilerParams(vmem_limit_bytes=limit),
            cost_estimate=pl.CostEstimate(
                flops=8 * rows * padded_pairs * row_length * LANES * chunks,
                bytes_accessed=20 * 1024 * 1024,
                transcendentals=0,
            ),
            name="inverse",
        )(where, gravity, stability, *ws, *columns[first : first + chunks], *extra_in)

    made = [forward(k) for k in range(chunk_count)]
    wide, _ = lax.optimization_barrier((living, made[1]))
    fresh = jnp.stack([send_clone(wide[i], route[i]) for i in range(count)])
    if extra:
        fresh = jnp.pad(fresh, ((0, 0), (0, 0), (0, extra), (0, 0)))
    sent = [exchange(to_wire(x)) for x in made]
    back = [from_wire(exchange(grid(k, x))) for k, x in enumerate(sent)]
    part = inverse(back[:-1], 0, False, None)
    out = inverse(back[-1:], chunk_count - 1, True, part)
    return out[:, :, :pairs] if extra else out


def solution(mesh):
    placed = (P("member", None, "space", None), P("space", None, None), P(), P(), P(), P())
    return jax.shard_map(
        shards,
        mesh=mesh,
        in_specs=placed,
        out_specs=P("member", None, "space", None),
        check_vma=False,
    )
```

```python
import functools
import math

import jax
import jax.numpy as jnp
from jax import lax
from jax.experimental import pallas as pl
from jax.experimental.pallas import tpu as pltpu
from jax.sharding import PartitionSpec as P


LANES = 128
SUB = 8
UNROLL_FORWARD = 2
UNROLL_INVERSE = 4
LONGITUDES_PER_WAVE = 2

time_step = 0.25
wave_scale = 16.0
diffusion = 0.02


def layout_terms(first_pair, count, lane0, lanes, truncation):
    pair = first_pair + lax.broadcasted_iota(jnp.int32, (count, lanes), 0)
    column = lane0 + lax.broadcasted_iota(jnp.int32, (count, lanes), 1)
    leading = column < truncation - pair
    offset = jnp.where(leading, column, column - (truncation - pair))
    order = jnp.where(leading, pair, truncation - 1 - pair)
    return leading, (offset & 1) == 1, order + offset


def forward_kernel(where_ref, spec_ref, fresh_ref, leg_ref, *refs, truncation, pairs, keep):
    step = pl.program_id(0)
    row_length = truncation + 1
    trajectories, comps, block, _ = spec_ref.shape
    rows = trajectories * comps
    slots = 2 * trajectories
    out_refs, refs = refs[:slots], refs[slots:]
    if keep:
        keep_ref, refs = refs[0], refs[1:]
    wide, xs, res = refs
    tiles = xs.shape[0]
    padded = tiles * LANES
    count = fresh_ref.shape[0]

    @pl.when(step == 0)
    def _():
        wide[row_length * block :, :] = jnp.zeros(
            (wide.shape[0] - row_length * block, LANES), jnp.float32
        )

    wide[: row_length * block, :] = (
        leg_ref[...].astype(jnp.float32).reshape(row_length * block, LANES)
    )
    for k in range(tiles):
        width = min(LANES, row_length - k * LANES)
        lanes = slice(k * LANES, k * LANES + width)
        if width < LANES:
            xs[k] = jnp.zeros((rows * block, LANES), jnp.float32)
        xs[k, :, :width] = spec_ref[:, :, :, lanes].reshape(rows * block, width)

    for i in range(count):
        slot = where_ref[1 + i]

        @pl.when(slot >= 0)
        def _():
            at = pl.multiple_of(slot * comps * block, SUB)
            for k in range(tiles):
                width = min(LANES, row_length - k * LANES)
                fresh = fresh_ref[i, :, :, k * LANES : k * LANES + width].astype(jnp.float32)
                xs[k, pl.ds(at, comps * block), :width] = fresh.reshape(comps * block, width)

    first_pair = where_ref[0] + step * block

    def one(q, carry):
        x = jnp.concatenate(
            [xs[k, pl.ds(q, rows, stride=block), :] for k in range(tiles)], axis=1
        )
        leading, odd, _ = layout_terms(first_pair + q, 1, 0, padded, truncation)
        lead = jnp.where(leading, x, 0.0)
        trail = jnp.where(leading, 0.0, x)
        lhs = jnp.concatenate(
            [lead, trail, jnp.where(odd, -lead, lead), jnp.where(odd, -trail, trail)], axis=0
        ).astype(jnp.bfloat16)
        rhs = wide[pl.ds(q, padded, stride=block), :].astype(jnp.bfloat16)
        if keep:
            keep_ref[q] = rhs
        got = jnp.dot(lhs, rhs, preferred_element_type=jnp.float32)
        res[pl.ds(step * block + q, 4 * rows, stride=pairs), :] = got
        return carry

    lax.fori_loop(0, block, one, 0, unroll=UNROLL_FORWARD)

    @pl.when(step == pl.num_programs(0) - 1)
    def _():
        for n in range(slots):
            place = where_ref[1 + count + n]
            t, s = lax.div(place, 2), lax.rem(place, 2)
            base = pl.multiple_of((s * (2 * rows) + t * comps) * pairs, SUB)
            for f in range(comps // 2):
                parts = []
                for r in range(2):
                    for h in range(2):
                        parts.append(res[pl.ds(base + (h * rows + 2 * f + r) * pairs, pairs), :])
                out_refs[n][f] = jnp.concatenate(parts, axis=0).astype(jnp.bfloat16)


def grid_kernel(order_ref, cor_ref, weight_ref, syn_ref, ana_ref, *refs, scale):
    sources = order_ref.shape[0]
    in_refs, out_refs, (modes, force) = refs[:sources], refs[sources:-2], refs[-2:]
    fields, rows, lanes = in_refs[0].shape
    longitudes = syn_ref.shape[0]
    for n in range(sources):
        at = pl.multiple_of(order_ref[n] * rows, 16)
        for f in range(fields):
            modes[pl.ds(at, rows), f * lanes : (f + 1) * lanes] = in_refs[n][f]
    cor = cor_ref[...]
    weight = weight_ref[...]
    span = 128

    def synth(b, carry):
        at = pl.multiple_of(b * span, span)
        g = (
            jnp.dot(syn_ref[pl.ds(at, span), :], modes[...], preferred_element_type=jnp.float32)
            * scale
        )
        field = [g[:, f * lanes : (f + 1) * lanes] for f in range(fields)]
        mean = 0.5 * (field[4] + field[5])
        out = [None] * fields
        for a in range(2):
            spin = field[a] + cor
            div = field[2 + a]
            out[a] = -spin * div
            out[2 + a] = spin * field[a] - 0.5 * div * div
            out[4 + a] = -(field[4 + a] + mean) * div
        for f in range(fields):
            force[pl.ds(at, span), f * lanes : (f + 1) * lanes] = out[f].astype(jnp.bfloat16)
        return carry

    lax.fori_loop(0, longitudes // span, synth, 0)

    def analyse(d, carry):
        at = pl.multiple_of(d * rows, 16)
        w = jnp.dot(ana_ref[pl.ds(at, rows), :], force[...], preferred_element_type=jnp.float32)
        for f in range(fields):
            lane = slice(f * lanes, (f + 1) * lanes)
            modes[pl.ds(at, rows), lane] = (w[:, lane] * weight).astype(jnp.bfloat16)
        return carry

    lax.fori_loop(0, sources, analyse, 0)
    for n in range(sources):
        at = pl.multiple_of(order_ref[n] * rows, 16)
        for f in range(fields):
            out_refs[n][f] = modes[pl.ds(at, rows), f * lanes : (f + 1) * lanes]


def semi_implicit_slabs(old, tend, degree, gm, hm, truncation):
    eig = wave_scale * (degree * (degree + 1)).astype(jnp.float32) / float(truncation * truncation)
    damping = 1.0 / (1.0 + diffusion * eig * eig)
    coupling = time_step * time_step * eig
    pm = [[gm[a][0] * hm[0][b] + gm[a][1] * hm[1][b] for b in range(2)] for a in range(2)]
    diag_one = 1.0 + coupling * pm[0][0]
    diag_two = 1.0 + coupling * pm[1][1]
    cross_one = coupling * pm[0][1]
    cross_two = coupling * pm[1][0]
    inverse = 1.0 / (diag_one * diag_two - cross_one * cross_two)
    out = [None] * 12
    for r in range(2):
        star = [old[c * 2 + r] + time_step * tend[c * 2 + r] for c in range(6)]
        right = [
            star[2 + a] + time_step * eig * (gm[a][0] * star[4] + gm[a][1] * star[5])
            for a in range(2)
        ]
        div = [
            (diag_two * right[0] - cross_one * right[1]) * inverse,
            (diag_one * right[1] - cross_two * right[0]) * inverse,
        ]
        for a in range(2):
            out[a * 2 + r] = damping * star[a]
            out[(2 + a) * 2 + r] = damping * div[a]
            out[(4 + a) * 2 + r] = damping * (
                star[4 + a] - time_step * (hm[a][0] * div[0] + hm[a][1] * div[1])
            )
    return out


def inverse_kernel(
    where_ref, gravity_ref, stability_ref, *refs, truncation, pairs, chunks, last, slots
):
    w_refs, refs = refs[: chunks * slots], refs[chunks * slots :]
    leg_refs, refs = refs[:chunks], refs[chunks:]
    if last:
        part_ref, spec_ref, fresh_ref, out_ref, ws, ten = refs
    else:
        out_ref, ws, ten, wide = refs
    step = pl.program_id(0)
    row_length = truncation + 1
    trajectories, comps, block, _ = out_ref.shape
    rows = trajectories * comps
    tiles = ten.shape[0]
    padded = tiles * LANES
    count = where_ref.shape[0] - 1 - slots

    @pl.when(step == 0)
    def _():
        if not last:
            for k in range(chunks):
                wide[k, row_length * block :, :] = jnp.zeros(
                    (wide.shape[1] - row_length * block, LANES), jnp.float32
                )
        for k in range(chunks):
            for n in range(slots):
                place = where_ref[1 + count + n]
                t, s = lax.div(place, 2), lax.rem(place, 2)
                base = pl.multiple_of((s * (2 * rows) + t * comps) * pairs, SUB)
                for f in range(comps // 2):
                    got = w_refs[k * slots + n][f].astype(jnp.float32)
                    for r in range(2):
                        for h in range(2):
                            at = (r * 2 + h) * pairs
                            ws[k, pl.ds(base + (h * rows + 2 * f + r) * pairs, pairs), :] = got[
                                at : at + pairs, :
                            ]

    if not last:
        for k in range(chunks):
            wide[k, : row_length * block, :] = (
                leg_refs[k][...].astype(jnp.float32).reshape(row_length * block, LANES)
            )
    first_pair = where_ref[0] + step * block

    def one(q, carry):
        got = None
        for k in range(chunks):
            lhs = ws[k, pl.ds(step * block + q, 4 * rows, stride=pairs), :].astype(jnp.bfloat16)
            if last:
                rhs = leg_refs[k][q]
            else:
                rhs = wide[k, pl.ds(q, padded, stride=block), :].astype(jnp.bfloat16)
            term = lax.dot_general(
                lhs, rhs, (((1,), (1,)), ((), ())), preferred_element_type=jnp.float32
            )
            got = term if got is None else got + term
        leading, odd, _ = layout_terms(first_pair + q, 1, 0, padded, truncation)
        north = jnp.where(leading, got[:rows], got[rows : 2 * rows])
        south = jnp.where(leading, got[2 * rows : 3 * rows], got[3 * rows :])
        total = north + jnp.where(odd, -south, south)
        for k in range(tiles):
            ten[k, pl.ds(q, rows, stride=block), :] = total[:, k * LANES : (k + 1) * LANES]
        return carry

    lax.fori_loop(0, block, one, 0, unroll=UNROLL_INVERSE)

    if last:
        gm = [[gravity_ref[a, b] for b in range(2)] for a in range(2)]
        hm = [[stability_ref[a, b] for b in range(2)] for a in range(2)]
    for k in range(tiles):
        width = min(LANES, row_length - k * LANES)
        lanes = slice(k * LANES, k * LANES + width)
        if last:
            _, _, degree = layout_terms(first_pair, block, k * LANES, width, truncation)

        def body(t, carry):
            tend = []
            for c in range(comps):
                at = pl.multiple_of((t * comps + c) * block, SUB)
                value = ten[k, pl.ds(at, block), :][:, :width]
                tend.append(value)
            if last:
                tend = [tend[c] + part_ref[t, c, :, lanes] for c in range(comps)]
                old = [spec_ref[t, c, :, lanes] for c in range(comps)]
                for i in range(fresh_ref.shape[0]):
                    mine = where_ref[1 + i] == t
                    old = [jnp.where(mine, fresh_ref[i, c, :, lanes], old[c]) for c in range(comps)]
                tend = semi_implicit_slabs(old, tend, degree, gm, hm, truncation)
            for c in range(comps):
                out_ref[t, c, :, lanes] = tend[c]
            return carry

        lax.fori_loop(0, trajectories, body, 0)


def fourier_tables(pair_count, groups, truncation, longitudes):
    index = jnp.arange(pair_count * 4, dtype=jnp.int32)
    local = pair_count // groups
    group = index // (4 * local)
    part = index // (2 * local) % 2
    half = index // local % 2
    pair = group * local + index % local
    order = jnp.where(half == 0, pair, truncation - 1 - pair)
    quarter = part * (longitudes // 4)
    half_turn = longitudes // 2
    column = jnp.arange(half_turn, dtype=jnp.int32)[None, :]
    phase = (order[:, None] * column + quarter[:, None]) % longitudes
    angle = phase.astype(jnp.float32) * (2.0 * math.pi / longitudes)
    first = jnp.cos(angle)
    second = jnp.where(order[:, None] % 2 == 0, first, -first)
    return jnp.concatenate([first, second], axis=1).astype(jnp.bfloat16)


def clone_routes(clones, local):
    members = lax.axis_size("member")
    me = lax.axis_index("member").astype(jnp.int32)
    owner = lax.div(clones, jnp.full_like(clones, local))
    index = clones - owner * local
    route = owner[:, 1] * members + owner[:, 0]
    slot = jnp.where(owner[:, 0] == me, index[:, 0], -1)
    return index[:, 1], route, slot


def send_clone(row, route):
    members = lax.axis_size("member")

    def move(a, b):
        if a == b:
            return lambda v: v
        return lambda v: lax.ppermute(v, "member", [(a, b)])

    branches = [move(a, b) for a in range(members) for b in range(members)]
    return lax.switch(route, branches, row)


def shards(spectra, legendre, sin_lat, gravity, stability, clones):
    trajectories, comps, pairs, row_length = spectra.shape
    truncation = row_length - 1
    half_lat = legendre.shape[2]
    longitudes = LONGITUDES_PER_WAVE * truncation
    space = lax.axis_size("space")
    position = lax.axis_index("space")
    fields = comps // 2
    split = space // (2 * trajectories)
    lane_count = LANES // split
    chunk_count = half_lat // LANES
    padded_pairs = -(-pairs // SUB) * SUB
    steps = padded_pairs // SUB
    tiles = -(-row_length // LANES)
    extra = padded_pairs - pairs
    rows = trajectories * comps

    survivor, route, slot = clone_routes(clones, trajectories)
    count = clones.shape[0]
    living = [
        lax.dynamic_index_in_dim(spectra, survivor[i], 0, keepdims=False) for i in range(count)
    ]
    fresh_narrow = jnp.stack(
        [send_clone(living[i].astype(jnp.bfloat16), route[i]) for i in range(count)]
    )
    state = spectra
    if extra:
        state = jnp.pad(state, ((0, 0), (0, 0), (0, extra), (0, 0)))
        fresh_narrow = jnp.pad(fresh_narrow, ((0, 0), (0, 0), (0, extra), (0, 0)))
    slots = 2 * trajectories
    direct = split == 1
    if direct:
        order = jnp.bitwise_xor(position.astype(jnp.int32), jnp.arange(space, dtype=jnp.int32))
        slot_order = order
    else:
        order = jnp.arange(space, dtype=jnp.int32)
        slot_order = jnp.arange(slots, dtype=jnp.int32)
    where = jnp.concatenate([(position * pairs).astype(jnp.int32).reshape(1), slot, slot_order])
    columns = jnp.transpose(legendre, (1, 0, 2))
    if extra:
        columns = jnp.pad(columns, ((0, 0), (0, extra), (0, 0)))

    smem = pl.BlockSpec(memory_space=pltpu.SMEM)
    state_spec = pl.BlockSpec((trajectories, comps, SUB, row_length), lambda i: (0, 0, i, 0))
    fresh_spec = pl.BlockSpec((count, comps, SUB, row_length), lambda i: (0, 0, i, 0))
    kept_spec = pl.BlockSpec((SUB, tiles * LANES, LANES), lambda i: (i, 0, 0))
    part_shape = (fields, 4 * padded_pairs, LANES)
    part_spec = pl.BlockSpec(part_shape, lambda i: (0, 0, 0))

    def leg_spec(k):
        return pl.BlockSpec((row_length, SUB, LANES), lambda i: (0, i, k))

    mib = 1024 * 1024

    def forward(k, where):
        keep = k == chunk_count - 1
        kept_shape = jax.ShapeDtypeStruct((padded_pairs, tiles * LANES, LANES), jnp.bfloat16)
        return pl.pallas_call(
            functools.partial(
                forward_kernel, truncation=truncation, pairs=padded_pairs, keep=keep
            ),
            out_shape=[jax.ShapeDtypeStruct(part_shape, jnp.bfloat16)] * slots
            + [kept_shape] * keep,
            grid=(steps,),
            in_specs=[smem, state_spec, fresh_spec, leg_spec(k)],
            out_specs=[part_spec] * slots + [kept_spec] * keep,
            scratch_shapes=[
                pltpu.VMEM((tiles * LANES * SUB, LANES), jnp.float32),
                pltpu.VMEM((tiles, rows * SUB, LANES), jnp.float32),
                pltpu.VMEM((4 * rows * padded_pairs, LANES), jnp.float32),
            ],
            compiler_params=pltpu.CompilerParams(vmem_limit_bytes=60 * mib),
            cost_estimate=pl.CostEstimate(
                flops=8 * rows * padded_pairs * row_length * LANES,
                bytes_accessed=16 * 1024 * 1024,
                transcendentals=0,
            ),
            name="forward",
        )(where, state, fresh_narrow, columns)

    def to_wire(x):
        if extra:
            x = x.reshape(slots, fields, 4, padded_pairs, LANES)[:, :, :, :pairs]
        x = x.reshape(slots, fields, 4 * pairs, split, lane_count)
        return jnp.transpose(x, (0, 3, 1, 2, 4)).reshape(space, fields, 4 * pairs, lane_count)

    def from_wire(x):
        x = x.reshape(slots, split, fields, 4, pairs, lane_count)
        x = jnp.transpose(x, (0, 2, 3, 4, 1, 5)).reshape(slots, fields, 4, pairs, LANES)
        if extra:
            x = jnp.pad(x, ((0, 0), (0, 0), (0, 0), (0, extra), (0, 0)))
        return x.reshape((slots,) + part_shape)

    def exchange(x):
        return lax.all_to_all(x, "space", split_axis=0, concat_axis=0, tiled=True)

    def swap(parts):
        return [
            lax.ppermute(x, "space", [(d, d ^ n) for d in range(space)]) if n else x
            for n, x in enumerate(parts)
        ]

    def spread(parts):
        if direct:
            return swap(parts)
        x = exchange(to_wire(jnp.stack(parts)))
        x = jnp.pad(x, ((0, 0), (0, 0), (0, 0), (0, LANES - lane_count)))
        return [x[d] for d in range(space)]

    def collect(parts):
        if direct:
            return swap(parts)
        x = from_wire(exchange(jnp.stack(parts)[..., :lane_count]))
        return [x[n] for n in range(slots)]

    analysis = lax.optimization_barrier(
        fourier_tables(pairs * space, space, truncation, longitudes)
    )
    synthesis = analysis.T
    south = position // split % 2
    hemisphere = jnp.where(south == 0, sin_lat, -sin_lat)
    weights_all = math.pi * jnp.sqrt(1.0 - hemisphere * hemisphere) / (2 * half_lat)
    vmem = pl.BlockSpec(memory_space=pltpu.VMEM)
    modes = 4 * pairs * space

    def grid(k, parts):
        first = k * LANES + position % split * lane_count
        mu = lax.dynamic_slice_in_dim(hemisphere, first, lane_count)
        weight = lax.dynamic_slice_in_dim(weights_all, first, lane_count)
        short = LANES - lane_count
        if short:
            mu = jnp.pad(mu, (0, short))
            weight = jnp.pad(weight, (0, short))
        return pl.pallas_call(
            functools.partial(grid_kernel, scale=1.0 / truncation),
            out_shape=[jax.ShapeDtypeStruct(x.shape, jnp.bfloat16) for x in parts],
            in_specs=[smem] + [vmem] * (4 + space),
            out_specs=[vmem] * space,
            scratch_shapes=[
                pltpu.VMEM((modes, fields * LANES), jnp.bfloat16),
                pltpu.VMEM((longitudes, fields * LANES), jnp.bfloat16),
            ],
            compiler_params=pltpu.CompilerParams(vmem_limit_bytes=60 * mib),
            cost_estimate=pl.CostEstimate(
                flops=4 * modes * longitudes * fields * LANES,
                bytes_accessed=12 * 1024 * 1024,
                transcendentals=0,
            ),
            name="grid",
        )(order, (2.0 * mu)[None], weight[None], synthesis, analysis, *parts)

    def inverse(ws, first, kept, part):
        chunks = len(ws)
        last = kept is not None
        extra_in = [part, state, fresh] if last else []
        wide_scratch = pltpu.VMEM((chunks, tiles * LANES * SUB, LANES), jnp.float32)
        legs = [kept] if last else [columns] * chunks
        return pl.pallas_call(
            functools.partial(
                inverse_kernel,
                truncation=truncation,
                pairs=padded_pairs,
                chunks=chunks,
                last=last,
                slots=slots,
            ),
            out_shape=jax.ShapeDtypeStruct(state.shape, jnp.float32),
            grid=(steps,),
            in_specs=[smem] * 3
            + [part_spec] * (chunks * slots)
            + ([kept_spec] if last else [leg_spec(first + k) for k in range(chunks)])
            + [state_spec, state_spec, fresh_spec][: len(extra_in)],
            out_specs=state_spec,
            scratch_shapes=[
                pltpu.VMEM((chunks, 4 * rows * padded_pairs, LANES), jnp.float32),
                pltpu.VMEM((tiles, rows * SUB, LANES), jnp.float32),
            ]
            + ([] if last else [wide_scratch]),
            compiler_params=pltpu.CompilerParams(vmem_limit_bytes=60 * mib),
            cost_estimate=pl.CostEstimate(
                flops=8 * rows * padded_pairs * row_length * LANES * chunks,
                bytes_accessed=20 * 1024 * 1024,
                transcendentals=0,
            ),
            name="inverse",
        )(where, gravity, stability, *[x for w in ws for x in w], *legs, *extra_in)

    made, turn = [], where
    for k in range(chunk_count):
        made.append(list(forward(k, turn)))
        turn, made[-1][0] = lax.optimization_barrier((where, made[-1][0]))
    kept = made[-1][-1]
    sent = []
    for x in made:
        sent.append(spread(x[:slots]))
    back = []
    for k in range(chunk_count):
        parts = sent[k]
        if k == 1:
            parts, fresh = lax.optimization_barrier((parts, fresh))
        got = grid(k, parts)
        if k == 0:
            wide, got = lax.optimization_barrier((living, got))
            fresh = jnp.stack([send_clone(wide[i], route[i]) for i in range(count)])
            if extra:
                fresh = jnp.pad(fresh, ((0, 0), (0, 0), (0, extra), (0, 0)))
        back.append(collect(got))
    part = inverse(back[:-1], 0, None, None)
    out = inverse(back[-1:], chunk_count - 1, kept, part)
    return out[:, :, :pairs] if extra else out


def solution(mesh):
    placed = (P("member", None, "space", None), P("space", None, None), P(), P(), P(), P())
    return jax.shard_map(
        shards,
        mesh=mesh,
        in_specs=placed,
        out_specs=P("member", None, "space", None),
        check_vma=False,
    )
```

```python
import functools
import math

import jax
import jax.numpy as jnp
from jax import lax
from jax.experimental import pallas as pl
from jax.experimental.pallas import tpu as pltpu
from jax.sharding import PartitionSpec as P


LANES = 128
SUB = 8
PACKED = 16
UNROLL_FORWARD = 8
UNROLL_INVERSE = 8
LONGITUDES_PER_WAVE = 2

time_step = 0.25
wave_scale = 16.0
diffusion = 0.02


def layout_terms(first_pair, count, lane0, lanes, truncation):
    pair = first_pair + lax.broadcasted_iota(jnp.int32, (count, lanes), 0)
    column = lane0 + lax.broadcasted_iota(jnp.int32, (count, lanes), 1)
    leading = column < truncation - pair
    offset = jnp.where(leading, column, column - (truncation - pair))
    order = jnp.where(leading, pair, truncation - 1 - pair)
    return leading, (offset & 1) == 1, order + offset


def forward_kernel(where_ref, spec_ref, leg_ref, *refs, truncation, pairs, keep, count):
    step = pl.program_id(0)
    row_length = truncation + 1
    trajectories, comps, block, _ = spec_ref.shape
    rows = trajectories * comps
    slots = 2 * trajectories
    fresh_refs, refs = refs[:count], refs[count:]
    out_refs, refs = refs[:slots], refs[slots:]
    if keep:
        keep_ref, refs = refs[0], refs[1:]
    wide, xs, res = refs
    tiles = xs.shape[0]
    padded = tiles * LANES

    @pl.when(step == 0)
    def _():
        wide[row_length * block :, :] = jnp.zeros(
            (wide.shape[0] - row_length * block, LANES), jnp.float32
        )

    wide[: row_length * block, :] = (
        leg_ref[...].astype(jnp.float32).reshape(row_length * block, LANES)
    )
    for k in range(tiles):
        width = min(LANES, row_length - k * LANES)
        lanes = slice(k * LANES, k * LANES + width)
        if width < LANES:
            xs[k] = jnp.zeros((rows * block, LANES), jnp.float32)
        xs[k, :, :width] = spec_ref[:, :, :, lanes].reshape(rows * block, width)

    for i in range(count):
        slot = where_ref[1 + i]

        @pl.when(slot >= 0)
        def _():
            at = pl.multiple_of(slot * comps * block, SUB)
            for k in range(tiles):
                width = min(LANES, row_length - k * LANES)
                fresh = fresh_refs[i][:, :, k * LANES : k * LANES + width].astype(jnp.float32)
                xs[k, pl.ds(at, comps * block), :width] = fresh.reshape(comps * block, width)

    first_pair = where_ref[0] + step * block

    def one(q, carry):
        x = jnp.concatenate(
            [xs[k, pl.ds(q, rows, stride=block), :] for k in range(tiles)], axis=1
        )
        x = x.astype(jnp.bfloat16)
        edge = truncation - first_pair - q
        column = lax.broadcasted_iota(jnp.int32, (PACKED, padded), 1)
        leading = column < edge
        odd = (jnp.where(leading, column, column - edge) & 1) == 1
        sign = jnp.where(odd, -1.0, 1.0)
        factors = [
            jnp.where(leading, 1.0, 0.0),
            jnp.where(leading, 0.0, 1.0),
            jnp.where(leading, sign, 0.0),
            jnp.where(leading, 0.0, sign),
        ]
        lhs = []
        for factor in factors:
            factor = factor.astype(jnp.bfloat16)
            for at in range(0, rows, PACKED):
                lhs.append(x[at : at + PACKED] * factor)
        lhs = jnp.concatenate(lhs, axis=0)
        rhs = wide[pl.ds(q, padded, stride=block), :].astype(jnp.bfloat16)
        if keep:
            keep_ref[q] = rhs
        got = jnp.dot(lhs, rhs, preferred_element_type=jnp.float32)
        res[pl.ds(step * block + q, 4 * rows, stride=pairs), :] = got
        return carry

    lax.fori_loop(0, block, one, 0, unroll=UNROLL_FORWARD)

    @pl.when(step == pl.num_programs(0) - 1)
    def _():
        for n in range(slots):
            place = where_ref[1 + count + n]
            t, s = lax.div(place, 2), lax.rem(place, 2)
            base = pl.multiple_of((s * (2 * rows) + t * comps) * pairs, SUB)
            for f in range(comps // 2):
                parts = []
                for r in range(2):
                    for h in range(2):
                        parts.append(res[pl.ds(base + (h * rows + 2 * f + r) * pairs, pairs), :])
                out_refs[n][f] = jnp.concatenate(parts, axis=0).astype(jnp.bfloat16)


def grid_kernel(order_ref, cor_ref, weight_ref, syn_ref, ana_ref, *refs, scale):
    sources = order_ref.shape[0]
    in_refs, out_refs, (modes, force) = refs[:sources], refs[sources:-2], refs[-2:]
    fields, rows, lanes = in_refs[0].shape
    longitudes = syn_ref.shape[0]
    for n in range(sources):
        at = pl.multiple_of(order_ref[n] * rows, 16)
        for f in range(fields):
            modes[pl.ds(at, rows), f * lanes : (f + 1) * lanes] = in_refs[n][f]
    cor = cor_ref[...]
    weight = weight_ref[...]
    span = 128

    def synth(b, carry):
        at = pl.multiple_of(b * span, span)
        g = (
            jnp.dot(syn_ref[pl.ds(at, span), :], modes[...], preferred_element_type=jnp.float32)
            * scale
        )
        field = [g[:, f * lanes : (f + 1) * lanes] for f in range(fields)]
        mean = 0.5 * (field[4] + field[5])
        out = [None] * fields
        for a in range(2):
            spin = field[a] + cor
            div = field[2 + a]
            out[a] = -spin * div
            out[2 + a] = spin * field[a] - 0.5 * div * div
            out[4 + a] = -(field[4 + a] + mean) * div
        for f in range(fields):
            force[pl.ds(at, span), f * lanes : (f + 1) * lanes] = out[f].astype(jnp.bfloat16)
        return carry

    lax.fori_loop(0, longitudes // span, synth, 0)

    def analyse(d, carry):
        at = pl.multiple_of(d * rows, 16)
        w = jnp.dot(ana_ref[pl.ds(at, rows), :], force[...], preferred_element_type=jnp.float32)
        for f in range(fields):
            lane = slice(f * lanes, (f + 1) * lanes)
            modes[pl.ds(at, rows), lane] = (w[:, lane] * weight).astype(jnp.bfloat16)
        return carry

    lax.fori_loop(0, sources, analyse, 0)
    for n in range(sources):
        at = pl.multiple_of(order_ref[n] * rows, 16)
        for f in range(fields):
            out_refs[n][f] = modes[pl.ds(at, rows), f * lanes : (f + 1) * lanes]


def semi_implicit_slabs(old, tend, degree, gm, hm, truncation):
    eig = wave_scale * (degree * (degree + 1)).astype(jnp.float32) / float(truncation * truncation)
    damping = 1.0 / (1.0 + diffusion * eig * eig)
    coupling = time_step * time_step * eig
    pm = [[gm[a][0] * hm[0][b] + gm[a][1] * hm[1][b] for b in range(2)] for a in range(2)]
    diag_one = 1.0 + coupling * pm[0][0]
    diag_two = 1.0 + coupling * pm[1][1]
    cross_one = coupling * pm[0][1]
    cross_two = coupling * pm[1][0]
    inverse = 1.0 / (diag_one * diag_two - cross_one * cross_two)
    out = [None] * 12
    for r in range(2):
        star = [old[c * 2 + r] + time_step * tend[c * 2 + r] for c in range(6)]
        right = [
            star[2 + a] + time_step * eig * (gm[a][0] * star[4] + gm[a][1] * star[5])
            for a in range(2)
        ]
        div = [
            (diag_two * right[0] - cross_one * right[1]) * inverse,
            (diag_one * right[1] - cross_two * right[0]) * inverse,
        ]
        for a in range(2):
            out[a * 2 + r] = damping * star[a]
            out[(2 + a) * 2 + r] = damping * div[a]
            out[(4 + a) * 2 + r] = damping * (
                star[4 + a] - time_step * (hm[a][0] * div[0] + hm[a][1] * div[1])
            )
    return out


def inverse_kernel(
    where_ref, gravity_ref, stability_ref, *refs, truncation, pairs, chunks, last, slots, count
):
    w_refs, refs = refs[: chunks * slots], refs[chunks * slots :]
    leg_refs, refs = refs[:chunks], refs[chunks:]
    spec_ref, refs = refs[0], refs[1:]
    if last:
        out_ref, ws, ten = refs
    else:
        fresh_refs, (out_ref, ws, ten, wide) = refs[:count], refs[count:]
    step = pl.program_id(0)
    row_length = truncation + 1
    trajectories, comps, block, _ = out_ref.shape
    rows = trajectories * comps
    tiles = ten.shape[0]
    padded = tiles * LANES

    @pl.when(step == 0)
    def _():
        if not last:
            for k in range(chunks):
                wide[k, row_length * block :, :] = jnp.zeros(
                    (wide.shape[1] - row_length * block, LANES), jnp.float32
                )
        for k in range(chunks):
            for n in range(slots):
                place = where_ref[1 + count + n]
                t, s = lax.div(place, 2), lax.rem(place, 2)
                base = pl.multiple_of((s * (2 * rows) + t * comps) * pairs, SUB)
                for f in range(comps // 2):
                    got = w_refs[k * slots + n][f].astype(jnp.float32)
                    for r in range(2):
                        for h in range(2):
                            at = (r * 2 + h) * pairs
                            ws[k, pl.ds(base + (h * rows + 2 * f + r) * pairs, pairs), :] = got[
                                at : at + pairs, :
                            ]

    if not last:
        for k in range(chunks):
            wide[k, : row_length * block, :] = (
                leg_refs[k][...].astype(jnp.float32).reshape(row_length * block, LANES)
            )
    first_pair = where_ref[0] + step * block

    def one(q, carry):
        at = pl.ds(step * block + q, 4 * rows, stride=pairs)
        lhs = jnp.concatenate([ws[k, at, :].astype(jnp.bfloat16) for k in range(chunks)], axis=1)
        if last:
            rhs = jnp.concatenate([leg_refs[k][q] for k in range(chunks)], axis=1)
        else:
            at = pl.ds(q, padded, stride=block)
            rhs = jnp.concatenate(
                [wide[k, at, :].astype(jnp.bfloat16) for k in range(chunks)], axis=1
            )
        got = lax.dot_general(
            lhs, rhs, (((1,), (1,)), ((), ())), preferred_element_type=jnp.float32
        )
        leading, odd, _ = layout_terms(first_pair + q, 1, 0, padded, truncation)
        north = jnp.where(leading, got[:rows], got[rows : 2 * rows])
        south = jnp.where(leading, got[2 * rows : 3 * rows], got[3 * rows :])
        total = north + jnp.where(odd, -south, south)
        for k in range(tiles):
            ten[k, pl.ds(q, rows, stride=block), :] = total[:, k * LANES : (k + 1) * LANES]
        return carry

    lax.fori_loop(0, block, one, 0, unroll=UNROLL_INVERSE)

    if last:
        gm = [[gravity_ref[a, b] for b in range(2)] for a in range(2)]
        hm = [[stability_ref[a, b] for b in range(2)] for a in range(2)]
    for k in range(tiles):
        width = min(LANES, row_length - k * LANES)
        lanes = slice(k * LANES, k * LANES + width)
        if last:
            _, _, degree = layout_terms(first_pair, block, k * LANES, width, truncation)

        def body(t, carry):
            tend = []
            for c in range(comps):
                at = pl.multiple_of((t * comps + c) * block, SUB)
                value = ten[k, pl.ds(at, block), :][:, :width]
                tend.append(value)
            old = [spec_ref[t, c, :, lanes] for c in range(comps)]
            if last:
                tend = semi_implicit_slabs(old, tend, degree, gm, hm, truncation)
            else:
                for i in range(count):
                    mine = where_ref[1 + i] == t
                    old = [jnp.where(mine, fresh_refs[i][c, :, lanes], old[c]) for c in range(comps)]
                tend = [old[c] + time_step * tend[c] for c in range(comps)]
            for c in range(comps):
                out_ref[t, c, :, lanes] = tend[c]
            return carry

        lax.fori_loop(0, trajectories, body, 0)


def fourier_tables(pair_count, groups, truncation, longitudes):
    index = jnp.arange(pair_count * 4, dtype=jnp.int32)
    local = pair_count // groups
    group = index // (4 * local)
    part = index // (2 * local) % 2
    half = index // local % 2
    pair = group * local + index % local
    order = jnp.where(half == 0, pair, truncation - 1 - pair)
    quarter = part * (longitudes // 4)
    half_turn = longitudes // 2
    column = jnp.arange(half_turn, dtype=jnp.int32)[None, :]
    phase = (order[:, None] * column + quarter[:, None]) % longitudes
    angle = phase.astype(jnp.float32) * (2.0 * math.pi / longitudes)
    first = jnp.cos(angle)
    second = jnp.where(order[:, None] % 2 == 0, first, -first)
    return jnp.concatenate([first, second], axis=1).astype(jnp.bfloat16)


def clone_routes(clones, local):
    members = lax.axis_size("member")
    me = lax.axis_index("member").astype(jnp.int32)
    owner = lax.div(clones, jnp.full_like(clones, local))
    index = clones - owner * local
    route = owner[:, 1] * members + owner[:, 0]
    slot = jnp.where(owner[:, 0] == me, index[:, 0], -1)
    return index[:, 1], owner[:, 1], route, slot


def send_clone(row, route):
    members = lax.axis_size("member")

    def move(a, b):
        if a == b:
            return lambda v: v
        return lambda v: lax.ppermute(v, "member", [(a, b)])

    branches = [move(a, b) for a in range(members) for b in range(members)]
    return lax.switch(route, branches, row)


def share_row(row, owner):
    members = lax.axis_size("member")
    differs = jnp.bitwise_xor(owner, lax.axis_index("member").astype(jnp.int32))
    bit = 1
    while bit < members:
        other = lax.ppermute(row, "member", [(m, m ^ bit) for m in range(members)])
        row = jnp.where(jnp.bitwise_and(differs, bit) != 0, other, row)
        bit *= 2
    return row


def shards(spectra, legendre, sin_lat, gravity, stability, clones):
    trajectories, comps, pairs, row_length = spectra.shape
    truncation = row_length - 1
    half_lat = legendre.shape[2]
    longitudes = LONGITUDES_PER_WAVE * truncation
    space = lax.axis_size("space")
    position = lax.axis_index("space")
    fields = comps // 2
    split = space // (2 * trajectories)
    lane_count = LANES // split
    chunk_count = half_lat // LANES
    padded_pairs = -(-pairs // SUB) * SUB
    steps = padded_pairs // SUB
    tiles = -(-row_length // LANES)
    extra = padded_pairs - pairs
    rows = trajectories * comps

    survivor, owner, route, slot = clone_routes(clones, trajectories)
    count = clones.shape[0]
    living = [
        lax.dynamic_index_in_dim(spectra, survivor[i], 0, keepdims=False) for i in range(count)
    ]
    fresh_narrow = [send_clone(living[i].astype(jnp.bfloat16), route[i]) for i in range(count)]
    state = spectra
    if extra:
        state = jnp.pad(state, ((0, 0), (0, 0), (0, extra), (0, 0)))
        fresh_narrow = [jnp.pad(x, ((0, 0), (0, extra), (0, 0))) for x in fresh_narrow]
    slots = 2 * trajectories
    direct = split == 1
    if direct:
        order = jnp.bitwise_xor(position.astype(jnp.int32), jnp.arange(space, dtype=jnp.int32))
        slot_order = order
    else:
        order = jnp.arange(space, dtype=jnp.int32)
        slot_order = jnp.arange(slots, dtype=jnp.int32)
    where = jnp.concatenate([(position * pairs).astype(jnp.int32).reshape(1), slot, slot_order])
    columns = jnp.transpose(legendre, (1, 0, 2))
    if extra:
        columns = jnp.pad(columns, ((0, 0), (0, extra), (0, 0)))

    smem = pl.BlockSpec(memory_space=pltpu.SMEM)
    state_spec = pl.BlockSpec((trajectories, comps, SUB, row_length), lambda i: (0, 0, i, 0))
    fresh_spec = pl.BlockSpec((comps, SUB, row_length), lambda i: (0, i, 0))
    kept_spec = pl.BlockSpec((SUB, tiles * LANES, LANES), lambda i: (i, 0, 0))
    part_shape = (fields, 4 * padded_pairs, LANES)
    part_spec = pl.BlockSpec(part_shape, lambda i: (0, 0, 0))

    def leg_spec(k):
        return pl.BlockSpec((row_length, SUB, LANES), lambda i: (0, i, k))

    mib = 1024 * 1024

    def forward(k, where):
        keep = k > 0
        kept_shape = jax.ShapeDtypeStruct((padded_pairs, tiles * LANES, LANES), jnp.bfloat16)
        return pl.pallas_call(
            functools.partial(
                forward_kernel, truncation=truncation, pairs=padded_pairs, keep=keep, count=count
            ),
            out_shape=[jax.ShapeDtypeStruct(part_shape, jnp.bfloat16)] * slots
            + [kept_shape] * keep,
            grid=(steps,),
            in_specs=[smem, state_spec, leg_spec(k)] + [fresh_spec] * count,
            out_specs=[part_spec] * slots + [kept_spec] * keep,
            scratch_shapes=[
                pltpu.VMEM((tiles * LANES * SUB, LANES), jnp.float32),
                pltpu.VMEM((tiles, rows * SUB, LANES), jnp.float32),
                pltpu.VMEM((4 * rows * padded_pairs, LANES), jnp.float32),
            ],
            compiler_params=pltpu.CompilerParams(vmem_limit_bytes=60 * mib),
            cost_estimate=pl.CostEstimate(
                flops=8 * rows * padded_pairs * row_length * LANES,
                bytes_accessed=16 * 1024 * 1024,
                transcendentals=0,
            ),
            name="forward",
        )(where, state, columns, *fresh_narrow)

    def to_wire(x):
        if extra:
            x = x.reshape(slots, fields, 4, padded_pairs, LANES)[:, :, :, :pairs]
        x = x.reshape(slots, fields, 4 * pairs, split, lane_count)
        return jnp.transpose(x, (0, 3, 1, 2, 4)).reshape(space, fields, 4 * pairs, lane_count)

    def from_wire(x):
        x = x.reshape(slots, split, fields, 4, pairs, lane_count)
        x = jnp.transpose(x, (0, 2, 3, 4, 1, 5)).reshape(slots, fields, 4, pairs, LANES)
        if extra:
            x = jnp.pad(x, ((0, 0), (0, 0), (0, 0), (0, extra), (0, 0)))
        return x.reshape((slots,) + part_shape)

    def exchange(x):
        return lax.all_to_all(x, "space", split_axis=0, concat_axis=0, tiled=True)

    def swap(parts):
        return [
            lax.ppermute(x, "space", [(d, d ^ n) for d in range(space)]) if n else x
            for n, x in enumerate(parts)
        ]

    def spread(parts):
        if direct:
            return swap(parts)
        x = exchange(to_wire(jnp.stack(parts)))
        x = jnp.pad(x, ((0, 0), (0, 0), (0, 0), (0, LANES - lane_count)))
        return [x[d] for d in range(space)]

    def collect(parts):
        if direct:
            return swap(parts)
        x = from_wire(exchange(jnp.stack(parts)[..., :lane_count]))
        return [x[n] for n in range(slots)]

    analysis = lax.optimization_barrier(
        fourier_tables(pairs * space, space, truncation, longitudes)
    )
    synthesis = analysis.T
    south = position // split % 2
    hemisphere = jnp.where(south == 0, sin_lat, -sin_lat)
    weights_all = math.pi * jnp.sqrt(1.0 - hemisphere * hemisphere) / (2 * half_lat)
    vmem = pl.BlockSpec(memory_space=pltpu.VMEM)
    modes = 4 * pairs * space

    def grid(k, parts):
        first = k * LANES + position % split * lane_count
        mu = lax.dynamic_slice_in_dim(hemisphere, first, lane_count)
        weight = lax.dynamic_slice_in_dim(weights_all, first, lane_count)
        short = LANES - lane_count
        if short:
            mu = jnp.pad(mu, (0, short))
            weight = jnp.pad(weight, (0, short))
        return pl.pallas_call(
            functools.partial(grid_kernel, scale=1.0 / truncation),
            out_shape=[jax.ShapeDtypeStruct(x.shape, jnp.bfloat16) for x in parts],
            in_specs=[smem] + [vmem] * (4 + space),
            out_specs=[vmem] * space,
            scratch_shapes=[
                pltpu.VMEM((modes, fields * LANES), jnp.bfloat16),
                pltpu.VMEM((longitudes, fields * LANES), jnp.bfloat16),
            ],
            compiler_params=pltpu.CompilerParams(vmem_limit_bytes=60 * mib),
            cost_estimate=pl.CostEstimate(
                flops=4 * modes * longitudes * fields * LANES,
                bytes_accessed=12 * 1024 * 1024,
                transcendentals=0,
            ),
            name="grid",
        )(order, (2.0 * mu)[None], weight[None], synthesis, analysis, *parts)

    def inverse(ws, legs, start, patches):
        chunks = len(ws)
        last = not patches
        wide_scratch = pltpu.VMEM((chunks, tiles * LANES * SUB, LANES), jnp.float32)
        return pl.pallas_call(
            functools.partial(
                inverse_kernel,
                truncation=truncation,
                pairs=padded_pairs,
                chunks=chunks,
                last=last,
                slots=slots,
                count=count,
            ),
            out_shape=jax.ShapeDtypeStruct(state.shape, jnp.float32),
            grid=(steps,),
            in_specs=[smem] * 3
            + [part_spec] * (chunks * slots)
            + ([kept_spec] * chunks if last else [leg_spec(k) for k in range(chunks)])
            + [state_spec]
            + [fresh_spec] * len(patches),
            out_specs=state_spec,
            scratch_shapes=[
                pltpu.VMEM((chunks, 4 * rows * padded_pairs, LANES), jnp.float32),
                pltpu.VMEM((tiles, rows * SUB, LANES), jnp.float32),
            ]
            + ([] if last else [wide_scratch]),
            compiler_params=pltpu.CompilerParams(vmem_limit_bytes=60 * mib),
            cost_estimate=pl.CostEstimate(
                flops=8 * rows * padded_pairs * row_length * LANES * chunks,
                bytes_accessed=20 * 1024 * 1024,
                transcendentals=0,
            ),
            name="inverse",
        )(where, gravity, stability, *[x for w in ws for x in w], *legs, start, *patches)

    made, turn = [], where
    for k in range(chunk_count):
        made.append(list(forward(k, turn)))
        turn, made[-1][0] = lax.optimization_barrier((where, made[-1][0]))
    kept = [x[-1] for x in made[1:]]
    sent = []
    for x in made:
        sent.append(spread(x[:slots]))
    wide, _ = lax.optimization_barrier((living, made[1][0]))
    fresh = [share_row(wide[i], owner[i]) for i in range(count)]
    if extra:
        fresh = [jnp.pad(x, ((0, 0), (0, extra), (0, 0))) for x in fresh]
    back = []
    for k in range(chunk_count):
        got = grid(k, sent[k])
        back.append(collect(got))
    start = inverse(back[:1], [columns], state, fresh)
    out = inverse(back[1:], kept, start, [])
    return out[:, :, :pairs] if extra else out


def solution(mesh):
    placed = (P("member", None, "space", None), P("space", None, None), P(), P(), P(), P())
    return jax.shard_map(
        shards,
        mesh=mesh,
        in_specs=placed,
        out_specs=P("member", None, "space", None),
        check_vma=False,
    )
```

```python
import functools
import math

import jax
import jax.numpy as jnp
from jax import lax
from jax.experimental import pallas as pl
from jax.experimental.pallas import tpu as pltpu
from jax.sharding import PartitionSpec as P


LANES = 128
SUB = 8
PACKED = 16
UNROLL_FORWARD = 8
UNROLL_INVERSE = 8
LONGITUDES_PER_WAVE = 2

time_step = 0.25
wave_scale = 16.0
diffusion = 0.02


def layout_terms(first_pair, count, lane0, lanes, truncation):
    pair = first_pair + lax.broadcasted_iota(jnp.int32, (count, lanes), 0)
    column = lane0 + lax.broadcasted_iota(jnp.int32, (count, lanes), 1)
    leading = column < truncation - pair
    offset = jnp.where(leading, column, column - (truncation - pair))
    order = jnp.where(leading, pair, truncation - 1 - pair)
    return leading, (offset & 1) == 1, order + offset


def forward_kernel(where_ref, spec_ref, leg_ref, *refs, truncation, pairs, keep, count):
    step = pl.program_id(0)
    row_length = truncation + 1
    trajectories, comps, block, _ = spec_ref.shape
    rows = trajectories * comps
    slots = 2 * trajectories
    fresh_refs, refs = refs[:count], refs[count:]
    out_refs, refs = refs[:slots], refs[slots:]
    if keep:
        keep_ref, refs = refs[0], refs[1:]
    wide, xs, res = refs
    tiles = xs.shape[0]
    padded = tiles * LANES

    @pl.when(step == 0)
    def _():
        wide[row_length * block :, :] = jnp.zeros(
            (wide.shape[0] - row_length * block, LANES), jnp.float32
        )

    wide[: row_length * block, :] = (
        leg_ref[...].astype(jnp.float32).reshape(row_length * block, LANES)
    )
    for k in range(tiles):
        width = min(LANES, row_length - k * LANES)
        lanes = slice(k * LANES, k * LANES + width)
        if width < LANES:
            xs[k] = jnp.zeros((rows * block, LANES), jnp.float32)
        xs[k, :, :width] = spec_ref[:, :, :, lanes].reshape(rows * block, width)

    for i in range(count):
        slot = where_ref[1 + i]

        @pl.when(slot >= 0)
        def _():
            at = pl.multiple_of(slot * comps * block, SUB)
            for k in range(tiles):
                width = min(LANES, row_length - k * LANES)
                fresh = fresh_refs[i][:, :, k * LANES : k * LANES + width].astype(jnp.float32)
                xs[k, pl.ds(at, comps * block), :width] = fresh.reshape(comps * block, width)

    first_pair = where_ref[0] + step * block

    def one(q, carry):
        x = jnp.concatenate(
            [xs[k, pl.ds(q, rows, stride=block), :] for k in range(tiles)], axis=1
        )
        x = x.astype(jnp.bfloat16)
        edge = truncation - first_pair - q
        column = lax.broadcasted_iota(jnp.int32, (PACKED, padded), 1)
        leading = column < edge
        odd = (jnp.where(leading, column, column - edge) & 1) == 1
        sign = jnp.where(odd, -1.0, 1.0)
        factors = [
            jnp.where(leading, 1.0, 0.0),
            jnp.where(leading, 0.0, 1.0),
            jnp.where(leading, sign, 0.0),
            jnp.where(leading, 0.0, sign),
        ]
        lhs = []
        for factor in factors:
            factor = factor.astype(jnp.bfloat16)
            for at in range(0, rows, PACKED):
                lhs.append(x[at : at + PACKED] * factor)
        lhs = jnp.concatenate(lhs, axis=0)
        rhs = wide[pl.ds(q, padded, stride=block), :].astype(jnp.bfloat16)
        if keep:
            keep_ref[q] = rhs
        got = jnp.dot(lhs, rhs, preferred_element_type=jnp.float32)
        res[pl.ds(step * block + q, 4 * rows, stride=pairs), :] = got
        return carry

    lax.fori_loop(0, block, one, 0, unroll=UNROLL_FORWARD)

    @pl.when(step == pl.num_programs(0) - 1)
    def _():
        for n in range(slots):
            place = where_ref[1 + count + n]
            t, s = lax.div(place, 2), lax.rem(place, 2)
            base = pl.multiple_of((s * (2 * rows) + t * comps) * pairs, SUB)
            for f in range(comps // 2):
                parts = []
                for r in range(2):
                    for h in range(2):
                        parts.append(res[pl.ds(base + (h * rows + 2 * f + r) * pairs, pairs), :])
                out_refs[n][f] = jnp.concatenate(parts, axis=0).astype(jnp.bfloat16)


def grid_kernel(order_ref, cor_ref, weight_ref, syn_ref, ana_ref, *refs, scale):
    sources = order_ref.shape[0]
    in_refs, out_refs, (modes, force) = refs[:sources], refs[sources:-2], refs[-2:]
    fields, rows, lanes = in_refs[0].shape
    longitudes = syn_ref.shape[0]
    for n in range(sources):
        at = pl.multiple_of(order_ref[n] * rows, 16)
        for f in range(fields):
            modes[pl.ds(at, rows), f * lanes : (f + 1) * lanes] = in_refs[n][f]
    cor = cor_ref[...]
    weight = weight_ref[...]
    span = 128

    def synth(b, carry):
        at = pl.multiple_of(b * span, span)
        g = (
            jnp.dot(syn_ref[pl.ds(at, span), :], modes[...], preferred_element_type=jnp.float32)
            * scale
        )
        field = [g[:, f * lanes : (f + 1) * lanes] for f in range(fields)]
        mean = 0.5 * (field[4] + field[5])
        out = [None] * fields
        for a in range(2):
            spin = field[a] + cor
            div = field[2 + a]
            out[a] = -spin * div
            out[2 + a] = spin * field[a] - 0.5 * div * div
            out[4 + a] = -(field[4 + a] + mean) * div
        for f in range(fields):
            force[pl.ds(at, span), f * lanes : (f + 1) * lanes] = out[f].astype(jnp.bfloat16)
        return carry

    lax.fori_loop(0, longitudes // span, synth, 0)

    def analyse(d, carry):
        at = pl.multiple_of(d * rows, 16)
        w = jnp.dot(ana_ref[pl.ds(at, rows), :], force[...], preferred_element_type=jnp.float32)
        for f in range(fields):
            lane = slice(f * lanes, (f + 1) * lanes)
            modes[pl.ds(at, rows), lane] = (w[:, lane] * weight).astype(jnp.bfloat16)
        return carry

    lax.fori_loop(0, sources, analyse, 0)
    for n in range(sources):
        at = pl.multiple_of(order_ref[n] * rows, 16)
        for f in range(fields):
            out_refs[n][f] = modes[pl.ds(at, rows), f * lanes : (f + 1) * lanes]


def step_terms(degree, gm, hm, truncation):
    eig = wave_scale * (degree * (degree + 1)).astype(jnp.float32) / float(truncation * truncation)
    damping = 1.0 / (1.0 + diffusion * eig * eig)
    coupling = time_step * time_step * eig
    pm = [[gm[a][0] * hm[0][b] + gm[a][1] * hm[1][b] for b in range(2)] for a in range(2)]
    diag = [1.0 + coupling * pm[a][a] for a in range(2)]
    cross = [coupling * pm[0][1], coupling * pm[1][0]]
    inverse = 1.0 / (diag[0] * diag[1] - cross[0] * cross[1])
    solve = [
        [diag[1] * inverse, -cross[0] * inverse],
        [-cross[1] * inverse, diag[0] * inverse],
    ]
    push = [[time_step * eig * gm[a][b] for b in range(2)] for a in range(2)]
    return damping, solve, push


def semi_implicit_slabs(old, tend, terms, hm):
    damping, solve, push = terms
    out = [None] * 12
    for r in range(2):
        star = [old[c * 2 + r] + time_step * tend[c * 2 + r] for c in range(6)]
        right = [star[2 + a] + push[a][0] * star[4] + push[a][1] * star[5] for a in range(2)]
        div = [solve[a][0] * right[0] + solve[a][1] * right[1] for a in range(2)]
        for a in range(2):
            heat = (time_step * hm[a][0]) * div[0] + (time_step * hm[a][1]) * div[1]
            out[a * 2 + r] = damping * star[a]
            out[(2 + a) * 2 + r] = damping * div[a]
            out[(4 + a) * 2 + r] = damping * (star[4 + a] - heat)
    return out


def inverse_kernel(
    where_ref, gravity_ref, stability_ref, *refs, truncation, pairs, chunks, last, slots, count
):
    w_refs, refs = refs[: chunks * slots], refs[chunks * slots :]
    leg_refs, refs = refs[:chunks], refs[chunks:]
    spec_ref, refs = refs[0], refs[1:]
    if last:
        out_ref, ws, ten = refs
    else:
        fresh_refs, (out_ref, ws, ten, wide) = refs[:count], refs[count:]
    step = pl.program_id(0)
    row_length = truncation + 1
    trajectories, comps, block, _ = out_ref.shape
    rows = trajectories * comps
    tiles = ten.shape[0]
    padded = tiles * LANES

    @pl.when(step == 0)
    def _():
        if not last:
            for k in range(chunks):
                wide[k, row_length * block :, :] = jnp.zeros(
                    (wide.shape[1] - row_length * block, LANES), jnp.float32
                )
        for k in range(chunks):
            for n in range(slots):
                place = where_ref[1 + count + n]
                t, s = lax.div(place, 2), lax.rem(place, 2)
                base = pl.multiple_of((s * (2 * rows) + t * comps) * pairs, SUB)
                for f in range(comps // 2):
                    got = w_refs[k * slots + n][f].astype(jnp.float32)
                    for r in range(2):
                        for h in range(2):
                            at = (r * 2 + h) * pairs
                            ws[k, pl.ds(base + (h * rows + 2 * f + r) * pairs, pairs), :] = got[
                                at : at + pairs, :
                            ]

    if not last:
        for k in range(chunks):
            wide[k, : row_length * block, :] = (
                leg_refs[k][...].astype(jnp.float32).reshape(row_length * block, LANES)
            )
    first_pair = where_ref[0] + step * block

    def one(q, carry):
        at = pl.ds(step * block + q, 4 * rows, stride=pairs)
        lhs = jnp.concatenate([ws[k, at, :].astype(jnp.bfloat16) for k in range(chunks)], axis=1)
        if last:
            rhs = jnp.concatenate([leg_refs[k][q] for k in range(chunks)], axis=1)
        else:
            at = pl.ds(q, padded, stride=block)
            rhs = jnp.concatenate(
                [wide[k, at, :].astype(jnp.bfloat16) for k in range(chunks)], axis=1
            )
        got = lax.dot_general(
            lhs, rhs, (((1,), (1,)), ((), ())), preferred_element_type=jnp.float32
        )
        leading, odd, _ = layout_terms(first_pair + q, 1, 0, padded, truncation)
        north = jnp.where(leading, got[:rows], got[rows : 2 * rows])
        south = jnp.where(leading, got[2 * rows : 3 * rows], got[3 * rows :])
        total = north + jnp.where(odd, -south, south)
        for k in range(tiles):
            ten[k, pl.ds(q, rows, stride=block), :] = total[:, k * LANES : (k + 1) * LANES]
        return carry

    lax.fori_loop(0, block, one, 0, unroll=UNROLL_INVERSE)

    if last:
        gm = [[gravity_ref[a, b] for b in range(2)] for a in range(2)]
        hm = [[stability_ref[a, b] for b in range(2)] for a in range(2)]
    for k in range(tiles):
        width = min(LANES, row_length - k * LANES)
        lanes = slice(k * LANES, k * LANES + width)
        if last:
            _, _, degree = layout_terms(first_pair, block, k * LANES, width, truncation)
            terms = step_terms(degree, gm, hm, truncation)

        def body(t, carry):
            tend = []
            for c in range(comps):
                at = pl.multiple_of((t * comps + c) * block, SUB)
                value = ten[k, pl.ds(at, block), :][:, :width]
                tend.append(value)
            old = [spec_ref[t, c, :, lanes] for c in range(comps)]
            if last:
                tend = semi_implicit_slabs(old, tend, terms, hm)
            else:
                for i in range(count):
                    mine = where_ref[1 + i] == t
                    old = [jnp.where(mine, fresh_refs[i][c, :, lanes], old[c]) for c in range(comps)]
                tend = [old[c] + time_step * tend[c] for c in range(comps)]
            for c in range(comps):
                out_ref[t, c, :, lanes] = tend[c]
            return carry

        lax.fori_loop(0, trajectories, body, 0)


def fourier_tables(pair_count, groups, truncation, longitudes):
    index = jnp.arange(pair_count * 4, dtype=jnp.int32)
    local = pair_count // groups
    group = index // (4 * local)
    part = index // (2 * local) % 2
    half = index // local % 2
    pair = group * local + index % local
    order = jnp.where(half == 0, pair, truncation - 1 - pair)
    quarter = part * (longitudes // 4)
    half_turn = longitudes // 2
    column = jnp.arange(half_turn, dtype=jnp.int32)[None, :]
    phase = (order[:, None] * column + quarter[:, None]) % longitudes
    angle = phase.astype(jnp.float32) * (2.0 * math.pi / longitudes)
    first = jnp.cos(angle)
    second = jnp.where(order[:, None] % 2 == 0, first, -first)
    return jnp.concatenate([first, second], axis=1).astype(jnp.bfloat16)


def pick_kernel(clones_ref, me_ref, spec_ref, row_ref, route_ref, slot_ref, *, members):
    i = pl.program_id(0)
    local = me_ref[1]
    row_ref[...] = spec_ref[...].astype(jnp.bfloat16)
    source = lax.div(clones_ref[i, 1], local)
    target = lax.div(clones_ref[i, 0], local)
    route_ref[i] = source * members + target
    slot_ref[i] = jnp.where(target == me_ref[0], clones_ref[i, 0] - target * local, -1)


def pick_clones(spectra, clones):
    local, comps, pairs, row_length = spectra.shape
    count = clones.shape[0]
    me = lax.axis_index("member").astype(jnp.int32)
    smem = pl.BlockSpec(memory_space=pltpu.SMEM)
    block = (1, comps, pairs, row_length)
    return pl.pallas_call(
        functools.partial(pick_kernel, members=lax.axis_size("member")),
        out_shape=[
            jax.ShapeDtypeStruct((count,) + block[1:], jnp.bfloat16),
            jax.ShapeDtypeStruct((count,), jnp.int32),
            jax.ShapeDtypeStruct((count,), jnp.int32),
        ],
        grid_spec=pltpu.PrefetchScalarGridSpec(
            num_scalar_prefetch=2,
            grid=(count,),
            in_specs=[
                pl.BlockSpec(block, lambda i, c, m: (lax.rem(c[i, 1], m[1]), 0, 0, 0)),
            ],
            out_specs=[pl.BlockSpec(block, lambda i, c, m: (i, 0, 0, 0)), smem, smem],
        ),
        cost_estimate=pl.CostEstimate(
            flops=0, bytes_accessed=6 * 1024 * 1024, transcendentals=0
        ),
        name="pick",
    )(clones, jnp.stack([me, jnp.int32(local)]), spectra)


def send_clone(row, route):
    members = lax.axis_size("member")

    def move(a, b):
        if a == b:
            return lambda v: v
        return lambda v: lax.ppermute(v, "member", [(a, b)])

    branches = [move(a, b) for a in range(members) for b in range(members)]
    return lax.switch(route, branches, row)


def share_row(row, owner):
    members = lax.axis_size("member")
    differs = jnp.bitwise_xor(owner, lax.axis_index("member").astype(jnp.int32))
    bit = 1
    while bit < members:
        other = lax.ppermute(row, "member", [(m, m ^ bit) for m in range(members)])
        row = jnp.where(jnp.bitwise_and(differs, bit) != 0, other, row)
        bit *= 2
    return row


def shards(spectra, legendre, sin_lat, gravity, stability, clones):
    trajectories, comps, pairs, row_length = spectra.shape
    truncation = row_length - 1
    half_lat = legendre.shape[2]
    longitudes = LONGITUDES_PER_WAVE * truncation
    space = lax.axis_size("space")
    position = lax.axis_index("space")
    fields = comps // 2
    split = space // (2 * trajectories)
    lane_count = LANES // split
    chunk_count = half_lat // LANES
    padded_pairs = -(-pairs // SUB) * SUB
    steps = padded_pairs // SUB
    tiles = -(-row_length // LANES)
    extra = padded_pairs - pairs
    rows = trajectories * comps

    count = clones.shape[0]
    picked, route, slot = pick_clones(spectra, clones)
    fresh_narrow = [send_clone(picked[i], route[i]) for i in range(count)]
    state = spectra
    if extra:
        state = jnp.pad(state, ((0, 0), (0, 0), (0, extra), (0, 0)))
        fresh_narrow = [jnp.pad(x, ((0, 0), (0, extra), (0, 0))) for x in fresh_narrow]
    slots = 2 * trajectories
    direct = split == 1
    if direct:
        order = jnp.bitwise_xor(position.astype(jnp.int32), jnp.arange(space, dtype=jnp.int32))
        slot_order = order
    else:
        order = jnp.arange(space, dtype=jnp.int32)
        slot_order = jnp.arange(slots, dtype=jnp.int32)
    where = jnp.concatenate([(position * pairs).astype(jnp.int32).reshape(1), slot, slot_order])
    columns = jnp.transpose(legendre, (1, 0, 2))
    if extra:
        columns = jnp.pad(columns, ((0, 0), (0, extra), (0, 0)))

    smem = pl.BlockSpec(memory_space=pltpu.SMEM)
    state_spec = pl.BlockSpec((trajectories, comps, SUB, row_length), lambda i: (0, 0, i, 0))
    fresh_spec = pl.BlockSpec((comps, SUB, row_length), lambda i: (0, i, 0))
    kept_spec = pl.BlockSpec((SUB, tiles * LANES, LANES), lambda i: (i, 0, 0))
    part_shape = (fields, 4 * padded_pairs, LANES)
    part_spec = pl.BlockSpec(part_shape, lambda i: (0, 0, 0))

    def leg_spec(k):
        return pl.BlockSpec((row_length, SUB, LANES), lambda i: (0, i, k))

    mib = 1024 * 1024

    def forward(k, where):
        keep = k > 0
        kept_shape = jax.ShapeDtypeStruct((padded_pairs, tiles * LANES, LANES), jnp.bfloat16)
        return pl.pallas_call(
            functools.partial(
                forward_kernel, truncation=truncation, pairs=padded_pairs, keep=keep, count=count
            ),
            out_shape=[jax.ShapeDtypeStruct(part_shape, jnp.bfloat16)] * slots
            + [kept_shape] * keep,
            grid=(steps,),
            in_specs=[smem, state_spec, leg_spec(k)] + [fresh_spec] * count,
            out_specs=[part_spec] * slots + [kept_spec] * keep,
            scratch_shapes=[
                pltpu.VMEM((tiles * LANES * SUB, LANES), jnp.float32),
                pltpu.VMEM((tiles, rows * SUB, LANES), jnp.float32),
                pltpu.VMEM((4 * rows * padded_pairs, LANES), jnp.float32),
            ],
            compiler_params=pltpu.CompilerParams(vmem_limit_bytes=60 * mib),
            cost_estimate=pl.CostEstimate(
                flops=8 * rows * padded_pairs * row_length * LANES,
                bytes_accessed=16 * 1024 * 1024,
                transcendentals=0,
            ),
            name="forward",
        )(where, state, columns, *fresh_narrow)

    def to_wire(x):
        if extra:
            x = x.reshape(slots, fields, 4, padded_pairs, LANES)[:, :, :, :pairs]
        x = x.reshape(slots, fields, 4 * pairs, split, lane_count)
        return jnp.transpose(x, (0, 3, 1, 2, 4)).reshape(space, fields, 4 * pairs, lane_count)

    def from_wire(x):
        x = x.reshape(slots, split, fields, 4, pairs, lane_count)
        x = jnp.transpose(x, (0, 2, 3, 4, 1, 5)).reshape(slots, fields, 4, pairs, LANES)
        if extra:
            x = jnp.pad(x, ((0, 0), (0, 0), (0, 0), (0, extra), (0, 0)))
        return x.reshape((slots,) + part_shape)

    def exchange(x):
        return lax.all_to_all(x, "space", split_axis=0, concat_axis=0, tiled=True)

    def swap(parts):
        got = list(parts)
        for n in reversed(range(1, space)):
            got[n] = lax.ppermute(parts[n], "space", [(d, d ^ n) for d in range(space)])
        return got

    def spread(parts):
        if direct:
            return swap(parts)
        x = exchange(to_wire(jnp.stack(parts)))
        x = jnp.pad(x, ((0, 0), (0, 0), (0, 0), (0, LANES - lane_count)))
        return [x[d] for d in range(space)]

    def collect(parts):
        if direct:
            return swap(parts)
        x = from_wire(exchange(jnp.stack(parts)[..., :lane_count]))
        return [x[n] for n in range(slots)]

    analysis = lax.optimization_barrier(
        fourier_tables(pairs * space, space, truncation, longitudes)
    )
    synthesis = analysis.T
    south = position // split % 2
    hemisphere = jnp.where(south == 0, sin_lat, -sin_lat)
    weights_all = math.pi * jnp.sqrt(1.0 - hemisphere * hemisphere) / (2 * half_lat)
    vmem = pl.BlockSpec(memory_space=pltpu.VMEM)
    modes = 4 * pairs * space

    def grid(k, parts):
        first = k * LANES + position % split * lane_count
        mu = lax.dynamic_slice_in_dim(hemisphere, first, lane_count)
        weight = lax.dynamic_slice_in_dim(weights_all, first, lane_count)
        short = LANES - lane_count
        if short:
            mu = jnp.pad(mu, (0, short))
            weight = jnp.pad(weight, (0, short))
        return pl.pallas_call(
            functools.partial(grid_kernel, scale=1.0 / truncation),
            out_shape=[jax.ShapeDtypeStruct(x.shape, jnp.bfloat16) for x in parts],
            in_specs=[smem] + [vmem] * (4 + space),
            out_specs=[vmem] * space,
            scratch_shapes=[
                pltpu.VMEM((modes, fields * LANES), jnp.bfloat16),
                pltpu.VMEM((longitudes, fields * LANES), jnp.bfloat16),
            ],
            compiler_params=pltpu.CompilerParams(vmem_limit_bytes=60 * mib),
            cost_estimate=pl.CostEstimate(
                flops=4 * modes * longitudes * fields * LANES,
                bytes_accessed=12 * 1024 * 1024,
                transcendentals=0,
            ),
            name="grid",
        )(order, (2.0 * mu)[None], weight[None], synthesis, analysis, *parts)

    def inverse(ws, legs, start, patches):
        chunks = len(ws)
        last = not patches
        wide_scratch = pltpu.VMEM((chunks, tiles * LANES * SUB, LANES), jnp.float32)
        return pl.pallas_call(
            functools.partial(
                inverse_kernel,
                truncation=truncation,
                pairs=padded_pairs,
                chunks=chunks,
                last=last,
                slots=slots,
                count=count,
            ),
            out_shape=jax.ShapeDtypeStruct(state.shape, jnp.float32),
            grid=(steps,),
            in_specs=[smem] * 3
            + [part_spec] * (chunks * slots)
            + ([kept_spec] * chunks if last else [leg_spec(k) for k in range(chunks)])
            + [state_spec]
            + [fresh_spec] * len(patches),
            out_specs=state_spec,
            scratch_shapes=[
                pltpu.VMEM((chunks, 4 * rows * padded_pairs, LANES), jnp.float32),
                pltpu.VMEM((tiles, rows * SUB, LANES), jnp.float32),
            ]
            + ([] if last else [wide_scratch]),
            compiler_params=pltpu.CompilerParams(vmem_limit_bytes=60 * mib),
            cost_estimate=pl.CostEstimate(
                flops=8 * rows * padded_pairs * row_length * LANES * chunks,
                bytes_accessed=20 * 1024 * 1024,
                transcendentals=0,
            ),
            name="inverse",
        )(where, gravity, stability, *[x for w in ws for x in w], *legs, start, *patches)

    made, turn = [], where
    for k in range(chunk_count):
        made.append(list(forward(k, turn)))
        turn, made[-1][0] = lax.optimization_barrier((where, made[-1][0]))
    kept = [x[-1] for x in made[1:]]
    sent = []
    for x in made:
        sent.append(spread(x[:slots]))
    later, _ = lax.optimization_barrier((clones[:, 1], made[1][0]))
    fresh = [
        share_row(
            lax.dynamic_index_in_dim(spectra, lax.rem(later[i], trajectories), 0, keepdims=False),
            lax.div(later[i], trajectories),
        )
        for i in range(count)
    ]
    if extra:
        fresh = [jnp.pad(x, ((0, 0), (0, extra), (0, 0))) for x in fresh]
    back = []
    for k in range(chunk_count):
        got = grid(k, sent[k])
        back.append(collect(got))
    start = inverse(back[:1], [columns], state, fresh)
    out = inverse(back[1:], kept, start, [])
    return out[:, :, :pairs] if extra else out


def solution(mesh):
    placed = (P("member", None, "space", None), P("space", None, None), P(), P(), P(), P())
    return jax.shard_map(
        shards,
        mesh=mesh,
        in_specs=placed,
        out_specs=P("member", None, "space", None),
        check_vma=False,
    )
```

```python
import functools
import math

import jax
import jax.numpy as jnp
from jax import lax
from jax.experimental import pallas as pl
from jax.experimental.pallas import tpu as pltpu
from jax.sharding import PartitionSpec as P


LANES = 128
SUB = 8
PACKED = 16
UNROLL_FORWARD = 8
UNROLL_INVERSE = 8
LONGITUDES_PER_WAVE = 2

time_step = 0.25
wave_scale = 16.0
diffusion = 0.02


def layout_terms(first_pair, count, lane0, lanes, truncation):
    pair = first_pair + lax.broadcasted_iota(jnp.int32, (count, lanes), 0)
    column = lane0 + lax.broadcasted_iota(jnp.int32, (count, lanes), 1)
    leading = column < truncation - pair
    offset = jnp.where(leading, column, column - (truncation - pair))
    order = jnp.where(leading, pair, truncation - 1 - pair)
    return leading, (offset & 1) == 1, order + offset


def forward_kernel(
    where_ref, spec_ref, leg_ref, *refs, truncation, pairs, keep, count, made, span
):
    step = pl.program_id(0)
    row_length = truncation + 1
    _, comps, block, _ = spec_ref.shape
    rows = span * comps
    fresh_refs, refs = refs[:count], refs[count:]
    out_refs, refs = refs[: len(made)], refs[len(made) :]
    if keep:
        keep_ref, refs = refs[0], refs[1:]
    wide, xs, res = refs
    tiles = xs.shape[0]
    padded = tiles * LANES
    first_place = lax.div(where_ref[1 + count + made[0]], 2)
    t0 = lax.div(first_place, span) * span

    @pl.when(step == 0)
    def _():
        wide[row_length * block :, :] = jnp.zeros(
            (wide.shape[0] - row_length * block, LANES), jnp.float32
        )

    wide[: row_length * block, :] = (
        leg_ref[...].astype(jnp.float32).reshape(row_length * block, LANES)
    )
    for k in range(tiles):
        width = min(LANES, row_length - k * LANES)
        lanes = slice(k * LANES, k * LANES + width)
        if width < LANES:
            xs[k] = jnp.zeros((rows * block, LANES), jnp.float32)
        xs[k, :, :width] = spec_ref[pl.ds(t0, span), :, :, lanes].reshape(rows * block, width)

    for i in range(count):
        slot = where_ref[1 + i] - t0

        @pl.when(jnp.logical_and(slot >= 0, slot < span))
        def _():
            at = pl.multiple_of(slot * comps * block, SUB)
            for k in range(tiles):
                width = min(LANES, row_length - k * LANES)
                fresh = fresh_refs[i][:, :, k * LANES : k * LANES + width].astype(jnp.float32)
                xs[k, pl.ds(at, comps * block), :width] = fresh.reshape(comps * block, width)

    first_pair = where_ref[0] + step * block

    def one(q, carry):
        x = jnp.concatenate(
            [xs[k, pl.ds(q, rows, stride=block), :] for k in range(tiles)], axis=1
        )
        edge = truncation - first_pair - q
        group = PACKED if rows % PACKED == 0 else SUB
        column = lax.broadcasted_iota(jnp.int32, (group, padded), 1)
        leading = column < edge
        odd = (jnp.where(leading, column, column - edge) & 1) == 1
        sign = jnp.where(odd, -1.0, 1.0)
        kind = jnp.bfloat16 if group == PACKED else jnp.float32
        factors = [
            jnp.where(leading, 1.0, 0.0),
            jnp.where(leading, 0.0, 1.0),
            jnp.where(leading, sign, 0.0),
            jnp.where(leading, 0.0, sign),
        ]
        x = x.astype(kind)
        lhs = []
        for factor in factors:
            factor = factor.astype(kind)
            for at in range(0, rows, group):
                lhs.append(x[at : at + group] * factor)
        lhs = jnp.concatenate(lhs, axis=0).astype(jnp.bfloat16)
        rhs = wide[pl.ds(q, padded, stride=block), :].astype(jnp.bfloat16)
        if keep:
            keep_ref[q] = rhs
        got = jnp.dot(lhs, rhs, preferred_element_type=jnp.float32)
        res[pl.ds(step * block + q, 4 * rows, stride=pairs), :] = got
        return carry

    lax.fori_loop(0, block, one, 0, unroll=UNROLL_FORWARD)

    @pl.when(step == pl.num_programs(0) - 1)
    def _():
        for n, slot in enumerate(made):
            place = where_ref[1 + count + slot]
            t, s = lax.div(place, 2) - t0, lax.rem(place, 2)
            base = pl.multiple_of((s * (2 * rows) + t * comps) * pairs, SUB)
            for f in range(comps // 2):
                parts = []
                for r in range(2):
                    for h in range(2):
                        parts.append(res[pl.ds(base + (h * rows + 2 * f + r) * pairs, pairs), :])
                out_refs[n][f] = jnp.concatenate(parts, axis=0).astype(jnp.bfloat16)


def grid_kernel(order_ref, cor_ref, weight_ref, syn_ref, ana_ref, *refs, scale):
    sources = order_ref.shape[0]
    in_refs, out_refs, (modes, force) = refs[:sources], refs[sources:-2], refs[-2:]
    fields, rows, lanes = in_refs[0].shape
    longitudes = syn_ref.shape[0]
    for n in range(sources):
        at = pl.multiple_of(order_ref[n] * rows, 16)
        for f in range(fields):
            modes[pl.ds(at, rows), f * lanes : (f + 1) * lanes] = in_refs[n][f]
    cor = cor_ref[...]
    weight = weight_ref[...]
    span = 128

    def synth(b, carry):
        at = pl.multiple_of(b * span, span)
        g = (
            jnp.dot(syn_ref[pl.ds(at, span), :], modes[...], preferred_element_type=jnp.float32)
            * scale
        )
        field = [g[:, f * lanes : (f + 1) * lanes] for f in range(fields)]
        mean = 0.5 * (field[4] + field[5])
        out = [None] * fields
        for a in range(2):
            spin = field[a] + cor
            div = field[2 + a]
            out[a] = -spin * div
            out[2 + a] = spin * field[a] - 0.5 * div * div
            out[4 + a] = -(field[4 + a] + mean) * div
        for f in range(fields):
            force[pl.ds(at, span), f * lanes : (f + 1) * lanes] = out[f].astype(jnp.bfloat16)
        return carry

    lax.fori_loop(0, longitudes // span, synth, 0)

    def analyse(d, carry):
        at = pl.multiple_of(d * rows, 16)
        w = jnp.dot(ana_ref[pl.ds(at, rows), :], force[...], preferred_element_type=jnp.float32)
        for f in range(fields):
            lane = slice(f * lanes, (f + 1) * lanes)
            modes[pl.ds(at, rows), lane] = (w[:, lane] * weight).astype(jnp.bfloat16)
        return carry

    lax.fori_loop(0, sources, analyse, 0)
    for n in range(sources):
        at = pl.multiple_of(order_ref[n] * rows, 16)
        for f in range(fields):
            out_refs[n][f] = modes[pl.ds(at, rows), f * lanes : (f + 1) * lanes]


def step_terms(degree, gm, hm, truncation):
    eig = wave_scale * (degree * (degree + 1)).astype(jnp.float32) / float(truncation * truncation)
    damping = 1.0 / (1.0 + diffusion * eig * eig)
    coupling = time_step * time_step * eig
    pm = [[gm[a][0] * hm[0][b] + gm[a][1] * hm[1][b] for b in range(2)] for a in range(2)]
    diag = [1.0 + coupling * pm[a][a] for a in range(2)]
    cross = [coupling * pm[0][1], coupling * pm[1][0]]
    inverse = 1.0 / (diag[0] * diag[1] - cross[0] * cross[1])
    solve = [
        [diag[1] * inverse, -cross[0] * inverse],
        [-cross[1] * inverse, diag[0] * inverse],
    ]
    push = [[time_step * eig * gm[a][b] for b in range(2)] for a in range(2)]
    return damping, solve, push


def semi_implicit_slabs(old, tend, terms, hm):
    damping, solve, push = terms
    out = [None] * 12
    for r in range(2):
        star = [old[c * 2 + r] + time_step * tend[c * 2 + r] for c in range(6)]
        right = [star[2 + a] + push[a][0] * star[4] + push[a][1] * star[5] for a in range(2)]
        div = [solve[a][0] * right[0] + solve[a][1] * right[1] for a in range(2)]
        for a in range(2):
            heat = (time_step * hm[a][0]) * div[0] + (time_step * hm[a][1]) * div[1]
            out[a * 2 + r] = damping * star[a]
            out[(2 + a) * 2 + r] = damping * div[a]
            out[(4 + a) * 2 + r] = damping * (star[4 + a] - heat)
    return out


def inverse_kernel(
    where_ref, gravity_ref, stability_ref, *refs, truncation, pairs, chunks, last, stored, slots, count
):
    w_refs, refs = refs[: chunks * slots], refs[chunks * slots :]
    leg_refs, refs = refs[:chunks], refs[chunks:]
    spec_ref, refs = refs[0], refs[1:]
    patches = count if stored else 0
    fresh_refs, refs = refs[:patches], refs[patches:]
    out_ref, ws, ten = refs[:3]
    if stored:
        wide = refs[3]
    step = pl.program_id(0)
    row_length = truncation + 1
    trajectories, comps, block, _ = out_ref.shape
    rows = trajectories * comps
    tiles = ten.shape[0]
    padded = tiles * LANES

    @pl.when(step == 0)
    def _():
        if stored:
            for k in range(chunks):
                wide[k, row_length * block :, :] = jnp.zeros(
                    (wide.shape[1] - row_length * block, LANES), jnp.float32
                )
        for k in range(chunks):
            for n in range(slots):
                place = where_ref[1 + count + n]
                t, s = lax.div(place, 2), lax.rem(place, 2)
                base = pl.multiple_of((s * (2 * rows) + t * comps) * pairs, SUB)
                for f in range(comps // 2):
                    got = w_refs[k * slots + n][f].astype(jnp.float32)
                    for r in range(2):
                        for h in range(2):
                            at = (r * 2 + h) * pairs
                            ws[k, pl.ds(base + (h * rows + 2 * f + r) * pairs, pairs), :] = got[
                                at : at + pairs, :
                            ]

    if stored:
        for k in range(chunks):
            wide[k, : row_length * block, :] = (
                leg_refs[k][...].astype(jnp.float32).reshape(row_length * block, LANES)
            )
    first_pair = where_ref[0] + step * block

    def one(q, carry):
        at = pl.ds(step * block + q, 4 * rows, stride=pairs)
        lhs = jnp.concatenate([ws[k, at, :].astype(jnp.bfloat16) for k in range(chunks)], axis=1)
        if not stored:
            rhs = jnp.concatenate([leg_refs[k][q] for k in range(chunks)], axis=1)
        else:
            at = pl.ds(q, padded, stride=block)
            rhs = jnp.concatenate(
                [wide[k, at, :].astype(jnp.bfloat16) for k in range(chunks)], axis=1
            )
        got = lax.dot_general(
            lhs, rhs, (((1,), (1,)), ((), ())), preferred_element_type=jnp.float32
        )
        leading, odd, _ = layout_terms(first_pair + q, 1, 0, padded, truncation)
        north = jnp.where(leading, got[:rows], got[rows : 2 * rows])
        south = jnp.where(leading, got[2 * rows : 3 * rows], got[3 * rows :])
        total = north + jnp.where(odd, -south, south)
        for k in range(tiles):
            ten[k, pl.ds(q, rows, stride=block), :] = total[:, k * LANES : (k + 1) * LANES]
        return carry

    lax.fori_loop(0, block, one, 0, unroll=UNROLL_INVERSE)

    if last:
        gm = [[gravity_ref[a, b] for b in range(2)] for a in range(2)]
        hm = [[stability_ref[a, b] for b in range(2)] for a in range(2)]
    for k in range(tiles):
        width = min(LANES, row_length - k * LANES)
        lanes = slice(k * LANES, k * LANES + width)
        if last:
            _, _, degree = layout_terms(first_pair, block, k * LANES, width, truncation)
            terms = step_terms(degree, gm, hm, truncation)

        def body(t, carry):
            tend = []
            for c in range(comps):
                at = pl.multiple_of((t * comps + c) * block, SUB)
                value = ten[k, pl.ds(at, block), :][:, :width]
                tend.append(value)
            old = [spec_ref[t, c, :, lanes] for c in range(comps)]
            if last:
                tend = semi_implicit_slabs(old, tend, terms, hm)
            else:
                for i in range(patches):
                    mine = where_ref[1 + i] == t
                    old = [jnp.where(mine, fresh_refs[i][c, :, lanes], old[c]) for c in range(comps)]
                tend = [old[c] + time_step * tend[c] for c in range(comps)]
            for c in range(comps):
                out_ref[t, c, :, lanes] = tend[c]
            return carry

        lax.fori_loop(0, trajectories, body, 0)


def fourier_tables(pair_count, groups, truncation, longitudes):
    index = jnp.arange(pair_count * 4, dtype=jnp.int32)
    local = pair_count // groups
    group = index // (4 * local)
    part = index // (2 * local) % 2
    half = index // local % 2
    pair = group * local + index % local
    order = jnp.where(half == 0, pair, truncation - 1 - pair)
    quarter = part * (longitudes // 4)
    half_turn = longitudes // 2
    column = jnp.arange(half_turn, dtype=jnp.int32)[None, :]
    phase = (order[:, None] * column + quarter[:, None]) % longitudes
    angle = phase.astype(jnp.float32) * (2.0 * math.pi / longitudes)
    first = jnp.cos(angle)
    second = jnp.where(order[:, None] % 2 == 0, first, -first)
    return jnp.concatenate([first, second], axis=1).astype(jnp.bfloat16)


def pick_kernel(clones_ref, spec_ref, row_ref, where_ref, *route_refs, local, pairs, slots, direct):
    row_ref[...] = spec_ref[...].astype(jnp.bfloat16)
    members, member = lax.axis_size("member"), lax.axis_index("member")
    position = lax.axis_index("space")
    count = len(route_refs)
    where_ref[0] = position * pairs
    for i in range(count):
        source = lax.div(clones_ref[i, 1], local)
        target = lax.div(clones_ref[i, 0], local)
        route_refs[i][0] = source * members + target
        where_ref[1 + i] = jnp.where(target == member, clones_ref[i, 0] - target * local, -1)
    for n in range(slots):
        where_ref[1 + count + n] = jnp.bitwise_xor(position, n) if direct else n


def pick_clones(spectra, clones, slots, direct):
    local, comps, pairs, row_length = spectra.shape
    count = clones.shape[0]
    smem = pl.BlockSpec(memory_space=pltpu.SMEM)
    block = (1, comps, pairs, row_length)
    got = pl.pallas_call(
        functools.partial(pick_kernel, local=local, pairs=pairs, slots=slots, direct=direct),
        out_shape=[
            jax.ShapeDtypeStruct((count,) + block[1:], jnp.bfloat16),
            jax.ShapeDtypeStruct((1 + count + slots,), jnp.int32),
        ]
        + [jax.ShapeDtypeStruct((1,), jnp.int32)] * count,
        grid_spec=pltpu.PrefetchScalarGridSpec(
            num_scalar_prefetch=1,
            grid=(count,),
            in_specs=[pl.BlockSpec(block, lambda i, c: (lax.rem(c[i, 1], local), 0, 0, 0))],
            out_specs=[pl.BlockSpec(block, lambda i, c: (i, 0, 0, 0))] + [smem] * (1 + count),
        ),
        cost_estimate=pl.CostEstimate(
            flops=0, bytes_accessed=6 * 1024 * 1024, transcendentals=0
        ),
        name="pick",
    )(clones, spectra)
    return got[0], got[1], [r.reshape(()) for r in got[2:]]


def send_clone(row, route):
    members = lax.axis_size("member")

    def move(a, b):
        if a == b:
            return lambda v: v
        return lambda v: lax.ppermute(v, "member", [(a, b)])

    branches = [move(a, b) for a in range(members) for b in range(members)]
    return lax.switch(route, branches, row)


def share_row(row, owner):
    members = lax.axis_size("member")
    differs = jnp.bitwise_xor(owner, lax.axis_index("member").astype(jnp.int32))
    bit = 1
    while bit < members:
        other = lax.ppermute(row, "member", [(m, m ^ bit) for m in range(members)])
        row = jnp.where(jnp.bitwise_and(differs, bit) != 0, other, row)
        bit *= 2
    return row


def shards(spectra, legendre, sin_lat, gravity, stability, clones):
    trajectories, comps, pairs, row_length = spectra.shape
    truncation = row_length - 1
    half_lat = legendre.shape[2]
    longitudes = LONGITUDES_PER_WAVE * truncation
    space = lax.axis_size("space")
    position = lax.axis_index("space")
    fields = comps // 2
    split = space // (2 * trajectories)
    lane_count = LANES // split
    chunk_count = half_lat // LANES
    padded_pairs = -(-pairs // SUB) * SUB
    steps = padded_pairs // SUB
    tiles = -(-row_length // LANES)
    extra = padded_pairs - pairs
    rows = trajectories * comps

    count = clones.shape[0]
    slots = 2 * trajectories
    direct = split == 1
    picked, where, route = pick_clones(spectra, clones, slots, direct)
    fresh_narrow = [send_clone(picked[i], route[i]) for i in range(count)]
    state = spectra
    if extra:
        state = jnp.pad(state, ((0, 0), (0, 0), (0, extra), (0, 0)))
        fresh_narrow = [jnp.pad(x, ((0, 0), (0, extra), (0, 0))) for x in fresh_narrow]
    order = jnp.arange(space, dtype=jnp.int32)
    if direct:
        order = jnp.bitwise_xor(position.astype(jnp.int32), order)
    columns = jnp.transpose(legendre, (1, 0, 2))
    if extra:
        columns = jnp.pad(columns, ((0, 0), (0, extra), (0, 0)))

    smem = pl.BlockSpec(memory_space=pltpu.SMEM)
    state_spec = pl.BlockSpec((trajectories, comps, SUB, row_length), lambda i: (0, 0, i, 0))
    fresh_spec = pl.BlockSpec((comps, SUB, row_length), lambda i: (0, i, 0))
    kept_spec = pl.BlockSpec((SUB, tiles * LANES, LANES), lambda i: (i, 0, 0))
    part_shape = (fields, 4 * padded_pairs, LANES)
    part_spec = pl.BlockSpec(part_shape, lambda i: (0, 0, 0))

    def leg_spec(k):
        return pl.BlockSpec((row_length, SUB, LANES), lambda i: (0, i, k))

    mib = 1024 * 1024

    def forward(k, where, made, span):
        keep = k > 0
        kept_shape = jax.ShapeDtypeStruct((padded_pairs, tiles * LANES, LANES), jnp.bfloat16)
        return pl.pallas_call(
            functools.partial(
                forward_kernel, truncation=truncation, pairs=padded_pairs, keep=keep, count=count, made=made, span=span
            ),
            out_shape=[jax.ShapeDtypeStruct(part_shape, jnp.bfloat16)] * len(made)
            + [kept_shape] * keep,
            grid=(steps,),
            in_specs=[smem, state_spec, leg_spec(k)] + [fresh_spec] * count,
            out_specs=[part_spec] * len(made) + [kept_spec] * keep,
            scratch_shapes=[
                pltpu.VMEM((tiles * LANES * SUB, LANES), jnp.float32),
                pltpu.VMEM((tiles, span * comps * SUB, LANES), jnp.float32),
                pltpu.VMEM((4 * span * comps * padded_pairs, LANES), jnp.float32),
            ],
            compiler_params=pltpu.CompilerParams(vmem_limit_bytes=60 * mib),
            cost_estimate=pl.CostEstimate(
                flops=8 * span * comps * padded_pairs * row_length * LANES,
                bytes_accessed=16 * 1024 * 1024,
                transcendentals=0,
            ),
            name="forward",
        )(where, state, columns, *fresh_narrow)

    def to_wire(x):
        if extra:
            x = x.reshape(slots, fields, 4, padded_pairs, LANES)[:, :, :, :pairs]
        x = x.reshape(slots, fields, 4 * pairs, split, lane_count)
        return jnp.transpose(x, (0, 3, 1, 2, 4)).reshape(space, fields, 4 * pairs, lane_count)

    def from_wire(x):
        x = x.reshape(slots, split, fields, 4, pairs, lane_count)
        x = jnp.transpose(x, (0, 2, 3, 4, 1, 5)).reshape(slots, fields, 4, pairs, LANES)
        if extra:
            x = jnp.pad(x, ((0, 0), (0, 0), (0, 0), (0, extra), (0, 0)))
        return x.reshape((slots,) + part_shape)

    def exchange(x):
        return lax.all_to_all(x, "space", split_axis=0, concat_axis=0, tiled=True)

    def swap(parts):
        got = list(parts)
        for n in reversed(range(1, space)):
            got[n] = lax.ppermute(parts[n], "space", [(d, d ^ n) for d in range(space)])
        return got

    def spread(parts):
        if direct:
            return swap(parts)
        x = exchange(to_wire(jnp.stack(parts)))
        x = jnp.pad(x, ((0, 0), (0, 0), (0, 0), (0, LANES - lane_count)))
        return [x[d] for d in range(space)]

    def collect(parts):
        if direct:
            return swap(parts)
        x = from_wire(exchange(jnp.stack(parts)[..., :lane_count]))
        return [x[n] for n in range(slots)]

    analysis = lax.optimization_barrier(
        fourier_tables(pairs * space, space, truncation, longitudes)
    )
    synthesis = analysis.T
    south = position // split % 2
    hemisphere = jnp.where(south == 0, sin_lat, -sin_lat)
    weights_all = math.pi * jnp.sqrt(1.0 - hemisphere * hemisphere) / (2 * half_lat)
    vmem = pl.BlockSpec(memory_space=pltpu.VMEM)
    modes = 4 * pairs * space

    def grid(k, parts):
        first = k * LANES + position % split * lane_count
        mu = lax.dynamic_slice_in_dim(hemisphere, first, lane_count)
        weight = lax.dynamic_slice_in_dim(weights_all, first, lane_count)
        short = LANES - lane_count
        if short:
            mu = jnp.pad(mu, (0, short))
            weight = jnp.pad(weight, (0, short))
        return pl.pallas_call(
            functools.partial(grid_kernel, scale=1.0 / truncation),
            out_shape=[jax.ShapeDtypeStruct(x.shape, jnp.bfloat16) for x in parts],
            in_specs=[smem] + [vmem] * (4 + space),
            out_specs=[vmem] * space,
            scratch_shapes=[
                pltpu.VMEM((modes, fields * LANES), jnp.bfloat16),
                pltpu.VMEM((longitudes, fields * LANES), jnp.bfloat16),
            ],
            compiler_params=pltpu.CompilerParams(vmem_limit_bytes=60 * mib),
            cost_estimate=pl.CostEstimate(
                flops=4 * modes * longitudes * fields * LANES,
                bytes_accessed=12 * 1024 * 1024,
                transcendentals=0,
            ),
            name="grid",
        )(order, (2.0 * mu)[None], weight[None], synthesis, analysis, *parts)

    def inverse(ws, legs, start, patches, last):
        chunks = len(ws)
        stored = bool(patches)
        wide_scratch = pltpu.VMEM((chunks, tiles * LANES * SUB, LANES), jnp.float32)
        return pl.pallas_call(
            functools.partial(
                inverse_kernel,
                truncation=truncation,
                pairs=padded_pairs,
                chunks=chunks,
                last=last,
                stored=stored,
                slots=slots,
                count=count,
            ),
            out_shape=jax.ShapeDtypeStruct(state.shape, jnp.float32),
            grid=(steps,),
            in_specs=[smem] * 3
            + [part_spec] * (chunks * slots)
            + ([leg_spec(k) for k in range(chunks)] if stored else [kept_spec] * chunks)
            + [state_spec]
            + [fresh_spec] * len(patches),
            out_specs=state_spec,
            scratch_shapes=[
                pltpu.VMEM((chunks, 4 * rows * padded_pairs, LANES), jnp.float32),
                pltpu.VMEM((tiles, rows * SUB, LANES), jnp.float32),
            ]
            + ([wide_scratch] if stored else []),
            compiler_params=pltpu.CompilerParams(vmem_limit_bytes=60 * mib),
            cost_estimate=pl.CostEstimate(
                flops=8 * rows * padded_pairs * row_length * LANES * chunks,
                bytes_accessed=20 * 1024 * 1024,
                transcendentals=0,
            ),
            name="inverse",
        )(where, gravity, stability, *[x for w in ws for x in w], *legs, start, *patches)

    made, turn = [], where
    everything = tuple(range(slots))
    halved = direct and trajectories % 2 == 0
    for k in range(chunk_count):
        if k == 0 and halved:
            near = everything[: slots // 2]
            far = everything[slots // 2 :]
            first = list(forward(k, turn, far, trajectories // 2))
            turn, first[0] = lax.optimization_barrier((where, first[0]))
            second = list(forward(k, turn, near, trajectories // 2))
            made.append(second + first)
        else:
            made.append(list(forward(k, turn, everything, trajectories)))
        turn, made[-1][0] = lax.optimization_barrier((where, made[-1][0]))
    kept = [x[-1] for x in made[1:]]
    sent = []
    for x in made:
        sent.append(spread(x[:slots]))
    later, _ = lax.optimization_barrier((clones[:, 1], made[1][0]))
    fresh = [
        share_row(
            lax.dynamic_index_in_dim(spectra, lax.rem(later[i], trajectories), 0, keepdims=False),
            lax.div(later[i], trajectories),
        )
        for i in range(count)
    ]
    if extra:
        fresh = [jnp.pad(x, ((0, 0), (0, extra), (0, 0))) for x in fresh]
    back = []
    for k in range(chunk_count):
        got = grid(k, sent[k])
        back.append(collect(got))
    start = inverse(back[:1], [columns], state, fresh, False)
    for k in range(1, chunk_count - 1):
        start = inverse(back[k : k + 1], kept[k - 1 : k], start, [], False)
    out = inverse(back[-1:], kept[-1:], start, [], True)
    return out[:, :, :pairs] if extra else out


def solution(mesh):
    placed = (P("member", None, "space", None), P("space", None, None), P(), P(), P(), P())
    return jax.shard_map(
        shards,
        mesh=mesh,
        in_specs=placed,
        out_specs=P("member", None, "space", None),
        check_vma=False,
    )
```

```python
import functools
import math

import jax
import jax.numpy as jnp
from jax import lax
from jax.experimental import pallas as pl
from jax.experimental.pallas import tpu as pltpu
from jax.sharding import PartitionSpec as P


LANES = 128
SUB = 8
PACKED = 16
UNROLL_FORWARD = 8
UNROLL_INVERSE = 8
LONGITUDES_PER_WAVE = 2

time_step = 0.25
wave_scale = 16.0
diffusion = 0.02


def layout_terms(first_pair, count, lane0, lanes, truncation):
    pair = first_pair + lax.broadcasted_iota(jnp.int32, (count, lanes), 0)
    column = lane0 + lax.broadcasted_iota(jnp.int32, (count, lanes), 1)
    leading = column < truncation - pair
    offset = jnp.where(leading, column, column - (truncation - pair))
    order = jnp.where(leading, pair, truncation - 1 - pair)
    return leading, (offset & 1) == 1, order + offset


def slot_place(n, direct):
    return jnp.bitwise_xor(lax.axis_index("space"), n) if direct else jnp.int32(n)


def forward_kernel(
    *refs, truncation, pairs, real_pairs, keep, count, made, span, direct
):
    if count:
        slot_ref, refs = refs[0], refs[1:]
    spec_ref, leg_ref, refs = refs[0], refs[1], refs[2:]
    step = pl.program_id(0)
    row_length = truncation + 1
    _, comps, block, _ = spec_ref.shape
    rows = span * comps
    fresh_refs, refs = refs[:count], refs[count:]
    out_refs, refs = refs[: len(made)], refs[len(made) :]
    if keep:
        keep_ref, refs = refs[0], refs[1:]
    wide, xs, res = refs
    tiles = xs.shape[0]
    padded = tiles * LANES
    first_place = lax.div(slot_place(made[0], direct), 2)
    t0 = lax.div(first_place, span) * span

    @pl.when(step == 0)
    def _():
        wide[row_length * block :, :] = jnp.zeros(
            (wide.shape[0] - row_length * block, LANES), jnp.float32
        )

    wide[: row_length * block, :] = (
        leg_ref[...].astype(jnp.float32).reshape(row_length * block, LANES)
    )
    for k in range(tiles):
        width = min(LANES, row_length - k * LANES)
        lanes = slice(k * LANES, k * LANES + width)
        if width < LANES:
            xs[k] = jnp.zeros((rows * block, LANES), jnp.float32)
        xs[k, :, :width] = spec_ref[pl.ds(t0, span), :, :, lanes].reshape(rows * block, width)

    for i in range(count):
        slot = slot_ref[i] - t0

        @pl.when(jnp.logical_and(slot >= 0, slot < span))
        def _():
            at = pl.multiple_of(slot * comps * block, SUB)
            for k in range(tiles):
                width = min(LANES, row_length - k * LANES)
                fresh = fresh_refs[i][:, :, k * LANES : k * LANES + width].astype(jnp.float32)
                xs[k, pl.ds(at, comps * block), :width] = fresh.reshape(comps * block, width)

    first_pair = lax.axis_index("space") * real_pairs + step * block

    def one(q, carry):
        x = jnp.concatenate(
            [xs[k, pl.ds(q, rows, stride=block), :] for k in range(tiles)], axis=1
        )
        edge = truncation - first_pair - q
        group = PACKED if rows % PACKED == 0 else SUB
        column = lax.broadcasted_iota(jnp.int32, (group, padded), 1)
        leading = column < edge
        odd = (jnp.where(leading, column, column - edge) & 1) == 1
        sign = jnp.where(odd, -1.0, 1.0)
        kind = jnp.bfloat16 if group == PACKED else jnp.float32
        factors = [
            jnp.where(leading, 1.0, 0.0),
            jnp.where(leading, 0.0, 1.0),
            jnp.where(leading, sign, 0.0),
            jnp.where(leading, 0.0, sign),
        ]
        x = x.astype(kind)
        lhs = []
        for factor in factors:
            factor = factor.astype(kind)
            for at in range(0, rows, group):
                lhs.append(x[at : at + group] * factor)
        lhs = jnp.concatenate(lhs, axis=0).astype(jnp.bfloat16)
        rhs = wide[pl.ds(q, padded, stride=block), :].astype(jnp.bfloat16)
        if keep:
            keep_ref[q] = rhs
        got = jnp.dot(lhs, rhs, preferred_element_type=jnp.float32)
        res[pl.ds(step * block + q, 4 * rows, stride=pairs), :] = got
        return carry

    lax.fori_loop(0, block, one, 0, unroll=UNROLL_FORWARD)

    @pl.when(step == pl.num_programs(0) - 1)
    def _():
        for n, slot in enumerate(made):
            place = slot_place(slot, direct)
            t, s = lax.div(place, 2) - t0, lax.rem(place, 2)
            base = pl.multiple_of((s * (2 * rows) + t * comps) * pairs, SUB)
            for f in range(comps // 2):
                parts = []
                for r in range(2):
                    for h in range(2):
                        parts.append(res[pl.ds(base + (h * rows + 2 * f + r) * pairs, pairs), :])
                out_refs[n][f] = jnp.concatenate(parts, axis=0).astype(jnp.bfloat16)


def grid_kernel(order_ref, cor_ref, weight_ref, syn_ref, ana_ref, *refs, scale):
    sources = order_ref.shape[0]
    in_refs, out_refs, (modes, force) = refs[:sources], refs[sources:-2], refs[-2:]
    fields, rows, lanes = in_refs[0].shape
    longitudes = syn_ref.shape[0]
    for n in range(sources):
        at = pl.multiple_of(order_ref[n] * rows, 16)
        for f in range(fields):
            modes[pl.ds(at, rows), f * lanes : (f + 1) * lanes] = in_refs[n][f]
    cor = cor_ref[...]
    weight = weight_ref[...]
    span = 128

    def synth(b, carry):
        at = pl.multiple_of(b * span, span)
        g = (
            jnp.dot(syn_ref[pl.ds(at, span), :], modes[...], preferred_element_type=jnp.float32)
            * scale
        )
        field = [g[:, f * lanes : (f + 1) * lanes] for f in range(fields)]
        mean = 0.5 * (field[4] + field[5])
        out = [None] * fields
        for a in range(2):
            spin = field[a] + cor
            div = field[2 + a]
            out[a] = -spin * div
            out[2 + a] = spin * field[a] - 0.5 * div * div
            out[4 + a] = -(field[4 + a] + mean) * div
        for f in range(fields):
            force[pl.ds(at, span), f * lanes : (f + 1) * lanes] = out[f].astype(jnp.bfloat16)
        return carry

    lax.fori_loop(0, longitudes // span, synth, 0)

    def analyse(d, carry):
        at = pl.multiple_of(d * rows, 16)
        w = jnp.dot(ana_ref[pl.ds(at, rows), :], force[...], preferred_element_type=jnp.float32)
        for f in range(fields):
            lane = slice(f * lanes, (f + 1) * lanes)
            modes[pl.ds(at, rows), lane] = (w[:, lane] * weight).astype(jnp.bfloat16)
        return carry

    lax.fori_loop(0, sources, analyse, 0)
    for n in range(sources):
        at = pl.multiple_of(order_ref[n] * rows, 16)
        for f in range(fields):
            out_refs[n][f] = modes[pl.ds(at, rows), f * lanes : (f + 1) * lanes]


def step_terms(degree, gm, hm, truncation):
    eig = wave_scale * (degree * (degree + 1)).astype(jnp.float32) / float(truncation * truncation)
    damping = 1.0 / (1.0 + diffusion * eig * eig)
    coupling = time_step * time_step * eig
    pm = [[gm[a][0] * hm[0][b] + gm[a][1] * hm[1][b] for b in range(2)] for a in range(2)]
    diag = [1.0 + coupling * pm[a][a] for a in range(2)]
    cross = [coupling * pm[0][1], coupling * pm[1][0]]
    inverse = 1.0 / (diag[0] * diag[1] - cross[0] * cross[1])
    solve = [
        [diag[1] * inverse, -cross[0] * inverse],
        [-cross[1] * inverse, diag[0] * inverse],
    ]
    push = [[time_step * eig * gm[a][b] for b in range(2)] for a in range(2)]
    return damping, solve, push


def semi_implicit_slabs(old, tend, terms, hm):
    damping, solve, push = terms
    out = [None] * 12
    for r in range(2):
        star = [old[c * 2 + r] + time_step * tend[c * 2 + r] for c in range(6)]
        right = [star[2 + a] + push[a][0] * star[4] + push[a][1] * star[5] for a in range(2)]
        div = [solve[a][0] * right[0] + solve[a][1] * right[1] for a in range(2)]
        for a in range(2):
            heat = (time_step * hm[a][0]) * div[0] + (time_step * hm[a][1]) * div[1]
            out[a * 2 + r] = damping * star[a]
            out[(2 + a) * 2 + r] = damping * div[a]
            out[(4 + a) * 2 + r] = damping * (star[4 + a] - heat)
    return out


def inverse_kernel(
    slot_ref,
    gravity_ref,
    stability_ref,
    *refs,
    truncation,
    pairs,
    real_pairs,
    chunks,
    last,
    stored,
    slots,
    count,
    direct,
):
    w_refs, refs = refs[: chunks * slots], refs[chunks * slots :]
    leg_refs, refs = refs[:chunks], refs[chunks:]
    spec_ref, refs = refs[0], refs[1:]
    patches = count if stored else 0
    fresh_refs, refs = refs[:patches], refs[patches:]
    mend_refs, refs = refs[:patches], refs[patches:]
    out_ref, ws, ten = refs[:3]
    if stored:
        wide = refs[3]
    step = pl.program_id(0)
    row_length = truncation + 1
    trajectories, comps, block, _ = out_ref.shape
    rows = trajectories * comps
    tiles = ten.shape[0]
    padded = tiles * LANES

    @pl.when(step == 0)
    def _():
        if stored:
            for k in range(chunks):
                wide[k, row_length * block :, :] = jnp.zeros(
                    (wide.shape[1] - row_length * block, LANES), jnp.float32
                )

        def fill(k, t, s, source):
            base = pl.multiple_of((s * (2 * rows) + t * comps) * pairs, SUB)
            for f in range(comps // 2):
                got = source(f).astype(jnp.float32)
                for r in range(2):
                    for h in range(2):
                        at = (r * 2 + h) * pairs
                        ws[k, pl.ds(base + (h * rows + 2 * f + r) * pairs, pairs), :] = got[
                            at : at + pairs, :
                        ]

        for k in range(chunks):
            for n in range(slots):
                place = slot_place(n, direct)
                fill(k, lax.div(place, 2), lax.rem(place, 2), lambda f: w_refs[k * slots + n][f])
        for i in range(patches):

            @pl.when(slot_ref[i] >= 0)
            def _():
                for s in range(2):
                    fill(0, slot_ref[i], s, lambda f: mend_refs[i][s, f])

    if stored:
        for k in range(chunks):
            wide[k, : row_length * block, :] = (
                leg_refs[k][...].astype(jnp.float32).reshape(row_length * block, LANES)
            )
    first_pair = lax.axis_index("space") * real_pairs + step * block

    def one(q, carry):
        at = pl.ds(step * block + q, 4 * rows, stride=pairs)
        lhs = jnp.concatenate([ws[k, at, :].astype(jnp.bfloat16) for k in range(chunks)], axis=1)
        if not stored:
            rhs = jnp.concatenate([leg_refs[k][q] for k in range(chunks)], axis=1)
        else:
            at = pl.ds(q, padded, stride=block)
            rhs = jnp.concatenate(
                [wide[k, at, :].astype(jnp.bfloat16) for k in range(chunks)], axis=1
            )
        got = lax.dot_general(
            lhs, rhs, (((1,), (1,)), ((), ())), preferred_element_type=jnp.float32
        )
        leading, odd, _ = layout_terms(first_pair + q, 1, 0, padded, truncation)
        north = jnp.where(leading, got[:rows], got[rows : 2 * rows])
        south = jnp.where(leading, got[2 * rows : 3 * rows], got[3 * rows :])
        total = north + jnp.where(odd, -south, south)
        for k in range(tiles):
            ten[k, pl.ds(q, rows, stride=block), :] = total[:, k * LANES : (k + 1) * LANES]
        return carry

    lax.fori_loop(0, block, one, 0, unroll=UNROLL_INVERSE)

    if last:
        gm = [[gravity_ref[a, b] for b in range(2)] for a in range(2)]
        hm = [[stability_ref[a, b] for b in range(2)] for a in range(2)]
    for k in range(tiles):
        width = min(LANES, row_length - k * LANES)
        lanes = slice(k * LANES, k * LANES + width)
        if last:
            _, _, degree = layout_terms(first_pair, block, k * LANES, width, truncation)
            terms = step_terms(degree, gm, hm, truncation)

        def body(t, carry):
            tend = []
            for c in range(comps):
                at = pl.multiple_of((t * comps + c) * block, SUB)
                value = ten[k, pl.ds(at, block), :][:, :width]
                tend.append(value)
            old = [spec_ref[t, c, :, lanes] for c in range(comps)]
            if last:
                tend = semi_implicit_slabs(old, tend, terms, hm)
            else:
                for i in range(patches):
                    mine = slot_ref[i] == t
                    old = [jnp.where(mine, fresh_refs[i][c, :, lanes], old[c]) for c in range(comps)]
                tend = [old[c] + time_step * tend[c] for c in range(comps)]
            for c in range(comps):
                out_ref[t, c, :, lanes] = tend[c]
            return carry

        lax.fori_loop(0, trajectories, body, 0)


def fourier_tables(pair_count, groups, truncation, longitudes):
    half_turn = longitudes // 2
    order = jnp.arange(pair_count + 1, dtype=jnp.int32)[None, :, None]
    column = jnp.arange(half_turn, dtype=jnp.int32)[None, None, :]
    quarter = jnp.arange(2, dtype=jnp.int32)[:, None, None] * (longitudes // 4)
    phase = (order * column + quarter) % longitudes
    angle = phase.astype(jnp.float32) * (2.0 * math.pi / longitudes)
    base = lax.optimization_barrier(jnp.cos(angle).astype(jnp.bfloat16))
    low = base[:, :pair_count]
    flip = (1 - 2 * (column % 2)) * (1 - 2 * jnp.arange(2, dtype=jnp.int32)[:, None, None])
    high = base[:, 1:] * flip.astype(jnp.bfloat16)
    pair = jnp.arange(pair_count, dtype=jnp.int32)[None, :, None]
    low_sign = (1 - 2 * (pair % 2)).astype(jnp.bfloat16)
    high_sign = (1 - 2 * ((truncation - 1 - pair) % 2)).astype(jnp.bfloat16)
    low = jnp.concatenate([low, low * low_sign], axis=2)
    high = jnp.concatenate([high, high * high_sign], axis=2)
    table = jnp.stack([low, high], axis=1)
    table = table.reshape(2, 2, groups, pair_count // groups, longitudes)
    return jnp.transpose(table, (2, 0, 1, 3, 4)).reshape(4 * pair_count, longitudes)


def far_members(members):
    return [(a, b) for a in range(members) for b in range(a + 1, members) if a ^ b != 1]


def pick_kernel(clones_ref, spec_ref, row_ref, slot_ref, *route_refs, local):
    row_ref[...] = spec_ref[...].astype(jnp.bfloat16)
    members, member = lax.axis_size("member"), lax.axis_index("member")
    for i, route_ref in enumerate(route_refs):
        source = lax.div(clones_ref[i, 1], local)
        target = lax.div(clones_ref[i, 0], local)
        route = jnp.where(source == target, 0, 1)
        low, high = jnp.minimum(source, target), jnp.maximum(source, target)
        for k, (a, b) in enumerate(far_members(members)):
            route = jnp.where(jnp.logical_and(low == a, high == b), 2 + k, route)
        route_ref[0] = route
        slot_ref[i] = jnp.where(target == member, clones_ref[i, 0] - target * local, -1)


def pick_clones(spectra, clones):
    local, comps, pairs, row_length = spectra.shape
    count = clones.shape[0]
    smem = pl.BlockSpec(memory_space=pltpu.SMEM)
    block = (1, comps, pairs, row_length)
    got = pl.pallas_call(
        functools.partial(pick_kernel, local=local),
        out_shape=[
            jax.ShapeDtypeStruct((count,) + block[1:], jnp.bfloat16),
            jax.ShapeDtypeStruct((count,), jnp.int32),
        ]
        + [jax.ShapeDtypeStruct((1,), jnp.int32)] * count,
        grid_spec=pltpu.PrefetchScalarGridSpec(
            num_scalar_prefetch=1,
            grid=(count,),
            in_specs=[pl.BlockSpec(block, lambda i, c: (lax.rem(c[i, 1], local), 0, 0, 0))],
            out_specs=[pl.BlockSpec(block, lambda i, c: (i, 0, 0, 0))] + [smem] * (1 + count),
        ),
        cost_estimate=pl.CostEstimate(
            flops=0, bytes_accessed=6 * 1024 * 1024, transcendentals=0
        ),
        name="pick",
    )(clones, spectra)
    return got[0], got[1], [r.reshape(()) for r in got[2:]]


def choose_kernel(clones_ref, *refs, local, slots, direct):
    in_refs, out_refs = refs[:slots], refs[slots:]
    for i, out_ref in enumerate(out_refs):
        t = lax.rem(clones_ref[i, 1], local)
        for n in range(slots):
            place = slot_place(n, direct)

            @pl.when(lax.div(place, 2) == t)
            def _():
                out_ref[lax.rem(place, 2)] = in_refs[n][...]


def choose_rows(parts, clones, local, direct):
    vmem = pl.BlockSpec(memory_space=pltpu.VMEM)
    return pl.pallas_call(
        functools.partial(choose_kernel, local=local, slots=len(parts), direct=direct),
        out_shape=[jax.ShapeDtypeStruct((2,) + parts[0].shape, parts[0].dtype)] * clones.shape[0],
        in_specs=[pl.BlockSpec(memory_space=pltpu.SMEM)] + [vmem] * len(parts),
        out_specs=[vmem] * clones.shape[0],
        cost_estimate=pl.CostEstimate(
            flops=0, bytes_accessed=4 * 1024 * 1024, transcendentals=0
        ),
        name="choose",
    )(clones, *parts)


def send_clone(row, route):
    members = lax.axis_size("member")

    def swap(pairs):
        both = pairs + [(b, a) for a, b in pairs]
        return lambda v: lax.ppermute(v, "member", both)

    branches = [lambda v: v, swap([(a, a + 1) for a in range(0, members, 2)])]
    branches += [swap([pair]) for pair in far_members(members)]
    return lax.switch(route, branches, row)


def share_row(row, owner):
    members = lax.axis_size("member")
    differs = jnp.bitwise_xor(owner, lax.axis_index("member").astype(jnp.int32))
    bit = 1
    while bit < members:
        other = lax.ppermute(row, "member", [(m, m ^ bit) for m in range(members)])
        row = jnp.where(jnp.bitwise_and(differs, bit) != 0, other, row)
        bit *= 2
    return row


def shards(spectra, legendre, sin_lat, gravity, stability, clones):
    trajectories, comps, pairs, row_length = spectra.shape
    truncation = row_length - 1
    half_lat = legendre.shape[2]
    longitudes = LONGITUDES_PER_WAVE * truncation
    space = lax.axis_size("space")
    position = lax.axis_index("space")
    fields = comps // 2
    split = space // (2 * trajectories)
    lane_count = LANES // split
    chunk_count = half_lat // LANES
    padded_pairs = -(-pairs // SUB) * SUB
    steps = padded_pairs // SUB
    tiles = -(-row_length // LANES)
    extra = padded_pairs - pairs
    rows = trajectories * comps

    count = clones.shape[0]
    slots = 2 * trajectories
    direct = split == 1
    state = spectra
    if extra:
        state = jnp.pad(state, ((0, 0), (0, 0), (0, extra), (0, 0)))
    order = jnp.arange(space, dtype=jnp.int32)
    if direct:
        order = jnp.bitwise_xor(position.astype(jnp.int32), order)
    columns = jnp.transpose(legendre, (1, 0, 2))
    if extra:
        columns = jnp.pad(columns, ((0, 0), (0, extra), (0, 0)))

    smem = pl.BlockSpec(memory_space=pltpu.SMEM)
    state_spec = pl.BlockSpec((trajectories, comps, SUB, row_length), lambda i: (0, 0, i, 0))
    fresh_spec = pl.BlockSpec((comps, SUB, row_length), lambda i: (0, i, 0))
    kept_spec = pl.BlockSpec((SUB, tiles * LANES, LANES), lambda i: (i, 0, 0))
    part_shape = (fields, 4 * padded_pairs, LANES)
    part_spec = pl.BlockSpec(part_shape, lambda i: (0, 0, 0))
    mend_spec = pl.BlockSpec((2,) + part_shape, lambda i: (0, 0, 0, 0))

    def leg_spec(k):
        return pl.BlockSpec((row_length, SUB, LANES), lambda i: (0, i, k))

    mib = 1024 * 1024

    def forward(k, made, span, clone_slot, patches):
        keep = k > 0
        kept_shape = jax.ShapeDtypeStruct((padded_pairs, tiles * LANES, LANES), jnp.bfloat16)
        return pl.pallas_call(
            functools.partial(
                forward_kernel, truncation=truncation, pairs=padded_pairs, keep=keep,
                real_pairs=pairs, count=len(patches), made=made, span=span, direct=direct,
            ),
            out_shape=[jax.ShapeDtypeStruct(part_shape, jnp.bfloat16)] * len(made)
            + [kept_shape] * keep,
            grid=(steps,),
            in_specs=[smem] * bool(patches)
            + [state_spec, leg_spec(k)]
            + [fresh_spec] * len(patches),
            out_specs=[part_spec] * len(made) + [kept_spec] * keep,
            scratch_shapes=[
                pltpu.VMEM((tiles * LANES * SUB, LANES), jnp.float32),
                pltpu.VMEM((tiles, span * comps * SUB, LANES), jnp.float32),
                pltpu.VMEM((4 * span * comps * padded_pairs, LANES), jnp.float32),
            ],
            compiler_params=pltpu.CompilerParams(vmem_limit_bytes=60 * mib),
            cost_estimate=pl.CostEstimate(
                flops=8 * span * comps * padded_pairs * row_length * LANES,
                bytes_accessed=16 * 1024 * 1024,
                transcendentals=0,
            ),
            name="forward",
        )(*([clone_slot] if patches else []), state, columns, *patches)

    def to_wire(x):
        if extra:
            x = x.reshape(slots, fields, 4, padded_pairs, LANES)[:, :, :, :pairs]
        x = x.reshape(slots, fields, 4 * pairs, split, lane_count)
        return jnp.transpose(x, (0, 3, 1, 2, 4)).reshape(space, fields, 4 * pairs, lane_count)

    def from_wire(x):
        x = x.reshape(slots, split, fields, 4, pairs, lane_count)
        x = jnp.transpose(x, (0, 2, 3, 4, 1, 5)).reshape(slots, fields, 4, pairs, LANES)
        if extra:
            x = jnp.pad(x, ((0, 0), (0, 0), (0, 0), (0, extra), (0, 0)))
        return x.reshape((slots,) + part_shape)

    def exchange(x):
        return lax.all_to_all(x, "space", split_axis=0, concat_axis=0, tiled=True)

    def swap(parts):
        got = list(parts)
        for n in reversed(range(1, space)):
            got[n] = lax.ppermute(parts[n], "space", [(d, d ^ n) for d in range(space)])
        return got

    def spread(parts):
        if direct:
            return swap(parts)
        x = exchange(to_wire(jnp.stack(parts)))
        x = jnp.pad(x, ((0, 0), (0, 0), (0, 0), (0, LANES - lane_count)))
        return [x[d] for d in range(space)]

    def collect(parts):
        if direct:
            return swap(parts)
        x = from_wire(exchange(jnp.stack(parts)[..., :lane_count]))
        return [x[n] for n in range(slots)]

    analysis = lax.optimization_barrier(
        fourier_tables(pairs * space, space, truncation, longitudes)
    )
    synthesis = analysis.T
    south = position // split % 2
    hemisphere = jnp.where(south == 0, sin_lat, -sin_lat)
    weights_all = math.pi * jnp.sqrt(1.0 - hemisphere * hemisphere) / (2 * half_lat)
    vmem = pl.BlockSpec(memory_space=pltpu.VMEM)
    modes = 4 * pairs * space

    def grid(k, parts):
        first = k * LANES + position % split * lane_count
        mu = lax.dynamic_slice_in_dim(hemisphere, first, lane_count)
        weight = lax.dynamic_slice_in_dim(weights_all, first, lane_count)
        short = LANES - lane_count
        if short:
            mu = jnp.pad(mu, (0, short))
            weight = jnp.pad(weight, (0, short))
        return pl.pallas_call(
            functools.partial(grid_kernel, scale=1.0 / truncation),
            out_shape=[jax.ShapeDtypeStruct(x.shape, jnp.bfloat16) for x in parts],
            in_specs=[smem] + [vmem] * (4 + space),
            out_specs=[vmem] * space,
            scratch_shapes=[
                pltpu.VMEM((modes, fields * LANES), jnp.bfloat16),
                pltpu.VMEM((longitudes, fields * LANES), jnp.bfloat16),
            ],
            compiler_params=pltpu.CompilerParams(vmem_limit_bytes=60 * mib),
            cost_estimate=pl.CostEstimate(
                flops=4 * modes * longitudes * fields * LANES,
                bytes_accessed=12 * 1024 * 1024,
                transcendentals=0,
            ),
            name="grid",
        )(order, (2.0 * mu)[None], weight[None], synthesis, analysis, *parts)

    def inverse(ws, legs, start, patches, mends, last):
        chunks = len(ws)
        stored = bool(patches)
        wide_scratch = pltpu.VMEM((chunks, tiles * LANES * SUB, LANES), jnp.float32)
        return pl.pallas_call(
            functools.partial(
                inverse_kernel,
                truncation=truncation,
                pairs=padded_pairs,
                chunks=chunks,
                last=last,
                stored=stored,
                slots=slots,
                count=count,
                real_pairs=pairs,
                direct=direct,
            ),
            out_shape=jax.ShapeDtypeStruct(state.shape, jnp.float32),
            grid=(steps,),
            in_specs=[smem] * 3
            + [part_spec] * (chunks * slots)
            + ([leg_spec(k) for k in range(chunks)] if stored else [kept_spec] * chunks)
            + [state_spec]
            + [fresh_spec] * len(patches)
            + [mend_spec] * len(mends),
            out_specs=state_spec,
            scratch_shapes=[
                pltpu.VMEM((chunks, 4 * rows * padded_pairs, LANES), jnp.float32),
                pltpu.VMEM((tiles, rows * SUB, LANES), jnp.float32),
            ]
            + ([wide_scratch] if stored else []),
            compiler_params=pltpu.CompilerParams(vmem_limit_bytes=60 * mib),
            cost_estimate=pl.CostEstimate(
                flops=8 * rows * padded_pairs * row_length * LANES * chunks,
                bytes_accessed=20 * 1024 * 1024,
                transcendentals=0,
            ),
            name="inverse",
        )(slot, gravity, stability, *[x for w in ws for x in w], *legs, start, *patches, *mends)

    everything = tuple(range(slots))
    if direct and trajectories % 2 == 0:
        near, far = everything[: slots // 2], everything[slots // 2 :]
        first = list(forward(0, far, trajectories // 2, None, []))
        second = list(forward(0, near, trajectories // 2, None, []))
        made = [second + first]
    else:
        made = [list(forward(0, everything, trajectories, None, []))]

    turn, made[0][0] = lax.optimization_barrier((clones, made[0][0]))
    picked, slot, route = pick_clones(spectra, turn)
    narrow = [send_clone(picked[i], route[i]) for i in range(count)]
    if extra:
        narrow = [jnp.pad(x, ((0, 0), (0, extra), (0, 0))) for x in narrow]
    turn = slot
    for k in range(1, chunk_count):
        made.append(list(forward(k, everything, trajectories, turn, narrow)))
        turn, made[k][0] = lax.optimization_barrier((slot, made[k][0]))
    kept = [x[-1] for x in made[1:]]
    sent = []
    for x in made:
        sent.append(spread(x[:slots]))
    back = []
    for k in range(chunk_count):
        got = grid(k, sent[k])
        if k == 0:
            later, got = lax.optimization_barrier((clones[:, 1], got))
        back.append(collect(got))
    fresh = [
        share_row(
            lax.dynamic_index_in_dim(spectra, lax.rem(later[i], trajectories), 0, keepdims=False),
            lax.div(later[i], trajectories),
        )
        for i in range(count)
    ]
    if extra:
        fresh = [jnp.pad(x, ((0, 0), (0, extra), (0, 0))) for x in fresh]
    back[0][0], fresh = lax.optimization_barrier((back[0][0], fresh))
    chosen = choose_rows(back[0], clones, trajectories, direct)
    mends = [send_clone(chosen[i], route[i]) for i in range(count)]
    start = inverse(back[:1], [columns], state, fresh, mends, False)
    for k in range(1, chunk_count - 1):
        start = inverse(back[k : k + 1], kept[k - 1 : k], start, [], [], False)
    out = inverse(back[-1:], kept[-1:], start, [], [], True)
    return out[:, :, :pairs] if extra else out


def solution(mesh):
    placed = (P("member", None, "space", None), P("space", None, None), P(), P(), P(), P())
    return jax.shard_map(
        shards,
        mesh=mesh,
        in_specs=placed,
        out_specs=P("member", None, "space", None),
        check_vma=False,
    )
```

```python
import functools
import math

import jax
import jax.numpy as jnp
from jax import lax
from jax.experimental import pallas as pl
from jax.experimental.pallas import tpu as pltpu
from jax.sharding import PartitionSpec as P


LANES = 128
SUB = 8
PACKED = 16
UNROLL_FORWARD = 8
UNROLL_INVERSE = 8
LONGITUDES_PER_WAVE = 2

time_step = 0.25
wave_scale = 16.0
diffusion = 0.02


def layout_terms(first_pair, count, lane0, lanes, truncation):
    pair = first_pair + lax.broadcasted_iota(jnp.int32, (count, lanes), 0)
    column = lane0 + lax.broadcasted_iota(jnp.int32, (count, lanes), 1)
    leading = column < truncation - pair
    offset = jnp.where(leading, column, column - (truncation - pair))
    order = jnp.where(leading, pair, truncation - 1 - pair)
    return leading, (offset & 1) == 1, order + offset


def slot_place(n, direct):
    return jnp.bitwise_xor(lax.axis_index("space"), n) if direct else jnp.int32(n)


def forward_kernel(
    *refs, truncation, pairs, real_pairs, keep, count, made, span, direct
):
    if count:
        slot_ref, refs = refs[0], refs[1:]
    spec_ref, leg_ref, refs = refs[0], refs[1], refs[2:]
    step = pl.program_id(0)
    row_length = truncation + 1
    _, comps, block, _ = spec_ref.shape
    rows = span * comps
    fresh_refs, refs = refs[:count], refs[count:]
    out_refs, refs = refs[: len(made)], refs[len(made) :]
    if keep:
        keep_ref, refs = refs[0], refs[1:]
    wide, xs, res = refs
    tiles = xs.shape[0]
    padded = tiles * LANES
    first_place = lax.div(slot_place(made[0], direct), 2)
    t0 = lax.div(first_place, span) * span

    @pl.when(step == 0)
    def _():
        wide[row_length * block :, :] = jnp.zeros(
            (wide.shape[0] - row_length * block, LANES), jnp.float32
        )

    wide[: row_length * block, :] = (
        leg_ref[...].astype(jnp.float32).reshape(row_length * block, LANES)
    )
    for k in range(tiles):
        width = min(LANES, row_length - k * LANES)
        lanes = slice(k * LANES, k * LANES + width)
        if width < LANES:
            xs[k] = jnp.zeros((rows * block, LANES), jnp.float32)
        xs[k, :, :width] = spec_ref[pl.ds(t0, span), :, :, lanes].reshape(rows * block, width)

    for i in range(count):
        slot = slot_ref[i] - t0

        @pl.when(jnp.logical_and(slot >= 0, slot < span))
        def _():
            at = pl.multiple_of(slot * comps * block, SUB)
            for k in range(tiles):
                width = min(LANES, row_length - k * LANES)
                fresh = fresh_refs[i][:, :, k * LANES : k * LANES + width].astype(jnp.float32)
                xs[k, pl.ds(at, comps * block), :width] = fresh.reshape(comps * block, width)

    first_pair = lax.axis_index("space") * real_pairs + step * block

    def one(q, carry):
        x = jnp.concatenate(
            [xs[k, pl.ds(q, rows, stride=block), :] for k in range(tiles)], axis=1
        )
        edge = truncation - first_pair - q
        group = PACKED if rows % PACKED == 0 else SUB
        column = lax.broadcasted_iota(jnp.int32, (group, padded), 1)
        leading = column < edge
        odd = (jnp.where(leading, column, column - edge) & 1) == 1
        sign = jnp.where(odd, -1.0, 1.0)
        kind = jnp.bfloat16 if group == PACKED else jnp.float32
        factors = [
            jnp.where(leading, 1.0, 0.0),
            jnp.where(leading, 0.0, 1.0),
            jnp.where(leading, sign, 0.0),
            jnp.where(leading, 0.0, sign),
        ]
        x = x.astype(kind)
        lhs = []
        for factor in factors:
            factor = factor.astype(kind)
            for at in range(0, rows, group):
                lhs.append(x[at : at + group] * factor)
        lhs = jnp.concatenate(lhs, axis=0).astype(jnp.bfloat16)
        rhs = wide[pl.ds(q, padded, stride=block), :].astype(jnp.bfloat16)
        if keep:
            keep_ref[q] = rhs
        got = jnp.dot(lhs, rhs, preferred_element_type=jnp.float32)
        res[pl.ds(step * block + q, 4 * rows, stride=pairs), :] = got
        return carry

    lax.fori_loop(0, block, one, 0, unroll=UNROLL_FORWARD)

    @pl.when(step == pl.num_programs(0) - 1)
    def _():
        for n, slot in enumerate(made):
            place = slot_place(slot, direct)
            t, s = lax.div(place, 2) - t0, lax.rem(place, 2)
            base = pl.multiple_of((s * (2 * rows) + t * comps) * pairs, SUB)
            for f in range(comps // 2):
                parts = []
                for r in range(2):
                    for h in range(2):
                        parts.append(res[pl.ds(base + (h * rows + 2 * f + r) * pairs, pairs), :])
                out_refs[n][f] = jnp.concatenate(parts, axis=0).astype(jnp.bfloat16)


def grid_kernel(order_ref, cor_ref, weight_ref, syn_ref, ana_ref, *refs, scale):
    sources = order_ref.shape[0]
    in_refs, out_refs, (modes, force) = refs[:sources], refs[sources:-2], refs[-2:]
    fields, rows, lanes = in_refs[0].shape
    longitudes = syn_ref.shape[0]
    for n in range(sources):
        at = pl.multiple_of(order_ref[n] * rows, 16)
        for f in range(fields):
            modes[pl.ds(at, rows), f * lanes : (f + 1) * lanes] = in_refs[n][f]
    cor = cor_ref[...]
    weight = weight_ref[...]
    span = 128

    def synth(b, carry):
        at = pl.multiple_of(b * span, span)
        g = (
            jnp.dot(syn_ref[pl.ds(at, span), :], modes[...], preferred_element_type=jnp.float32)
            * scale
        )
        field = [g[:, f * lanes : (f + 1) * lanes] for f in range(fields)]
        mean = 0.5 * (field[4] + field[5])
        out = [None] * fields
        for a in range(2):
            spin = field[a] + cor
            div = field[2 + a]
            out[a] = -spin * div
            out[2 + a] = spin * field[a] - 0.5 * div * div
            out[4 + a] = -(field[4 + a] + mean) * div
        for f in range(fields):
            force[pl.ds(at, span), f * lanes : (f + 1) * lanes] = out[f].astype(jnp.bfloat16)
        return carry

    lax.fori_loop(0, longitudes // span, synth, 0)

    def analyse(d, carry):
        at = pl.multiple_of(d * rows, 16)
        w = jnp.dot(ana_ref[pl.ds(at, rows), :], force[...], preferred_element_type=jnp.float32)
        for f in range(fields):
            lane = slice(f * lanes, (f + 1) * lanes)
            modes[pl.ds(at, rows), lane] = (w[:, lane] * weight).astype(jnp.bfloat16)
        return carry

    lax.fori_loop(0, sources, analyse, 0)
    for n in range(sources):
        at = pl.multiple_of(order_ref[n] * rows, 16)
        for f in range(fields):
            out_refs[n][f] = modes[pl.ds(at, rows), f * lanes : (f + 1) * lanes]


def step_terms(degree, gm, hm, truncation):
    eig = wave_scale * (degree * (degree + 1)).astype(jnp.float32) / float(truncation * truncation)
    damping = 1.0 / (1.0 + diffusion * eig * eig)
    coupling = time_step * time_step * eig
    pm = [[gm[a][0] * hm[0][b] + gm[a][1] * hm[1][b] for b in range(2)] for a in range(2)]
    diag = [1.0 + coupling * pm[a][a] for a in range(2)]
    cross = [coupling * pm[0][1], coupling * pm[1][0]]
    inverse = 1.0 / (diag[0] * diag[1] - cross[0] * cross[1])
    solve = [
        [diag[1] * inverse, -cross[0] * inverse],
        [-cross[1] * inverse, diag[0] * inverse],
    ]
    push = [[time_step * eig * gm[a][b] for b in range(2)] for a in range(2)]
    return damping, solve, push


def semi_implicit_slabs(old, tend, terms, hm):
    damping, solve, push = terms
    out = [None] * 12
    for r in range(2):
        star = [old[c * 2 + r] + time_step * tend[c * 2 + r] for c in range(6)]
        right = [star[2 + a] + push[a][0] * star[4] + push[a][1] * star[5] for a in range(2)]
        div = [solve[a][0] * right[0] + solve[a][1] * right[1] for a in range(2)]
        for a in range(2):
            heat = (time_step * hm[a][0]) * div[0] + (time_step * hm[a][1]) * div[1]
            out[a * 2 + r] = damping * star[a]
            out[(2 + a) * 2 + r] = damping * div[a]
            out[(4 + a) * 2 + r] = damping * (star[4 + a] - heat)
    return out


def inverse_kernel(
    slot_ref,
    gravity_ref,
    stability_ref,
    *refs,
    truncation,
    pairs,
    real_pairs,
    chunks,
    last,
    stored,
    slots,
    count,
    direct,
):
    w_refs, refs = refs[: chunks * slots], refs[chunks * slots :]
    leg_refs, refs = refs[:chunks], refs[chunks:]
    spec_ref, refs = refs[0], refs[1:]
    patches = count if stored else 0
    fresh_refs, refs = refs[:patches], refs[patches:]
    mend_refs, refs = refs[:patches], refs[patches:]
    out_ref, ws, ten = refs[:3]
    if stored:
        wide = refs[3]
    step = pl.program_id(0)
    row_length = truncation + 1
    trajectories, comps, block, _ = out_ref.shape
    rows = trajectories * comps
    tiles = ten.shape[0]
    padded = tiles * LANES

    @pl.when(step == 0)
    def _():
        if stored:
            for k in range(chunks):
                wide[k, row_length * block :, :] = jnp.zeros(
                    (wide.shape[1] - row_length * block, LANES), jnp.float32
                )

        def fill(k, t, s, source):
            base = pl.multiple_of((s * (2 * rows) + t * comps) * pairs, SUB)
            for f in range(comps // 2):
                got = source(f).astype(jnp.float32)
                for r in range(2):
                    for h in range(2):
                        at = (r * 2 + h) * pairs
                        ws[k, pl.ds(base + (h * rows + 2 * f + r) * pairs, pairs), :] = got[
                            at : at + pairs, :
                        ]

        for k in range(chunks):
            for n in range(slots):
                place = slot_place(n, direct)
                fill(k, lax.div(place, 2), lax.rem(place, 2), lambda f: w_refs[k * slots + n][f])
        for i in range(patches):

            @pl.when(slot_ref[i] >= 0)
            def _():
                for s in range(2):
                    fill(0, slot_ref[i], s, lambda f: mend_refs[i][s, f])

    if stored:
        for k in range(chunks):
            wide[k, : row_length * block, :] = (
                leg_refs[k][...].astype(jnp.float32).reshape(row_length * block, LANES)
            )
    first_pair = lax.axis_index("space") * real_pairs + step * block

    def one(q, carry):
        at = pl.ds(step * block + q, 4 * rows, stride=pairs)
        lhs = jnp.concatenate([ws[k, at, :].astype(jnp.bfloat16) for k in range(chunks)], axis=1)
        if not stored:
            rhs = jnp.concatenate([leg_refs[k][q] for k in range(chunks)], axis=1)
        else:
            at = pl.ds(q, padded, stride=block)
            rhs = jnp.concatenate(
                [wide[k, at, :].astype(jnp.bfloat16) for k in range(chunks)], axis=1
            )
        got = lax.dot_general(
            lhs, rhs, (((1,), (1,)), ((), ())), preferred_element_type=jnp.float32
        )
        leading, odd, _ = layout_terms(first_pair + q, 1, 0, padded, truncation)
        north = jnp.where(leading, got[:rows], got[rows : 2 * rows])
        south = jnp.where(leading, got[2 * rows : 3 * rows], got[3 * rows :])
        total = north + jnp.where(odd, -south, south)
        for k in range(tiles):
            ten[k, pl.ds(q, rows, stride=block), :] = total[:, k * LANES : (k + 1) * LANES]
        return carry

    lax.fori_loop(0, block, one, 0, unroll=UNROLL_INVERSE)

    if last:
        gm = [[gravity_ref[a, b] for b in range(2)] for a in range(2)]
        hm = [[stability_ref[a, b] for b in range(2)] for a in range(2)]
    for k in range(tiles):
        width = min(LANES, row_length - k * LANES)
        lanes = slice(k * LANES, k * LANES + width)
        if last:
            _, _, degree = layout_terms(first_pair, block, k * LANES, width, truncation)
            terms = step_terms(degree, gm, hm, truncation)

        def body(t, carry):
            tend = []
            for c in range(comps):
                at = pl.multiple_of((t * comps + c) * block, SUB)
                value = ten[k, pl.ds(at, block), :][:, :width]
                tend.append(value)
            old = [spec_ref[t, c, :, lanes] for c in range(comps)]
            if last:
                tend = semi_implicit_slabs(old, tend, terms, hm)
            else:
                for i in range(patches):
                    mine = slot_ref[i] == t
                    old = [jnp.where(mine, fresh_refs[i][c, :, lanes], old[c]) for c in range(comps)]
                tend = [old[c] + time_step * tend[c] for c in range(comps)]
            for c in range(comps):
                out_ref[t, c, :, lanes] = tend[c]
            return carry

        lax.fori_loop(0, trajectories, body, 0)


def fourier_tables(pair_count, groups, truncation, longitudes):
    half_turn = longitudes // 2
    order = jnp.arange(pair_count + 1, dtype=jnp.int32)[None, :, None]
    column = jnp.arange(half_turn, dtype=jnp.int32)[None, None, :]
    quarter = jnp.arange(2, dtype=jnp.int32)[:, None, None] * (longitudes // 4)
    phase = (order * column + quarter) % longitudes
    angle = phase.astype(jnp.float32) * (2.0 * math.pi / longitudes)
    base = lax.optimization_barrier(jnp.cos(angle).astype(jnp.bfloat16))
    low = base[:, :pair_count]
    flip = (1 - 2 * (column % 2)) * (1 - 2 * jnp.arange(2, dtype=jnp.int32)[:, None, None])
    high = base[:, 1:] * flip.astype(jnp.bfloat16)
    pair = jnp.arange(pair_count, dtype=jnp.int32)[None, :, None]
    low_sign = (1 - 2 * (pair % 2)).astype(jnp.bfloat16)
    high_sign = (1 - 2 * ((truncation - 1 - pair) % 2)).astype(jnp.bfloat16)
    low = jnp.concatenate([low, low * low_sign], axis=2)
    high = jnp.concatenate([high, high * high_sign], axis=2)
    table = jnp.stack([low, high], axis=1)
    table = table.reshape(2, 2, groups, pair_count // groups, longitudes)
    return jnp.transpose(table, (2, 0, 1, 3, 4)).reshape(4 * pair_count, longitudes)


def far_members(members):
    return [(a, b) for a in range(members) for b in range(a + 1, members) if a ^ b != 1]


def pick_kernel(clones_ref, spec_ref, row_ref, slot_ref, *route_refs, local):
    row_ref[...] = spec_ref[...].astype(jnp.bfloat16)
    members, member = lax.axis_size("member"), lax.axis_index("member")
    for i, route_ref in enumerate(route_refs):
        source = lax.div(clones_ref[i, 1], local)
        target = lax.div(clones_ref[i, 0], local)
        route = jnp.where(source == target, 0, 1)
        low, high = jnp.minimum(source, target), jnp.maximum(source, target)
        for k, (a, b) in enumerate(far_members(members)):
            route = jnp.where(jnp.logical_and(low == a, high == b), 2 + k, route)
        route_ref[0] = route
        slot_ref[i] = jnp.where(target == member, clones_ref[i, 0] - target * local, -1)


def pick_clones(spectra, clones):
    local, comps, pairs, row_length = spectra.shape
    count = clones.shape[0]
    smem = pl.BlockSpec(memory_space=pltpu.SMEM)
    block = (1, comps, pairs, row_length)
    got = pl.pallas_call(
        functools.partial(pick_kernel, local=local),
        out_shape=[
            jax.ShapeDtypeStruct((count,) + block[1:], jnp.bfloat16),
            jax.ShapeDtypeStruct((count,), jnp.int32),
        ]
        + [jax.ShapeDtypeStruct((1,), jnp.int32)] * count,
        grid_spec=pltpu.PrefetchScalarGridSpec(
            num_scalar_prefetch=1,
            grid=(count,),
            in_specs=[pl.BlockSpec(block, lambda i, c: (lax.rem(c[i, 1], local), 0, 0, 0))],
            out_specs=[pl.BlockSpec(block, lambda i, c: (i, 0, 0, 0))] + [smem] * (1 + count),
        ),
        cost_estimate=pl.CostEstimate(
            flops=0, bytes_accessed=6 * 1024 * 1024, transcendentals=0
        ),
        name="pick",
    )(clones, spectra)
    return got[0], got[1], [r.reshape(()) for r in got[2:]]


def choose_kernel(clones_ref, *refs, local, slots, direct):
    in_refs, out_refs = refs[:slots], refs[slots:]
    for i, out_ref in enumerate(out_refs):
        t = lax.rem(clones_ref[i, 1], local)
        for n in range(slots):
            place = slot_place(n, direct)

            @pl.when(lax.div(place, 2) == t)
            def _():
                out_ref[lax.rem(place, 2)] = in_refs[n][...]


def choose_rows(parts, clones, local, direct):
    vmem = pl.BlockSpec(memory_space=pltpu.VMEM)
    return pl.pallas_call(
        functools.partial(choose_kernel, local=local, slots=len(parts), direct=direct),
        out_shape=[jax.ShapeDtypeStruct((2,) + parts[0].shape, parts[0].dtype)] * clones.shape[0],
        in_specs=[pl.BlockSpec(memory_space=pltpu.SMEM)] + [vmem] * len(parts),
        out_specs=[vmem] * clones.shape[0],
        cost_estimate=pl.CostEstimate(
            flops=0, bytes_accessed=4 * 1024 * 1024, transcendentals=0
        ),
        name="choose",
    )(clones, *parts)


def send_clone(row, route):
    members = lax.axis_size("member")

    def swap(pairs):
        both = pairs + [(b, a) for a, b in pairs]
        return lambda v: lax.ppermute(v, "member", both)

    branches = [lambda v: v, swap([(a, a + 1) for a in range(0, members, 2)])]
    branches += [swap([pair]) for pair in far_members(members)]
    return lax.switch(route, branches, row)


def share_row(row, owner):
    members = lax.axis_size("member")
    differs = jnp.bitwise_xor(owner, lax.axis_index("member").astype(jnp.int32))
    bit = 1
    while bit < members:
        other = lax.ppermute(row, "member", [(m, m ^ bit) for m in range(members)])
        row = jnp.where(jnp.bitwise_and(differs, bit) != 0, other, row)
        bit *= 2
    return row


def shards(spectra, legendre, sin_lat, gravity, stability, clones):
    trajectories, comps, pairs, row_length = spectra.shape
    truncation = row_length - 1
    half_lat = legendre.shape[2]
    longitudes = LONGITUDES_PER_WAVE * truncation
    space = lax.axis_size("space")
    position = lax.axis_index("space")
    fields = comps // 2
    split = space // (2 * trajectories)
    lane_count = LANES // split
    chunk_count = half_lat // LANES
    padded_pairs = -(-pairs // SUB) * SUB
    steps = padded_pairs // SUB
    tiles = -(-row_length // LANES)
    extra = padded_pairs - pairs
    rows = trajectories * comps

    count = clones.shape[0]
    slots = 2 * trajectories
    direct = split == 1
    state = spectra
    if extra:
        state = jnp.pad(state, ((0, 0), (0, 0), (0, extra), (0, 0)))
    order = jnp.arange(space, dtype=jnp.int32)
    if direct:
        order = jnp.bitwise_xor(position.astype(jnp.int32), order)
    columns = jnp.transpose(legendre, (1, 0, 2))
    if extra:
        columns = jnp.pad(columns, ((0, 0), (0, extra), (0, 0)))

    smem = pl.BlockSpec(memory_space=pltpu.SMEM)
    state_spec = pl.BlockSpec((trajectories, comps, SUB, row_length), lambda i: (0, 0, i, 0))
    fresh_spec = pl.BlockSpec((comps, SUB, row_length), lambda i: (0, i, 0))
    kept_spec = pl.BlockSpec((SUB, tiles * LANES, LANES), lambda i: (i, 0, 0))
    part_shape = (fields, 4 * padded_pairs, LANES)
    part_spec = pl.BlockSpec(part_shape, lambda i: (0, 0, 0))
    mend_spec = pl.BlockSpec((2,) + part_shape, lambda i: (0, 0, 0, 0))

    def leg_spec(k):
        return pl.BlockSpec((row_length, SUB, LANES), lambda i: (0, i, k))

    mib = 1024 * 1024

    def forward(k, made, span, clone_slot, patches):
        keep = k > 0
        kept_shape = jax.ShapeDtypeStruct((padded_pairs, tiles * LANES, LANES), jnp.bfloat16)
        return pl.pallas_call(
            functools.partial(
                forward_kernel, truncation=truncation, pairs=padded_pairs, keep=keep,
                real_pairs=pairs, count=len(patches), made=made, span=span, direct=direct,
            ),
            out_shape=[jax.ShapeDtypeStruct(part_shape, jnp.bfloat16)] * len(made)
            + [kept_shape] * keep,
            grid=(steps,),
            in_specs=[smem] * bool(patches)
            + [state_spec, leg_spec(k)]
            + [fresh_spec] * len(patches),
            out_specs=[part_spec] * len(made) + [kept_spec] * keep,
            scratch_shapes=[
                pltpu.VMEM((tiles * LANES * SUB, LANES), jnp.float32),
                pltpu.VMEM((tiles, span * comps * SUB, LANES), jnp.float32),
                pltpu.VMEM((4 * span * comps * padded_pairs, LANES), jnp.float32),
            ],
            compiler_params=pltpu.CompilerParams(vmem_limit_bytes=60 * mib),
            cost_estimate=pl.CostEstimate(
                flops=8 * span * comps * padded_pairs * row_length * LANES,
                bytes_accessed=16 * 1024 * 1024,
                transcendentals=0,
            ),
            name="forward",
        )(*([clone_slot] if patches else []), state, columns, *patches)

    def to_wire(x):
        if extra:
            x = x.reshape(slots, fields, 4, padded_pairs, LANES)[:, :, :, :pairs]
        x = x.reshape(slots, fields, 4 * pairs, split, lane_count)
        return jnp.transpose(x, (0, 3, 1, 2, 4)).reshape(space, fields, 4 * pairs, lane_count)

    def from_wire(x):
        x = x.reshape(slots, split, fields, 4, pairs, lane_count)
        x = jnp.transpose(x, (0, 2, 3, 4, 1, 5)).reshape(slots, fields, 4, pairs, LANES)
        if extra:
            x = jnp.pad(x, ((0, 0), (0, 0), (0, 0), (0, extra), (0, 0)))
        return x.reshape((slots,) + part_shape)

    def exchange(x):
        return lax.all_to_all(x, "space", split_axis=0, concat_axis=0, tiled=True)

    def swap(parts):
        got = list(parts)
        for n in reversed(range(1, space)):
            got[n] = lax.ppermute(parts[n], "space", [(d, d ^ n) for d in range(space)])
        return got

    def spread(parts):
        if direct:
            return swap(parts)
        x = exchange(to_wire(jnp.stack(parts)))
        x = jnp.pad(x, ((0, 0), (0, 0), (0, 0), (0, LANES - lane_count)))
        return [x[d] for d in range(space)]

    def collect(parts):
        if direct:
            return swap(parts)
        x = from_wire(exchange(jnp.stack(parts)[..., :lane_count]))
        return [x[n] for n in range(slots)]

    analysis = lax.optimization_barrier(
        fourier_tables(pairs * space, space, truncation, longitudes)
    )
    synthesis = analysis.T
    south = position // split % 2
    hemisphere = jnp.where(south == 0, sin_lat, -sin_lat)
    weights_all = math.pi * jnp.sqrt(1.0 - hemisphere * hemisphere) / (2 * half_lat)
    vmem = pl.BlockSpec(memory_space=pltpu.VMEM)
    modes = 4 * pairs * space

    def grid(k, parts):
        first = k * LANES + position % split * lane_count
        mu = lax.dynamic_slice_in_dim(hemisphere, first, lane_count)
        weight = lax.dynamic_slice_in_dim(weights_all, first, lane_count)
        short = LANES - lane_count
        if short:
            mu = jnp.pad(mu, (0, short))
            weight = jnp.pad(weight, (0, short))
        return pl.pallas_call(
            functools.partial(grid_kernel, scale=1.0 / truncation),
            out_shape=[jax.ShapeDtypeStruct(x.shape, jnp.bfloat16) for x in parts],
            in_specs=[smem] + [vmem] * (4 + space),
            out_specs=[vmem] * space,
            scratch_shapes=[
                pltpu.VMEM((modes, fields * LANES), jnp.bfloat16),
                pltpu.VMEM((longitudes, fields * LANES), jnp.bfloat16),
            ],
            compiler_params=pltpu.CompilerParams(vmem_limit_bytes=60 * mib),
            cost_estimate=pl.CostEstimate(
                flops=4 * modes * longitudes * fields * LANES,
                bytes_accessed=12 * 1024 * 1024,
                transcendentals=0,
            ),
            name="grid",
        )(order, (2.0 * mu)[None], weight[None], synthesis, analysis, *parts)

    def inverse(ws, legs, start, patches, mends, last):
        chunks = len(ws)
        stored = bool(patches)
        wide_scratch = pltpu.VMEM((chunks, tiles * LANES * SUB, LANES), jnp.float32)
        return pl.pallas_call(
            functools.partial(
                inverse_kernel,
                truncation=truncation,
                pairs=padded_pairs,
                chunks=chunks,
                last=last,
                stored=stored,
                slots=slots,
                count=count,
                real_pairs=pairs,
                direct=direct,
            ),
            out_shape=jax.ShapeDtypeStruct(state.shape, jnp.float32),
            grid=(steps,),
            in_specs=[smem] * 3
            + [part_spec] * (chunks * slots)
            + ([leg_spec(k) for k in range(chunks)] if stored else [kept_spec] * chunks)
            + [state_spec]
            + [fresh_spec] * len(patches)
            + [mend_spec] * len(mends),
            out_specs=state_spec,
            scratch_shapes=[
                pltpu.VMEM((chunks, 4 * rows * padded_pairs, LANES), jnp.float32),
                pltpu.VMEM((tiles, rows * SUB, LANES), jnp.float32),
            ]
            + ([wide_scratch] if stored else []),
            compiler_params=pltpu.CompilerParams(vmem_limit_bytes=60 * mib),
            cost_estimate=pl.CostEstimate(
                flops=8 * rows * padded_pairs * row_length * LANES * chunks,
                bytes_accessed=20 * 1024 * 1024,
                transcendentals=0,
            ),
            name="inverse",
        )(slot, gravity, stability, *[x for w in ws for x in w], *legs, start, *patches, *mends)

    everything = tuple(range(slots))
    halved = direct and trajectories % 2 == 0
    near, far = everything[: slots // 2], everything[slots // 2 :]
    if halved:
        first = list(forward(0, far, trajectories // 2, None, []))
        second = list(forward(0, near, trajectories // 2, None, []))
    else:
        first = list(forward(0, everything, trajectories, None, []))

    turn, first[0] = lax.optimization_barrier((clones, first[0]))
    made = [second + first if halved else first]
    picked, slot, route = pick_clones(spectra, turn)
    narrow = [send_clone(picked[i], route[i]) for i in range(count)]
    if extra:
        narrow = [jnp.pad(x, ((0, 0), (0, extra), (0, 0))) for x in narrow]
    turn = slot
    for k in range(1, chunk_count):
        made.append(list(forward(k, everything, trajectories, turn, narrow)))
        turn, made[k][0] = lax.optimization_barrier((slot, made[k][0]))
    kept = [x[-1] for x in made[1:]]
    sent = []
    for x in made:
        sent.append(spread(x[:slots]))
    back = []
    for k in range(chunk_count):
        got = grid(k, sent[k])
        if k == 0:
            later, got = lax.optimization_barrier((clones[:, 1], got))
        back.append(collect(got))
    fresh = [
        share_row(
            lax.dynamic_index_in_dim(spectra, lax.rem(later[i], trajectories), 0, keepdims=False),
            lax.div(later[i], trajectories),
        )
        for i in range(count)
    ]
    if extra:
        fresh = [jnp.pad(x, ((0, 0), (0, extra), (0, 0))) for x in fresh]
    back[0][0], fresh = lax.optimization_barrier((back[0][0], fresh))
    chosen = choose_rows(back[0], clones, trajectories, direct)
    mends = [send_clone(chosen[i], route[i]) for i in range(count)]
    start = inverse(back[:1], [columns], state, fresh, mends, False)
    for k in range(1, chunk_count - 1):
        start = inverse(back[k : k + 1], kept[k - 1 : k], start, [], [], False)
    out = inverse(back[-1:], kept[-1:], start, [], [], True)
    return out[:, :, :pairs] if extra else out


def solution(mesh):
    placed = (P("member", None, "space", None), P("space", None, None), P(), P(), P(), P())
    return jax.shard_map(
        shards,
        mesh=mesh,
        in_specs=placed,
        out_specs=P("member", None, "space", None),
        check_vma=False,
    )
```

```python
import functools
import math

import jax
import jax.numpy as jnp
from jax import lax
from jax.experimental import pallas as pl
from jax.experimental.pallas import tpu as pltpu
from jax.sharding import PartitionSpec as P


LANES = 128
SUB = 8
PACKED = 16
UNROLL_FORWARD = 8
UNROLL_INVERSE = 8
LONGITUDES_PER_WAVE = 2

time_step = 0.25
wave_scale = 16.0
diffusion = 0.02


def layout_terms(first_pair, count, lane0, lanes, truncation):
    pair = first_pair + lax.broadcasted_iota(jnp.int32, (count, lanes), 0)
    column = lane0 + lax.broadcasted_iota(jnp.int32, (count, lanes), 1)
    leading = column < truncation - pair
    offset = jnp.where(leading, column, column - (truncation - pair))
    order = jnp.where(leading, pair, truncation - 1 - pair)
    return leading, (offset & 1) == 1, order + offset


def slot_place(n, direct):
    return jnp.bitwise_xor(lax.axis_index("space"), n) if direct else jnp.int32(n)


def forward_kernel(
    *refs, truncation, pairs, real_pairs, keep, count, made, span, direct
):
    if count:
        slot_ref, refs = refs[0], refs[1:]
    spec_ref, leg_ref, refs = refs[0], refs[1], refs[2:]
    step = pl.program_id(0)
    row_length = truncation + 1
    _, comps, block, _ = spec_ref.shape
    rows = span * comps
    fresh_refs, refs = refs[:count], refs[count:]
    out_refs, refs = refs[: len(made)], refs[len(made) :]
    if keep:
        keep_ref, refs = refs[0], refs[1:]
    wide, xs, res = refs
    tiles = xs.shape[0]
    padded = tiles * LANES
    first_place = lax.div(slot_place(made[0], direct), 2)
    t0 = lax.div(first_place, span) * span

    @pl.when(step == 0)
    def _():
        wide[row_length * block :, :] = jnp.zeros(
            (wide.shape[0] - row_length * block, LANES), jnp.float32
        )

    wide[: row_length * block, :] = (
        leg_ref[...].astype(jnp.float32).reshape(row_length * block, LANES)
    )
    for k in range(tiles):
        width = min(LANES, row_length - k * LANES)
        lanes = slice(k * LANES, k * LANES + width)
        if width < LANES:
            xs[k] = jnp.zeros((rows * block, LANES), jnp.float32)
        xs[k, :, :width] = spec_ref[pl.ds(t0, span), :, :, lanes].reshape(rows * block, width)

    for i in range(count):
        slot = slot_ref[i] - t0

        @pl.when(jnp.logical_and(slot >= 0, slot < span))
        def _():
            at = pl.multiple_of(slot * comps * block, SUB)
            for k in range(tiles):
                width = min(LANES, row_length - k * LANES)
                fresh = fresh_refs[i][:, :, k * LANES : k * LANES + width].astype(jnp.float32)
                xs[k, pl.ds(at, comps * block), :width] = fresh.reshape(comps * block, width)

    first_pair = lax.axis_index("space") * real_pairs + step * block

    def one(q, carry):
        x = jnp.concatenate(
            [xs[k, pl.ds(q, rows, stride=block), :] for k in range(tiles)], axis=1
        )
        edge = truncation - first_pair - q
        group = PACKED if rows % PACKED == 0 else SUB
        column = lax.broadcasted_iota(jnp.int32, (group, padded), 1)
        leading = column < edge
        odd = (jnp.where(leading, column, column - edge) & 1) == 1
        sign = jnp.where(odd, -1.0, 1.0)
        kind = jnp.bfloat16 if group == PACKED else jnp.float32
        factors = [
            jnp.where(leading, 1.0, 0.0),
            jnp.where(leading, 0.0, 1.0),
            jnp.where(leading, sign, 0.0),
            jnp.where(leading, 0.0, sign),
        ]
        x = x.astype(kind)
        lhs = []
        for factor in factors:
            factor = factor.astype(kind)
            for at in range(0, rows, group):
                lhs.append(x[at : at + group] * factor)
        lhs = jnp.concatenate(lhs, axis=0).astype(jnp.bfloat16)
        rhs = wide[pl.ds(q, padded, stride=block), :].astype(jnp.bfloat16)
        if keep:
            keep_ref[q] = rhs
        got = jnp.dot(lhs, rhs, preferred_element_type=jnp.float32)
        res[pl.ds(step * block + q, 4 * rows, stride=pairs), :] = got
        return carry

    lax.fori_loop(0, block, one, 0, unroll=UNROLL_FORWARD)

    @pl.when(step == pl.num_programs(0) - 1)
    def _():
        for n, slot in enumerate(made):
            place = slot_place(slot, direct)
            t, s = lax.div(place, 2) - t0, lax.rem(place, 2)
            base = pl.multiple_of((s * (2 * rows) + t * comps) * pairs, SUB)
            for f in range(comps // 2):
                parts = []
                for r in range(2):
                    for h in range(2):
                        parts.append(res[pl.ds(base + (h * rows + 2 * f + r) * pairs, pairs), :])
                out_refs[n][f] = jnp.concatenate(parts, axis=0).astype(jnp.bfloat16)


def grid_kernel(order_ref, cor_ref, weight_ref, syn_ref, ana_ref, *refs, scale):
    sources = order_ref.shape[0]
    in_refs, out_refs, (modes, force) = refs[:sources], refs[sources:-2], refs[-2:]
    fields, rows, lanes = in_refs[0].shape
    longitudes = syn_ref.shape[0]
    for n in range(sources):
        at = pl.multiple_of(order_ref[n] * rows, 16)
        for f in range(fields):
            modes[pl.ds(at, rows), f * lanes : (f + 1) * lanes] = in_refs[n][f]
    cor = cor_ref[...]
    weight = weight_ref[...]
    span = 128

    def synth(b, carry):
        at = pl.multiple_of(b * span, span)
        g = (
            jnp.dot(syn_ref[pl.ds(at, span), :], modes[...], preferred_element_type=jnp.float32)
            * scale
        )
        field = [g[:, f * lanes : (f + 1) * lanes] for f in range(fields)]
        mean = 0.5 * (field[4] + field[5])
        out = [None] * fields
        for a in range(2):
            spin = field[a] + cor
            div = field[2 + a]
            out[a] = -spin * div
            out[2 + a] = spin * field[a] - 0.5 * div * div
            out[4 + a] = -(field[4 + a] + mean) * div
        for f in range(fields):
            force[pl.ds(at, span), f * lanes : (f + 1) * lanes] = out[f].astype(jnp.bfloat16)
        return carry

    lax.fori_loop(0, longitudes // span, synth, 0)

    def analyse(d, carry):
        at = pl.multiple_of(d * rows, 16)
        w = jnp.dot(ana_ref[pl.ds(at, rows), :], force[...], preferred_element_type=jnp.float32)
        for f in range(fields):
            lane = slice(f * lanes, (f + 1) * lanes)
            modes[pl.ds(at, rows), lane] = (w[:, lane] * weight).astype(jnp.bfloat16)
        return carry

    lax.fori_loop(0, sources, analyse, 0)
    for n in range(sources):
        at = pl.multiple_of(order_ref[n] * rows, 16)
        for f in range(fields):
            out_refs[n][f] = modes[pl.ds(at, rows), f * lanes : (f + 1) * lanes]


def step_terms(degree, gm, hm, truncation):
    eig = wave_scale * (degree * (degree + 1)).astype(jnp.float32) / float(truncation * truncation)
    damping = 1.0 / (1.0 + diffusion * eig * eig)
    coupling = time_step * time_step * eig
    pm = [[gm[a][0] * hm[0][b] + gm[a][1] * hm[1][b] for b in range(2)] for a in range(2)]
    diag = [1.0 + coupling * pm[a][a] for a in range(2)]
    cross = [coupling * pm[0][1], coupling * pm[1][0]]
    inverse = 1.0 / (diag[0] * diag[1] - cross[0] * cross[1])
    solve = [
        [diag[1] * inverse, -cross[0] * inverse],
        [-cross[1] * inverse, diag[0] * inverse],
    ]
    push = [[time_step * eig * gm[a][b] for b in range(2)] for a in range(2)]
    return damping, solve, push


def semi_implicit_slabs(old, tend, terms, hm):
    damping, solve, push = terms
    out = [None] * 12
    for r in range(2):
        star = [old[c * 2 + r] + time_step * tend[c * 2 + r] for c in range(6)]
        right = [star[2 + a] + push[a][0] * star[4] + push[a][1] * star[5] for a in range(2)]
        div = [solve[a][0] * right[0] + solve[a][1] * right[1] for a in range(2)]
        for a in range(2):
            heat = (time_step * hm[a][0]) * div[0] + (time_step * hm[a][1]) * div[1]
            out[a * 2 + r] = damping * star[a]
            out[(2 + a) * 2 + r] = damping * div[a]
            out[(4 + a) * 2 + r] = damping * (star[4 + a] - heat)
    return out


def inverse_kernel(
    slot_ref,
    gravity_ref,
    stability_ref,
    *refs,
    truncation,
    pairs,
    real_pairs,
    chunks,
    last,
    stored,
    slots,
    count,
    patches,
    direct,
):
    w_refs, refs = refs[: chunks * slots], refs[chunks * slots :]
    leg_refs, refs = refs[:chunks], refs[chunks:]
    spec_ref, refs = refs[0], refs[1:]
    mended = count if stored else 0
    fresh_refs, refs = refs[: 2 * patches], refs[2 * patches :]
    mend_refs, refs = refs[:mended], refs[mended:]
    out_ref, ws, ten = refs[:3]
    if stored:
        wide = refs[3]
    step = pl.program_id(0)
    row_length = truncation + 1
    trajectories, comps, block, _ = out_ref.shape
    rows = trajectories * comps
    tiles = ten.shape[0]
    padded = tiles * LANES

    @pl.when(step == 0)
    def _():
        if stored:
            for k in range(chunks):
                wide[k, row_length * block :, :] = jnp.zeros(
                    (wide.shape[1] - row_length * block, LANES), jnp.float32
                )

        def fill(k, t, s, source):
            base = pl.multiple_of((s * (2 * rows) + t * comps) * pairs, SUB)
            for f in range(comps // 2):
                got = source(f).astype(jnp.float32)
                for r in range(2):
                    for h in range(2):
                        at = (r * 2 + h) * pairs
                        ws[k, pl.ds(base + (h * rows + 2 * f + r) * pairs, pairs), :] = got[
                            at : at + pairs, :
                        ]

        for k in range(chunks):
            for n in range(slots):
                place = slot_place(n, direct)
                fill(k, lax.div(place, 2), lax.rem(place, 2), lambda f: w_refs[k * slots + n][f])
        for i in range(mended):

            @pl.when(slot_ref[i] >= 0)
            def _():
                for s in range(2):
                    fill(0, slot_ref[i], s, lambda f: mend_refs[i][s, f])

    if stored:
        for k in range(chunks):
            wide[k, : row_length * block, :] = (
                leg_refs[k][...].astype(jnp.float32).reshape(row_length * block, LANES)
            )
    first_pair = lax.axis_index("space") * real_pairs + step * block

    def one(q, carry):
        at = pl.ds(step * block + q, 4 * rows, stride=pairs)
        lhs = jnp.concatenate([ws[k, at, :].astype(jnp.bfloat16) for k in range(chunks)], axis=1)
        if not stored:
            rhs = jnp.concatenate([leg_refs[k][q] for k in range(chunks)], axis=1)
        else:
            at = pl.ds(q, padded, stride=block)
            rhs = jnp.concatenate(
                [wide[k, at, :].astype(jnp.bfloat16) for k in range(chunks)], axis=1
            )
        got = lax.dot_general(
            lhs, rhs, (((1,), (1,)), ((), ())), preferred_element_type=jnp.float32
        )
        leading, odd, _ = layout_terms(first_pair + q, 1, 0, padded, truncation)
        north = jnp.where(leading, got[:rows], got[rows : 2 * rows])
        south = jnp.where(leading, got[2 * rows : 3 * rows], got[3 * rows :])
        total = north + jnp.where(odd, -south, south)
        for k in range(tiles):
            ten[k, pl.ds(q, rows, stride=block), :] = total[:, k * LANES : (k + 1) * LANES]
        return carry

    lax.fori_loop(0, block, one, 0, unroll=UNROLL_INVERSE)

    if last:
        gm = [[gravity_ref[a, b] for b in range(2)] for a in range(2)]
        hm = [[stability_ref[a, b] for b in range(2)] for a in range(2)]
    for k in range(tiles):
        width = min(LANES, row_length - k * LANES)
        lanes = slice(k * LANES, k * LANES + width)
        if last:
            _, _, degree = layout_terms(first_pair, block, k * LANES, width, truncation)
            terms = step_terms(degree, gm, hm, truncation)

        def body(t, carry):
            tend = []
            for c in range(comps):
                at = pl.multiple_of((t * comps + c) * block, SUB)
                value = ten[k, pl.ds(at, block), :][:, :width]
                tend.append(value)
            old = [spec_ref[t, c, :, lanes] for c in range(comps)]
            for i in range(mended):
                mine = slot_ref[i] == t
                old = [jnp.where(mine, 0.0, old[c]) for c in range(comps)]
            for i in range(patches):
                here = jnp.logical_and(slot_ref[i] == t, slot_ref[count + i] == 0)
                there = jnp.logical_and(slot_ref[i] == t, slot_ref[count + i] != 0)
                for c in range(comps):
                    old[c] = old[c] + jnp.where(here, fresh_refs[2 * i][c, :, lanes], 0.0)
                    old[c] = old[c] + jnp.where(there, fresh_refs[2 * i + 1][c, :, lanes], 0.0)
            if last:
                tend = semi_implicit_slabs(old, tend, terms, hm)
            else:
                tend = [old[c] + time_step * tend[c] for c in range(comps)]
            for c in range(comps):
                out_ref[t, c, :, lanes] = tend[c]
            return carry

        lax.fori_loop(0, trajectories, body, 0)


def fourier_tables(pair_count, groups, truncation, longitudes):
    half_turn = longitudes // 2
    order = jnp.arange(pair_count + 1, dtype=jnp.int32)[None, :, None]
    column = jnp.arange(half_turn, dtype=jnp.int32)[None, None, :]
    quarter = jnp.arange(2, dtype=jnp.int32)[:, None, None] * (longitudes // 4)
    phase = (order * column + quarter) % longitudes
    angle = phase.astype(jnp.float32) * (2.0 * math.pi / longitudes)
    base = lax.optimization_barrier(jnp.cos(angle).astype(jnp.bfloat16))
    low = base[:, :pair_count]
    flip = (1 - 2 * (column % 2)) * (1 - 2 * jnp.arange(2, dtype=jnp.int32)[:, None, None])
    high = base[:, 1:] * flip.astype(jnp.bfloat16)
    pair = jnp.arange(pair_count, dtype=jnp.int32)[None, :, None]
    low_sign = (1 - 2 * (pair % 2)).astype(jnp.bfloat16)
    high_sign = (1 - 2 * ((truncation - 1 - pair) % 2)).astype(jnp.bfloat16)
    low = jnp.concatenate([low, low * low_sign], axis=2)
    high = jnp.concatenate([high, high * high_sign], axis=2)
    table = jnp.stack([low, high], axis=1)
    table = table.reshape(2, 2, groups, pair_count // groups, longitudes)
    return jnp.transpose(table, (2, 0, 1, 3, 4)).reshape(4 * pair_count, longitudes)


def far_members(members):
    return [(a, b) for a in range(members) for b in range(a + 1, members) if a ^ b != 1]


def pick_kernel(clones_ref, spec_ref, row_ref, slot_ref, *route_refs, local):
    row_ref[...] = spec_ref[...].astype(jnp.bfloat16)
    members, member = lax.axis_size("member"), lax.axis_index("member")
    for i, route_ref in enumerate(route_refs):
        source = lax.div(clones_ref[i, 1], local)
        target = lax.div(clones_ref[i, 0], local)
        route = jnp.where(source == target, 0, 1)
        low, high = jnp.minimum(source, target), jnp.maximum(source, target)
        for k, (a, b) in enumerate(far_members(members)):
            route = jnp.where(jnp.logical_and(low == a, high == b), 2 + k, route)
        route_ref[0] = route
        slot_ref[i] = jnp.where(target == member, clones_ref[i, 0] - target * local, -1)
        slot_ref[len(route_refs) + i] = jnp.bitwise_and(
            jnp.bitwise_xor(source, member), members // 2
        )


def pick_clones(spectra, clones):
    local, comps, pairs, row_length = spectra.shape
    count = clones.shape[0]
    smem = pl.BlockSpec(memory_space=pltpu.SMEM)
    block = (1, comps, pairs, row_length)
    got = pl.pallas_call(
        functools.partial(pick_kernel, local=local),
        out_shape=[
            jax.ShapeDtypeStruct((count,) + block[1:], jnp.bfloat16),
            jax.ShapeDtypeStruct((2 * count,), jnp.int32),
        ]
        + [jax.ShapeDtypeStruct((1,), jnp.int32)] * count,
        grid_spec=pltpu.PrefetchScalarGridSpec(
            num_scalar_prefetch=1,
            grid=(count,),
            in_specs=[pl.BlockSpec(block, lambda i, c: (lax.rem(c[i, 1], local), 0, 0, 0))],
            out_specs=[pl.BlockSpec(block, lambda i, c: (i, 0, 0, 0))] + [smem] * (1 + count),
        ),
        cost_estimate=pl.CostEstimate(
            flops=0, bytes_accessed=6 * 1024 * 1024, transcendentals=0
        ),
        name="pick",
    )(clones, spectra)
    return got[0], got[1], [r.reshape(()) for r in got[2:]]


def choose_kernel(clones_ref, *refs, local, slots, direct):
    in_refs, out_refs = refs[:slots], refs[slots:]
    for i, out_ref in enumerate(out_refs):
        t = lax.rem(clones_ref[i, 1], local)
        for n in range(slots):
            place = slot_place(n, direct)

            @pl.when(lax.div(place, 2) == t)
            def _():
                out_ref[lax.rem(place, 2)] = in_refs[n][...]


def choose_rows(parts, clones, local, direct):
    vmem = pl.BlockSpec(memory_space=pltpu.VMEM)
    return pl.pallas_call(
        functools.partial(choose_kernel, local=local, slots=len(parts), direct=direct),
        out_shape=[jax.ShapeDtypeStruct((2,) + parts[0].shape, parts[0].dtype)] * clones.shape[0],
        in_specs=[pl.BlockSpec(memory_space=pltpu.SMEM)] + [vmem] * len(parts),
        out_specs=[vmem] * clones.shape[0],
        cost_estimate=pl.CostEstimate(
            flops=0, bytes_accessed=4 * 1024 * 1024, transcendentals=0
        ),
        name="choose",
    )(clones, *parts)


def send_clone(row, route):
    members = lax.axis_size("member")

    def swap(pairs):
        both = pairs + [(b, a) for a, b in pairs]
        return lambda v: lax.ppermute(v, "member", both)

    branches = [lambda v: v, swap([(a, a + 1) for a in range(0, members, 2)])]
    branches += [swap([pair]) for pair in far_members(members)]
    return lax.switch(route, branches, row)


def share_row(row, owner):
    members = lax.axis_size("member")
    differs = jnp.bitwise_xor(owner, lax.axis_index("member").astype(jnp.int32))
    bit = 1
    while True:
        other = lax.ppermute(row, "member", [(m, m ^ bit) for m in range(members)])
        if 2 * bit >= members:
            return [row, other]
        row = jnp.where(jnp.bitwise_and(differs, bit) != 0, other, row)
        bit *= 2


def shards(spectra, legendre, sin_lat, gravity, stability, clones):
    trajectories, comps, pairs, row_length = spectra.shape
    truncation = row_length - 1
    half_lat = legendre.shape[2]
    longitudes = LONGITUDES_PER_WAVE * truncation
    space = lax.axis_size("space")
    position = lax.axis_index("space")
    fields = comps // 2
    split = space // (2 * trajectories)
    lane_count = LANES // split
    chunk_count = half_lat // LANES
    padded_pairs = -(-pairs // SUB) * SUB
    steps = padded_pairs // SUB
    tiles = -(-row_length // LANES)
    extra = padded_pairs - pairs
    rows = trajectories * comps

    count = clones.shape[0]
    slots = 2 * trajectories
    direct = split == 1
    state = spectra
    if extra:
        state = jnp.pad(state, ((0, 0), (0, 0), (0, extra), (0, 0)))
    order = jnp.arange(space, dtype=jnp.int32)
    if direct:
        order = jnp.bitwise_xor(position.astype(jnp.int32), order)
    columns = jnp.transpose(legendre, (1, 0, 2))
    if extra:
        columns = jnp.pad(columns, ((0, 0), (0, extra), (0, 0)))

    smem = pl.BlockSpec(memory_space=pltpu.SMEM)
    state_spec = pl.BlockSpec((trajectories, comps, SUB, row_length), lambda i: (0, 0, i, 0))
    fresh_spec = pl.BlockSpec((comps, SUB, row_length), lambda i: (0, i, 0))
    kept_spec = pl.BlockSpec((SUB, tiles * LANES, LANES), lambda i: (i, 0, 0))
    part_shape = (fields, 4 * padded_pairs, LANES)
    part_spec = pl.BlockSpec(part_shape, lambda i: (0, 0, 0))
    mend_spec = pl.BlockSpec((2,) + part_shape, lambda i: (0, 0, 0, 0))

    def leg_spec(k):
        return pl.BlockSpec((row_length, SUB, LANES), lambda i: (0, i, k))

    mib = 1024 * 1024

    def forward(k, made, span, clone_slot, patches):
        keep = k > 0
        kept_shape = jax.ShapeDtypeStruct((padded_pairs, tiles * LANES, LANES), jnp.bfloat16)
        return pl.pallas_call(
            functools.partial(
                forward_kernel, truncation=truncation, pairs=padded_pairs, keep=keep,
                real_pairs=pairs, count=len(patches), made=made, span=span, direct=direct,
            ),
            out_shape=[jax.ShapeDtypeStruct(part_shape, jnp.bfloat16)] * len(made)
            + [kept_shape] * keep,
            grid=(steps,),
            in_specs=[smem] * bool(patches)
            + [state_spec, leg_spec(k)]
            + [fresh_spec] * len(patches),
            out_specs=[part_spec] * len(made) + [kept_spec] * keep,
            scratch_shapes=[
                pltpu.VMEM((tiles * LANES * SUB, LANES), jnp.float32),
                pltpu.VMEM((tiles, span * comps * SUB, LANES), jnp.float32),
                pltpu.VMEM((4 * span * comps * padded_pairs, LANES), jnp.float32),
            ],
            compiler_params=pltpu.CompilerParams(vmem_limit_bytes=60 * mib),
            cost_estimate=pl.CostEstimate(
                flops=8 * span * comps * padded_pairs * row_length * LANES,
                bytes_accessed=16 * 1024 * 1024,
                transcendentals=0,
            ),
            name="forward",
        )(*([clone_slot] if patches else []), state, columns, *patches)

    def to_wire(x):
        if extra:
            x = x.reshape(slots, fields, 4, padded_pairs, LANES)[:, :, :, :pairs]
        x = x.reshape(slots, fields, 4 * pairs, split, lane_count)
        return jnp.transpose(x, (0, 3, 1, 2, 4)).reshape(space, fields, 4 * pairs, lane_count)

    def from_wire(x):
        x = x.reshape(slots, split, fields, 4, pairs, lane_count)
        x = jnp.transpose(x, (0, 2, 3, 4, 1, 5)).reshape(slots, fields, 4, pairs, LANES)
        if extra:
            x = jnp.pad(x, ((0, 0), (0, 0), (0, 0), (0, extra), (0, 0)))
        return x.reshape((slots,) + part_shape)

    def exchange(x):
        return lax.all_to_all(x, "space", split_axis=0, concat_axis=0, tiled=True)

    def swap(parts):
        got = list(parts)
        for n in reversed(range(1, space)):
            got[n] = lax.ppermute(parts[n], "space", [(d, d ^ n) for d in range(space)])
        return got

    def spread(parts):
        if direct:
            return swap(parts)
        x = exchange(to_wire(jnp.stack(parts)))
        x = jnp.pad(x, ((0, 0), (0, 0), (0, 0), (0, LANES - lane_count)))
        return [x[d] for d in range(space)]

    def collect(parts):
        if direct:
            return swap(parts)
        x = from_wire(exchange(jnp.stack(parts)[..., :lane_count]))
        return [x[n] for n in range(slots)]

    analysis = lax.optimization_barrier(
        fourier_tables(pairs * space, space, truncation, longitudes)
    )
    synthesis = analysis.T
    south = position // split % 2
    hemisphere = jnp.where(south == 0, sin_lat, -sin_lat)
    weights_all = math.pi * jnp.sqrt(1.0 - hemisphere * hemisphere) / (2 * half_lat)
    vmem = pl.BlockSpec(memory_space=pltpu.VMEM)
    modes = 4 * pairs * space

    def grid(k, parts):
        first = k * LANES + position % split * lane_count
        mu = lax.dynamic_slice_in_dim(hemisphere, first, lane_count)
        weight = lax.dynamic_slice_in_dim(weights_all, first, lane_count)
        short = LANES - lane_count
        if short:
            mu = jnp.pad(mu, (0, short))
            weight = jnp.pad(weight, (0, short))
        return pl.pallas_call(
            functools.partial(grid_kernel, scale=1.0 / truncation),
            out_shape=[jax.ShapeDtypeStruct(x.shape, jnp.bfloat16) for x in parts],
            in_specs=[smem] + [vmem] * (4 + space),
            out_specs=[vmem] * space,
            scratch_shapes=[
                pltpu.VMEM((modes, fields * LANES), jnp.bfloat16),
                pltpu.VMEM((longitudes, fields * LANES), jnp.bfloat16),
            ],
            compiler_params=pltpu.CompilerParams(vmem_limit_bytes=60 * mib),
            cost_estimate=pl.CostEstimate(
                flops=4 * modes * longitudes * fields * LANES,
                bytes_accessed=12 * 1024 * 1024,
                transcendentals=0,
            ),
            name="grid",
        )(order, (2.0 * mu)[None], weight[None], synthesis, analysis, *parts)

    def inverse(ws, legs, start, patches, mends, last):
        chunks = len(ws)
        stored = bool(mends)
        wide_scratch = pltpu.VMEM((chunks, tiles * LANES * SUB, LANES), jnp.float32)
        return pl.pallas_call(
            functools.partial(
                inverse_kernel,
                truncation=truncation,
                pairs=padded_pairs,
                chunks=chunks,
                last=last,
                stored=stored,
                slots=slots,
                count=count,
                patches=len(patches) // 2,
                real_pairs=pairs,
                direct=direct,
            ),
            out_shape=jax.ShapeDtypeStruct(state.shape, jnp.float32),
            grid=(steps,),
            in_specs=[smem] * 3
            + [part_spec] * (chunks * slots)
            + ([leg_spec(k) for k in range(chunks)] if stored else [kept_spec] * chunks)
            + [state_spec]
            + [fresh_spec] * len(patches)
            + [mend_spec] * len(mends),
            out_specs=state_spec,
            scratch_shapes=[
                pltpu.VMEM((chunks, 4 * rows * padded_pairs, LANES), jnp.float32),
                pltpu.VMEM((tiles, rows * SUB, LANES), jnp.float32),
            ]
            + ([wide_scratch] if stored else []),
            compiler_params=pltpu.CompilerParams(vmem_limit_bytes=60 * mib),
            cost_estimate=pl.CostEstimate(
                flops=8 * rows * padded_pairs * row_length * LANES * chunks,
                bytes_accessed=20 * 1024 * 1024,
                transcendentals=0,
            ),
            name="inverse",
        )(slot, gravity, stability, *[x for w in ws for x in w], *legs, start, *patches, *mends)

    everything = tuple(range(slots))
    halved = direct and trajectories % 2 == 0
    near, far = everything[: slots // 2], everything[slots // 2 :]
    if halved:
        first = list(forward(0, far, trajectories // 2, None, []))
        second = list(forward(0, near, trajectories // 2, None, []))
    else:
        first = list(forward(0, everything, trajectories, None, []))

    turn, first[0] = lax.optimization_barrier((clones, first[0]))
    made = [second + first if halved else first]
    picked, slot, route = pick_clones(spectra, turn)
    narrow = [send_clone(picked[i], route[i]) for i in range(count)]
    if extra:
        narrow = [jnp.pad(x, ((0, 0), (0, extra), (0, 0))) for x in narrow]
    turn = slot
    for k in range(1, chunk_count):
        made.append(list(forward(k, everything, trajectories, turn, narrow)))
        turn, made[k][0] = lax.optimization_barrier((slot, made[k][0]))
    later, made[-1][0] = lax.optimization_barrier((clones[:, 1], made[-1][0]))
    kept = [x[-1] for x in made[1:]]
    sent = []
    for x in made:
        sent.append(spread(x[:slots]))
    back = []
    for k in range(chunk_count):
        got = grid(k, sent[k])
        back.append(collect(got))
    fresh = [
        share_row(
            lax.dynamic_index_in_dim(spectra, lax.rem(later[i], trajectories), 0, keepdims=False),
            lax.div(later[i], trajectories),
        )
        for i in range(count)
    ]
    fresh = [x for pair in fresh for x in pair]
    if extra:
        fresh = [jnp.pad(x, ((0, 0), (0, extra), (0, 0))) for x in fresh]
    chosen = choose_rows(back[0], clones, trajectories, direct)
    mends = [send_clone(chosen[i], route[i]) for i in range(count)]
    start = inverse(back[:1], [columns], state, [], mends, False)
    for k in range(1, chunk_count - 1):
        start = inverse(back[k : k + 1], kept[k - 1 : k], start, fresh, [], False)
        fresh = []
    out = inverse(back[-1:], kept[-1:], start, fresh, [], True)
    return out[:, :, :pairs] if extra else out


def solution(mesh):
    placed = (P("member", None, "space", None), P("space", None, None), P(), P(), P(), P())
    return jax.shard_map(
        shards,
        mesh=mesh,
        in_specs=placed,
        out_specs=P("member", None, "space", None),
        check_vma=False,
    )
```

```python
import functools
import math

import jax
import jax.numpy as jnp
from jax import lax
from jax.experimental import pallas as pl
from jax.experimental.pallas import tpu as pltpu
from jax.sharding import PartitionSpec as P


LANES = 128
SUB = 8
PACKED = 16
UNROLL_FORWARD = 8
UNROLL_INVERSE = 8
LONGITUDES_PER_WAVE = 2

time_step = 0.25
wave_scale = 16.0
diffusion = 0.02


def layout_terms(first_pair, count, lane0, lanes, truncation):
    pair = first_pair + lax.broadcasted_iota(jnp.int32, (count, lanes), 0)
    column = lane0 + lax.broadcasted_iota(jnp.int32, (count, lanes), 1)
    leading = column < truncation - pair
    offset = jnp.where(leading, column, column - (truncation - pair))
    order = jnp.where(leading, pair, truncation - 1 - pair)
    return leading, (offset & 1) == 1, order + offset


def slot_place(n, direct):
    return jnp.bitwise_xor(lax.axis_index("space"), n) if direct else jnp.int32(n)


def forward_kernel(
    *refs, truncation, pairs, real_pairs, keep, count, made, span, direct
):
    if count:
        slot_ref, refs = refs[0], refs[1:]
    spec_ref, leg_ref, refs = refs[0], refs[1], refs[2:]
    step = pl.program_id(0)
    row_length = truncation + 1
    _, comps, block, _ = spec_ref.shape
    rows = span * comps
    fresh_refs, refs = refs[:count], refs[count:]
    out_refs, refs = refs[: len(made)], refs[len(made) :]
    if keep:
        keep_ref, refs = refs[0], refs[1:]
    wide, xs, res = refs
    tiles = xs.shape[0]
    padded = tiles * LANES
    first_place = lax.div(slot_place(made[0], direct), 2)
    t0 = lax.div(first_place, span) * span

    @pl.when(step == 0)
    def _():
        wide[row_length * block :, :] = jnp.zeros(
            (wide.shape[0] - row_length * block, LANES), jnp.float32
        )

    wide[: row_length * block, :] = (
        leg_ref[...].astype(jnp.float32).reshape(row_length * block, LANES)
    )
    for k in range(tiles):
        width = min(LANES, row_length - k * LANES)
        lanes = slice(k * LANES, k * LANES + width)
        if width < LANES:
            xs[k] = jnp.zeros((rows * block, LANES), jnp.float32)
        xs[k, :, :width] = spec_ref[pl.ds(t0, span), :, :, lanes].reshape(rows * block, width)

    for i in range(count):
        slot = slot_ref[i] - t0

        @pl.when(jnp.logical_and(slot >= 0, slot < span))
        def _():
            at = pl.multiple_of(slot * comps * block, SUB)
            for k in range(tiles):
                width = min(LANES, row_length - k * LANES)
                fresh = fresh_refs[i][:, :, k * LANES : k * LANES + width].astype(jnp.float32)
                xs[k, pl.ds(at, comps * block), :width] = fresh.reshape(comps * block, width)

    first_pair = lax.axis_index("space") * real_pairs + step * block

    def one(q, carry):
        x = jnp.concatenate(
            [xs[k, pl.ds(q, rows, stride=block), :] for k in range(tiles)], axis=1
        )
        edge = truncation - first_pair - q
        group = PACKED if rows % PACKED == 0 else SUB
        column = lax.broadcasted_iota(jnp.int32, (group, padded), 1)
        leading = column < edge
        odd = (jnp.where(leading, column, column - edge) & 1) == 1
        sign = jnp.where(odd, -1.0, 1.0)
        kind = jnp.bfloat16 if group == PACKED else jnp.float32
        factors = [
            jnp.where(leading, 1.0, 0.0),
            jnp.where(leading, 0.0, 1.0),
            jnp.where(leading, sign, 0.0),
            jnp.where(leading, 0.0, sign),
        ]
        x = x.astype(kind)
        lhs = []
        for factor in factors:
            factor = factor.astype(kind)
            for at in range(0, rows, group):
                lhs.append(x[at : at + group] * factor)
        lhs = jnp.concatenate(lhs, axis=0).astype(jnp.bfloat16)
        rhs = wide[pl.ds(q, padded, stride=block), :].astype(jnp.bfloat16)
        if keep:
            keep_ref[q] = rhs
        got = jnp.dot(lhs, rhs, preferred_element_type=jnp.float32)
        res[pl.ds(step * block + q, 4 * rows, stride=pairs), :] = got
        return carry

    lax.fori_loop(0, block, one, 0, unroll=UNROLL_FORWARD)

    @pl.when(step == pl.num_programs(0) - 1)
    def _():
        for n, slot in enumerate(made):
            place = slot_place(slot, direct)
            t, s = lax.div(place, 2) - t0, lax.rem(place, 2)
            base = pl.multiple_of((s * (2 * rows) + t * comps) * pairs, SUB)
            for f in range(comps // 2):
                parts = []
                for r in range(2):
                    for h in range(2):
                        parts.append(res[pl.ds(base + (h * rows + 2 * f + r) * pairs, pairs), :])
                out_refs[n][f] = jnp.concatenate(parts, axis=0).astype(jnp.bfloat16)


def grid_kernel(order_ref, cor_ref, weight_ref, syn_ref, ana_ref, *refs, scale):
    sources = order_ref.shape[0]
    in_refs, out_refs, (modes, force) = refs[:sources], refs[sources:-2], refs[-2:]
    fields, rows, lanes = in_refs[0].shape
    longitudes = syn_ref.shape[0]
    for n in range(sources):
        at = pl.multiple_of(order_ref[n] * rows, 16)
        for f in range(fields):
            modes[pl.ds(at, rows), f * lanes : (f + 1) * lanes] = in_refs[n][f]
    cor = cor_ref[...]
    weight = weight_ref[...]
    span = 128

    def synth(b, carry):
        at = pl.multiple_of(b * span, span)
        g = (
            jnp.dot(syn_ref[pl.ds(at, span), :], modes[...], preferred_element_type=jnp.float32)
            * scale
        )
        field = [g[:, f * lanes : (f + 1) * lanes] for f in range(fields)]
        mean = 0.5 * (field[4] + field[5])
        out = [None] * fields
        for a in range(2):
            spin = field[a] + cor
            div = field[2 + a]
            out[a] = -spin * div
            out[2 + a] = spin * field[a] - 0.5 * div * div
            out[4 + a] = -(field[4 + a] + mean) * div
        for f in range(fields):
            force[pl.ds(at, span), f * lanes : (f + 1) * lanes] = out[f].astype(jnp.bfloat16)
        return carry

    lax.fori_loop(0, longitudes // span, synth, 0)

    def analyse(d, carry):
        at = pl.multiple_of(d * rows, 16)
        w = jnp.dot(ana_ref[pl.ds(at, rows), :], force[...], preferred_element_type=jnp.float32)
        for f in range(fields):
            lane = slice(f * lanes, (f + 1) * lanes)
            modes[pl.ds(at, rows), lane] = (w[:, lane] * weight).astype(jnp.bfloat16)
        return carry

    lax.fori_loop(0, sources, analyse, 0)
    for n in range(sources):
        at = pl.multiple_of(order_ref[n] * rows, 16)
        for f in range(fields):
            out_refs[n][f] = modes[pl.ds(at, rows), f * lanes : (f + 1) * lanes]


def step_terms(degree, gm, hm, truncation):
    eig = wave_scale * (degree * (degree + 1)).astype(jnp.float32) / float(truncation * truncation)
    damping = 1.0 / (1.0 + diffusion * eig * eig)
    coupling = time_step * time_step * eig
    pm = [[gm[a][0] * hm[0][b] + gm[a][1] * hm[1][b] for b in range(2)] for a in range(2)]
    diag = [1.0 + coupling * pm[a][a] for a in range(2)]
    cross = [coupling * pm[0][1], coupling * pm[1][0]]
    inverse = 1.0 / (diag[0] * diag[1] - cross[0] * cross[1])
    solve = [
        [diag[1] * inverse, -cross[0] * inverse],
        [-cross[1] * inverse, diag[0] * inverse],
    ]
    push = [[time_step * eig * gm[a][b] for b in range(2)] for a in range(2)]
    return damping, solve, push


def semi_implicit_slabs(old, tend, terms, hm):
    damping, solve, push = terms
    out = [None] * 12
    for r in range(2):
        star = [old[c * 2 + r] + time_step * tend[c * 2 + r] for c in range(6)]
        right = [star[2 + a] + push[a][0] * star[4] + push[a][1] * star[5] for a in range(2)]
        div = [solve[a][0] * right[0] + solve[a][1] * right[1] for a in range(2)]
        for a in range(2):
            heat = (time_step * hm[a][0]) * div[0] + (time_step * hm[a][1]) * div[1]
            out[a * 2 + r] = damping * star[a]
            out[(2 + a) * 2 + r] = damping * div[a]
            out[(4 + a) * 2 + r] = damping * (star[4 + a] - heat)
    return out


def inverse_kernel(
    slot_ref,
    gravity_ref,
    stability_ref,
    *refs,
    truncation,
    pairs,
    real_pairs,
    chunks,
    last,
    stored,
    made,
    count,
    patches,
    direct,
    prior=False,
):
    slots = len(made)
    w_refs, refs = refs[: chunks * slots], refs[chunks * slots :]
    leg_refs, refs = refs[:chunks], refs[chunks:]
    spec_ref, refs = refs[0], refs[1:]
    if prior:
        refs = refs[1:]
    mended = count if stored else 0
    fresh_refs, refs = refs[: 2 * patches], refs[2 * patches :]
    mend_refs, refs = refs[:mended], refs[mended:]
    out_ref, ws, ten = refs[:3]
    if stored:
        wide = refs[3]
    step = pl.program_id(0)
    row_length = truncation + 1
    trajectories, comps, block, _ = out_ref.shape
    rows = trajectories * comps
    tiles = ten.shape[0]
    padded = tiles * LANES
    t0 = lax.div(lax.div(slot_place(made[0], direct), 2), trajectories) * trajectories

    @pl.when(step == 0)
    def _():
        if stored:
            for k in range(chunks):
                wide[k, row_length * block :, :] = jnp.zeros(
                    (wide.shape[1] - row_length * block, LANES), jnp.float32
                )

        def fill(k, t, s, source):
            base = pl.multiple_of((s * (2 * rows) + t * comps) * pairs, SUB)
            for f in range(comps // 2):
                got = source(f).astype(jnp.float32)
                for r in range(2):
                    for h in range(2):
                        at = (r * 2 + h) * pairs
                        ws[k, pl.ds(base + (h * rows + 2 * f + r) * pairs, pairs), :] = got[
                            at : at + pairs, :
                        ]

        for k in range(chunks):
            for n, slot in enumerate(made):
                place = slot_place(slot, direct)
                t = lax.div(place, 2) - t0
                fill(k, t, lax.rem(place, 2), lambda f: w_refs[k * slots + n][f])
        for i in range(mended):

            @pl.when(slot_ref[i] >= 0)
            def _():
                for s in range(2):
                    fill(0, slot_ref[i], s, lambda f: mend_refs[i][s, f])

    if stored:
        for k in range(chunks):
            wide[k, : row_length * block, :] = (
                leg_refs[k][...].astype(jnp.float32).reshape(row_length * block, LANES)
            )
    first_pair = lax.axis_index("space") * real_pairs + step * block

    def one(q, carry):
        at = pl.ds(step * block + q, 4 * rows, stride=pairs)
        lhs = jnp.concatenate([ws[k, at, :].astype(jnp.bfloat16) for k in range(chunks)], axis=1)
        if not stored:
            rhs = jnp.concatenate([leg_refs[k][q] for k in range(chunks)], axis=1)
        else:
            at = pl.ds(q, padded, stride=block)
            rhs = jnp.concatenate(
                [wide[k, at, :].astype(jnp.bfloat16) for k in range(chunks)], axis=1
            )
        got = lax.dot_general(
            lhs, rhs, (((1,), (1,)), ((), ())), preferred_element_type=jnp.float32
        )
        leading, odd, _ = layout_terms(first_pair + q, 1, 0, padded, truncation)
        north = jnp.where(leading, got[:rows], got[rows : 2 * rows])
        south = jnp.where(leading, got[2 * rows : 3 * rows], got[3 * rows :])
        total = north + jnp.where(odd, -south, south)
        for k in range(tiles):
            ten[k, pl.ds(q, rows, stride=block), :] = total[:, k * LANES : (k + 1) * LANES]
        return carry

    lax.fori_loop(0, block, one, 0, unroll=UNROLL_INVERSE)

    if last:
        gm = [[gravity_ref[a, b] for b in range(2)] for a in range(2)]
        hm = [[stability_ref[a, b] for b in range(2)] for a in range(2)]
    for k in range(tiles):
        width = min(LANES, row_length - k * LANES)
        lanes = slice(k * LANES, k * LANES + width)
        if last:
            _, _, degree = layout_terms(first_pair, block, k * LANES, width, truncation)
            terms = step_terms(degree, gm, hm, truncation)

        def body(t, carry):
            tend = []
            for c in range(comps):
                at = pl.multiple_of((t * comps + c) * block, SUB)
                value = ten[k, pl.ds(at, block), :][:, :width]
                tend.append(value)
            old = [spec_ref[t, c, :, lanes] for c in range(comps)]
            for i in range(mended):
                mine = slot_ref[i] == t
                old = [jnp.where(mine, 0.0, old[c]) for c in range(comps)]
            for i in range(patches):
                here = jnp.logical_and(slot_ref[i] == t, slot_ref[count + i] == 0)
                there = jnp.logical_and(slot_ref[i] == t, slot_ref[count + i] != 0)
                for c in range(comps):
                    old[c] = old[c] + jnp.where(here, fresh_refs[2 * i][c, :, lanes], 0.0)
                    old[c] = old[c] + jnp.where(there, fresh_refs[2 * i + 1][c, :, lanes], 0.0)
            if last:
                tend = semi_implicit_slabs(old, tend, terms, hm)
            else:
                tend = [old[c] + time_step * tend[c] for c in range(comps)]
            for c in range(comps):
                out_ref[t, c, :, lanes] = tend[c]
            return carry

        lax.fori_loop(0, trajectories, body, 0)


def fourier_tables(pair_count, groups, truncation, longitudes):
    half_turn = longitudes // 2
    order = jnp.arange(pair_count + 1, dtype=jnp.int32)[None, :, None]
    column = jnp.arange(half_turn, dtype=jnp.int32)[None, None, :]
    quarter = jnp.arange(2, dtype=jnp.int32)[:, None, None] * (longitudes // 4)
    phase = (order * column + quarter) % longitudes
    angle = phase.astype(jnp.float32) * (2.0 * math.pi / longitudes)
    base = lax.optimization_barrier(jnp.cos(angle).astype(jnp.bfloat16))
    low = base[:, :pair_count]
    flip = (1 - 2 * (column % 2)) * (1 - 2 * jnp.arange(2, dtype=jnp.int32)[:, None, None])
    high = base[:, 1:] * flip.astype(jnp.bfloat16)
    pair = jnp.arange(pair_count, dtype=jnp.int32)[None, :, None]
    low_sign = (1 - 2 * (pair % 2)).astype(jnp.bfloat16)
    high_sign = (1 - 2 * ((truncation - 1 - pair) % 2)).astype(jnp.bfloat16)
    low = jnp.concatenate([low, low * low_sign], axis=2)
    high = jnp.concatenate([high, high * high_sign], axis=2)
    table = jnp.stack([low, high], axis=1)
    table = table.reshape(2, 2, groups, pair_count // groups, longitudes)
    return jnp.transpose(table, (2, 0, 1, 3, 4)).reshape(4 * pair_count, longitudes)


def far_members(members):
    return [(a, b) for a in range(members) for b in range(a + 1, members) if a ^ b != 1]


def pick_kernel(clones_ref, spec_ref, row_ref, slot_ref, *route_refs, local):
    row_ref[...] = spec_ref[...].astype(jnp.bfloat16)
    members, member = lax.axis_size("member"), lax.axis_index("member")
    for i, route_ref in enumerate(route_refs):
        source = lax.div(clones_ref[i, 1], local)
        target = lax.div(clones_ref[i, 0], local)
        route = jnp.where(source == target, 0, 1)
        low, high = jnp.minimum(source, target), jnp.maximum(source, target)
        for k, (a, b) in enumerate(far_members(members)):
            route = jnp.where(jnp.logical_and(low == a, high == b), 2 + k, route)
        route_ref[0] = route
        slot_ref[i] = jnp.where(target == member, clones_ref[i, 0] - target * local, -1)
        slot_ref[len(route_refs) + i] = jnp.bitwise_and(
            jnp.bitwise_xor(source, member), members // 2
        )


def pick_clones(spectra, clones):
    local, comps, pairs, row_length = spectra.shape
    count = clones.shape[0]
    smem = pl.BlockSpec(memory_space=pltpu.SMEM)
    block = (1, comps, pairs, row_length)
    got = pl.pallas_call(
        functools.partial(pick_kernel, local=local),
        out_shape=[
            jax.ShapeDtypeStruct((count,) + block[1:], jnp.bfloat16),
            jax.ShapeDtypeStruct((2 * count,), jnp.int32),
        ]
        + [jax.ShapeDtypeStruct((1,), jnp.int32)] * count,
        grid_spec=pltpu.PrefetchScalarGridSpec(
            num_scalar_prefetch=1,
            grid=(count,),
            in_specs=[pl.BlockSpec(block, lambda i, c: (lax.rem(c[i, 1], local), 0, 0, 0))],
            out_specs=[pl.BlockSpec(block, lambda i, c: (i, 0, 0, 0))] + [smem] * (1 + count),
        ),
        cost_estimate=pl.CostEstimate(
            flops=0, bytes_accessed=6 * 1024 * 1024, transcendentals=0
        ),
        name="pick",
    )(clones, spectra)
    return got[0], got[1], [r.reshape(()) for r in got[2:]]


def choose_kernel(clones_ref, *refs, local, slots, direct):
    in_refs, out_refs = refs[:slots], refs[slots:]
    for i, out_ref in enumerate(out_refs):
        t = lax.rem(clones_ref[i, 1], local)
        for n in range(slots):
            place = slot_place(n, direct)

            @pl.when(lax.div(place, 2) == t)
            def _():
                out_ref[lax.rem(place, 2)] = in_refs[n][...]


def choose_rows(parts, clones, local, direct):
    vmem = pl.BlockSpec(memory_space=pltpu.VMEM)
    return pl.pallas_call(
        functools.partial(choose_kernel, local=local, slots=len(parts), direct=direct),
        out_shape=[jax.ShapeDtypeStruct((2,) + parts[0].shape, parts[0].dtype)] * clones.shape[0],
        in_specs=[pl.BlockSpec(memory_space=pltpu.SMEM)] + [vmem] * len(parts),
        out_specs=[vmem] * clones.shape[0],
        cost_estimate=pl.CostEstimate(
            flops=0, bytes_accessed=4 * 1024 * 1024, transcendentals=0
        ),
        name="choose",
    )(clones, *parts)


def send_clone(row, route):
    members = lax.axis_size("member")

    def swap(pairs):
        both = pairs + [(b, a) for a, b in pairs]
        return lambda v: lax.ppermute(v, "member", both)

    branches = [lambda v: v, swap([(a, a + 1) for a in range(0, members, 2)])]
    branches += [swap([pair]) for pair in far_members(members)]
    return lax.switch(route, branches, row)


def share_row(row, owner):
    members = lax.axis_size("member")
    differs = jnp.bitwise_xor(owner, lax.axis_index("member").astype(jnp.int32))
    bit = 1
    while True:
        other = lax.ppermute(row, "member", [(m, m ^ bit) for m in range(members)])
        if 2 * bit >= members:
            return [row, other]
        row = jnp.where(jnp.bitwise_and(differs, bit) != 0, other, row)
        bit *= 2


def shards(spectra, legendre, sin_lat, gravity, stability, clones):
    trajectories, comps, pairs, row_length = spectra.shape
    truncation = row_length - 1
    half_lat = legendre.shape[2]
    longitudes = LONGITUDES_PER_WAVE * truncation
    space = lax.axis_size("space")
    position = lax.axis_index("space")
    fields = comps // 2
    split = space // (2 * trajectories)
    lane_count = LANES // split
    chunk_count = half_lat // LANES
    padded_pairs = -(-pairs // SUB) * SUB
    steps = padded_pairs // SUB
    tiles = -(-row_length // LANES)
    extra = padded_pairs - pairs
    rows = trajectories * comps

    count = clones.shape[0]
    slots = 2 * trajectories
    direct = split == 1
    state = spectra
    if extra:
        state = jnp.pad(state, ((0, 0), (0, 0), (0, extra), (0, 0)))
    order = jnp.arange(space, dtype=jnp.int32)
    if direct:
        order = jnp.bitwise_xor(position.astype(jnp.int32), order)
    columns = jnp.transpose(legendre, (1, 0, 2))
    if extra:
        columns = jnp.pad(columns, ((0, 0), (0, extra), (0, 0)))

    smem = pl.BlockSpec(memory_space=pltpu.SMEM)
    state_spec = pl.BlockSpec((trajectories, comps, SUB, row_length), lambda i: (0, 0, i, 0))
    fresh_spec = pl.BlockSpec((comps, SUB, row_length), lambda i: (0, i, 0))
    kept_spec = pl.BlockSpec((SUB, tiles * LANES, LANES), lambda i: (i, 0, 0))
    part_shape = (fields, 4 * padded_pairs, LANES)
    part_spec = pl.BlockSpec(part_shape, lambda i: (0, 0, 0))
    mend_spec = pl.BlockSpec((2,) + part_shape, lambda i: (0, 0, 0, 0))

    def leg_spec(k):
        return pl.BlockSpec((row_length, SUB, LANES), lambda i: (0, i, k))

    mib = 1024 * 1024

    def forward(k, made, span, clone_slot, patches):
        keep = k > 0
        kept_shape = jax.ShapeDtypeStruct((padded_pairs, tiles * LANES, LANES), jnp.bfloat16)
        return pl.pallas_call(
            functools.partial(
                forward_kernel, truncation=truncation, pairs=padded_pairs, keep=keep,
                real_pairs=pairs, count=len(patches), made=made, span=span, direct=direct,
            ),
            out_shape=[jax.ShapeDtypeStruct(part_shape, jnp.bfloat16)] * len(made)
            + [kept_shape] * keep,
            grid=(steps,),
            in_specs=[smem] * bool(patches)
            + [state_spec, leg_spec(k)]
            + [fresh_spec] * len(patches),
            out_specs=[part_spec] * len(made) + [kept_spec] * keep,
            scratch_shapes=[
                pltpu.VMEM((tiles * LANES * SUB, LANES), jnp.float32),
                pltpu.VMEM((tiles, span * comps * SUB, LANES), jnp.float32),
                pltpu.VMEM((4 * span * comps * padded_pairs, LANES), jnp.float32),
            ],
            compiler_params=pltpu.CompilerParams(vmem_limit_bytes=60 * mib),
            cost_estimate=pl.CostEstimate(
                flops=8 * span * comps * padded_pairs * row_length * LANES,
                bytes_accessed=16 * 1024 * 1024,
                transcendentals=0,
            ),
            name="forward",
        )(*([clone_slot] if patches else []), state, columns, *patches)

    def to_wire(x):
        if extra:
            x = x.reshape(slots, fields, 4, padded_pairs, LANES)[:, :, :, :pairs]
        x = x.reshape(slots, fields, 4 * pairs, split, lane_count)
        return jnp.transpose(x, (0, 3, 1, 2, 4)).reshape(space, fields, 4 * pairs, lane_count)

    def from_wire(x):
        x = x.reshape(slots, split, fields, 4, pairs, lane_count)
        x = jnp.transpose(x, (0, 2, 3, 4, 1, 5)).reshape(slots, fields, 4, pairs, LANES)
        if extra:
            x = jnp.pad(x, ((0, 0), (0, 0), (0, 0), (0, extra), (0, 0)))
        return x.reshape((slots,) + part_shape)

    def exchange(x):
        return lax.all_to_all(x, "space", split_axis=0, concat_axis=0, tiled=True)

    def swap(parts):
        got = list(parts)
        for n in reversed(range(1, space)):
            got[n] = lax.ppermute(parts[n], "space", [(d, d ^ n) for d in range(space)])
        return got

    def spread(parts):
        if direct:
            return swap(parts)
        x = exchange(to_wire(jnp.stack(parts)))
        x = jnp.pad(x, ((0, 0), (0, 0), (0, 0), (0, LANES - lane_count)))
        return [x[d] for d in range(space)]

    def collect(parts):
        if direct:
            return swap(parts)
        x = from_wire(exchange(jnp.stack(parts)[..., :lane_count]))
        return [x[n] for n in range(slots)]

    analysis = lax.optimization_barrier(
        fourier_tables(pairs * space, space, truncation, longitudes)
    )
    synthesis = analysis.T
    south = position // split % 2
    hemisphere = jnp.where(south == 0, sin_lat, -sin_lat)
    weights_all = math.pi * jnp.sqrt(1.0 - hemisphere * hemisphere) / (2 * half_lat)
    vmem = pl.BlockSpec(memory_space=pltpu.VMEM)
    modes = 4 * pairs * space

    def grid(k, parts):
        first = k * LANES + position % split * lane_count
        mu = lax.dynamic_slice_in_dim(hemisphere, first, lane_count)
        weight = lax.dynamic_slice_in_dim(weights_all, first, lane_count)
        short = LANES - lane_count
        if short:
            mu = jnp.pad(mu, (0, short))
            weight = jnp.pad(weight, (0, short))
        return pl.pallas_call(
            functools.partial(grid_kernel, scale=1.0 / truncation),
            out_shape=[jax.ShapeDtypeStruct(x.shape, jnp.bfloat16) for x in parts],
            in_specs=[smem] + [vmem] * (4 + space),
            out_specs=[vmem] * space,
            scratch_shapes=[
                pltpu.VMEM((modes, fields * LANES), jnp.bfloat16),
                pltpu.VMEM((longitudes, fields * LANES), jnp.bfloat16),
            ],
            compiler_params=pltpu.CompilerParams(vmem_limit_bytes=60 * mib),
            cost_estimate=pl.CostEstimate(
                flops=4 * modes * longitudes * fields * LANES,
                bytes_accessed=12 * 1024 * 1024,
                transcendentals=0,
            ),
            name="grid",
        )(order, (2.0 * mu)[None], weight[None], synthesis, analysis, *parts)

    everything = tuple(range(slots))

    def finish(parts, leg, start, made, group, prior):
        span = trajectories // 2
        some_spec = pl.BlockSpec((span, comps, SUB, row_length), lambda i, g: (g[0], 0, i, 0))
        kernel = functools.partial(
            inverse_kernel,
            truncation=truncation,
            pairs=padded_pairs,
            chunks=1,
            last=True,
            stored=False,
            made=made,
            count=count,
            patches=0,
            real_pairs=pairs,
            direct=direct,
            prior=bool(prior),
        )
        return pl.pallas_call(
            lambda group_ref, *refs: kernel(*refs),
            out_shape=jax.ShapeDtypeStruct(state.shape, jnp.float32),
            grid_spec=pltpu.PrefetchScalarGridSpec(
                num_scalar_prefetch=1,
                grid=(steps,),
                in_specs=[smem] * 3
                + [pl.BlockSpec(part_shape, lambda i, g: (0, 0, 0))] * len(made)
                + [pl.BlockSpec((SUB, tiles * LANES, LANES), lambda i, g: (i, 0, 0)), some_spec]
                + [pl.BlockSpec(memory_space=pl.ANY)] * len(prior),
                out_specs=some_spec,
                scratch_shapes=[
                    pltpu.VMEM((1, 4 * span * comps * padded_pairs, LANES), jnp.float32),
                    pltpu.VMEM((tiles, span * comps * SUB, LANES), jnp.float32),
                ],
            ),
            input_output_aliases={6 + len(made): 0} if prior else {},
            compiler_params=pltpu.CompilerParams(vmem_limit_bytes=60 * mib),
            cost_estimate=pl.CostEstimate(
                flops=8 * span * comps * padded_pairs * row_length * LANES,
                bytes_accessed=16 * mib,
                transcendentals=0,
            ),
            name="finish",
        )(group, slot, gravity, stability, *[parts[n] for n in made], leg, start, *prior)

    def inverse(ws, legs, start, patches, mends, last):
        chunks = len(ws)
        stored = bool(mends)
        wide_scratch = pltpu.VMEM((chunks, tiles * LANES * SUB, LANES), jnp.float32)
        return pl.pallas_call(
            functools.partial(
                inverse_kernel,
                truncation=truncation,
                pairs=padded_pairs,
                chunks=chunks,
                last=last,
                stored=stored,
                made=everything,
                count=count,
                patches=len(patches) // 2,
                real_pairs=pairs,
                direct=direct,
            ),
            out_shape=jax.ShapeDtypeStruct(state.shape, jnp.float32),
            grid=(steps,),
            in_specs=[smem] * 3
            + [part_spec] * (chunks * slots)
            + ([leg_spec(k) for k in range(chunks)] if stored else [kept_spec] * chunks)
            + [state_spec]
            + [fresh_spec] * len(patches)
            + [mend_spec] * len(mends),
            out_specs=state_spec,
            scratch_shapes=[
                pltpu.VMEM((chunks, 4 * rows * padded_pairs, LANES), jnp.float32),
                pltpu.VMEM((tiles, rows * SUB, LANES), jnp.float32),
            ]
            + ([wide_scratch] if stored else []),
            compiler_params=pltpu.CompilerParams(vmem_limit_bytes=60 * mib),
            cost_estimate=pl.CostEstimate(
                flops=8 * rows * padded_pairs * row_length * LANES * chunks,
                bytes_accessed=20 * 1024 * 1024,
                transcendentals=0,
            ),
            name="inverse",
        )(slot, gravity, stability, *[x for w in ws for x in w], *legs, start, *patches, *mends)

    halved = direct and trajectories % 2 == 0
    near, far = everything[: slots // 2], everything[slots // 2 :]
    if halved:
        first = list(forward(0, far, trajectories // 2, None, []))
        second = list(forward(0, near, trajectories // 2, None, []))
    else:
        first = list(forward(0, everything, trajectories, None, []))

    turn, first[0] = lax.optimization_barrier((clones, first[0]))
    made = [second + first if halved else first]
    picked, slot, route = pick_clones(spectra, turn)
    narrow = [send_clone(picked[i], route[i]) for i in range(count)]
    if extra:
        narrow = [jnp.pad(x, ((0, 0), (0, extra), (0, 0))) for x in narrow]
    turn = slot
    for k in range(1, chunk_count):
        made.append(list(forward(k, everything, trajectories, turn, narrow)))
        turn, made[k][0] = lax.optimization_barrier((slot, made[k][0]))
    later, made[-1][0] = lax.optimization_barrier((clones[:, 1], made[-1][0]))
    kept = [x[-1] for x in made[1:]]
    sent = []
    for x in made:
        sent.append(spread(x[:slots]))
    back = []
    for k in range(chunk_count):
        got = grid(k, sent[k])
        back.append(collect(got))
    fresh = [
        share_row(
            lax.dynamic_index_in_dim(spectra, lax.rem(later[i], trajectories), 0, keepdims=False),
            lax.div(later[i], trajectories),
        )
        for i in range(count)
    ]
    fresh = [x for pair in fresh for x in pair]
    if extra:
        fresh = [jnp.pad(x, ((0, 0), (0, extra), (0, 0))) for x in fresh]
    chosen = choose_rows(back[0], clones, trajectories, direct)
    mends = [send_clone(chosen[i], route[i]) for i in range(count)]
    start = inverse(back[:1], [columns], state, [], mends, False)
    for k in range(1, chunk_count - 1):
        start = inverse(back[k : k + 1], kept[k - 1 : k], start, fresh, [], False)
        fresh = []
    if halved:
        side = lax.div(position.astype(jnp.int32), space // 2).reshape(1)
        out = finish(back[-1], kept[-1], start, far, 1 - side, [])
        out = finish(back[-1], kept[-1], start, near, side, [out])
    else:
        out = inverse(back[-1:], kept[-1:], start, fresh, [], True)
    return out[:, :, :pairs] if extra else out


def solution(mesh):
    placed = (P("member", None, "space", None), P("space", None, None), P(), P(), P(), P())
    return jax.shard_map(
        shards,
        mesh=mesh,
        in_specs=placed,
        out_specs=P("member", None, "space", None),
        check_vma=False,
    )
```

```python
import functools
import math

import jax
import jax.numpy as jnp
from jax import lax
from jax.experimental import pallas as pl
from jax.experimental.pallas import tpu as pltpu
from jax.sharding import PartitionSpec as P


LANES = 128
SUB = 8
PACKED = 16
UNROLL_FORWARD = 8
UNROLL_INVERSE = 8
LONGITUDES_PER_WAVE = 2

time_step = 0.25
wave_scale = 16.0
diffusion = 0.02


def layout_terms(first_pair, count, lane0, lanes, truncation):
    pair = first_pair + lax.broadcasted_iota(jnp.int32, (count, lanes), 0)
    column = lane0 + lax.broadcasted_iota(jnp.int32, (count, lanes), 1)
    leading = column < truncation - pair
    offset = jnp.where(leading, column, column - (truncation - pair))
    order = jnp.where(leading, pair, truncation - 1 - pair)
    return leading, (offset & 1) == 1, order + offset


def slot_place(n, direct):
    return jnp.bitwise_xor(lax.axis_index("space"), n) if direct else jnp.int32(n)


def forward_kernel(
    *refs, truncation, pairs, real_pairs, keep, count, made, span, direct
):
    if count:
        slot_ref, refs = refs[0], refs[1:]
    spec_ref, leg_ref, refs = refs[0], refs[1], refs[2:]
    step = pl.program_id(0)
    row_length = truncation + 1
    _, comps, block, _ = spec_ref.shape
    rows = span * comps
    fresh_refs, refs = refs[:count], refs[count:]
    out_refs, refs = refs[: len(made)], refs[len(made) :]
    if keep:
        keep_ref, refs = refs[0], refs[1:]
    wide, xs, res = refs
    tiles = xs.shape[0]
    padded = tiles * LANES
    first_place = lax.div(slot_place(made[0], direct), 2)
    t0 = lax.div(first_place, span) * span

    @pl.when(step == 0)
    def _():
        wide[row_length * block :, :] = jnp.zeros(
            (wide.shape[0] - row_length * block, LANES), jnp.float32
        )

    wide[: row_length * block, :] = (
        leg_ref[...].astype(jnp.float32).reshape(row_length * block, LANES)
    )
    for k in range(tiles):
        width = min(LANES, row_length - k * LANES)
        lanes = slice(k * LANES, k * LANES + width)
        if width < LANES:
            xs[k] = jnp.zeros((rows * block, LANES), jnp.float32)
        xs[k, :, :width] = spec_ref[pl.ds(t0, span), :, :, lanes].reshape(rows * block, width)

    for i in range(count):
        slot = slot_ref[i] - t0

        @pl.when(jnp.logical_and(slot >= 0, slot < span))
        def _():
            at = pl.multiple_of(slot * comps * block, SUB)
            for k in range(tiles):
                width = min(LANES, row_length - k * LANES)
                fresh = fresh_refs[i][:, :, k * LANES : k * LANES + width].astype(jnp.float32)
                xs[k, pl.ds(at, comps * block), :width] = fresh.reshape(comps * block, width)

    first_pair = lax.axis_index("space") * real_pairs + step * block

    def one(q, carry):
        x = jnp.concatenate(
            [xs[k, pl.ds(q, rows, stride=block), :] for k in range(tiles)], axis=1
        )
        edge = truncation - first_pair - q
        group = PACKED if rows % PACKED == 0 else SUB
        column = lax.broadcasted_iota(jnp.int32, (group, padded), 1)
        leading = column < edge
        odd = (jnp.where(leading, column, column - edge) & 1) == 1
        sign = jnp.where(odd, -1.0, 1.0)
        kind = jnp.bfloat16 if group == PACKED else jnp.float32
        factors = [
            jnp.where(leading, 1.0, 0.0),
            jnp.where(leading, 0.0, 1.0),
            jnp.where(leading, sign, 0.0),
            jnp.where(leading, 0.0, sign),
        ]
        x = x.astype(kind)
        lhs = []
        for factor in factors:
            factor = factor.astype(kind)
            for at in range(0, rows, group):
                lhs.append(x[at : at + group] * factor)
        lhs = jnp.concatenate(lhs, axis=0).astype(jnp.bfloat16)
        rhs = wide[pl.ds(q, padded, stride=block), :].astype(jnp.bfloat16)
        if keep:
            keep_ref[q] = rhs
        got = jnp.dot(lhs, rhs, preferred_element_type=jnp.float32)
        res[pl.ds(step * block + q, 4 * rows, stride=pairs), :] = got
        return carry

    lax.fori_loop(0, block, one, 0, unroll=UNROLL_FORWARD)

    @pl.when(step == pl.num_programs(0) - 1)
    def _():
        for n, slot in enumerate(made):
            place = slot_place(slot, direct)
            t, s = lax.div(place, 2) - t0, lax.rem(place, 2)
            base = pl.multiple_of((s * (2 * rows) + t * comps) * pairs, SUB)
            for f in range(comps // 2):
                parts = []
                for r in range(2):
                    for h in range(2):
                        parts.append(res[pl.ds(base + (h * rows + 2 * f + r) * pairs, pairs), :])
                out_refs[n][f] = jnp.concatenate(parts, axis=0).astype(jnp.bfloat16)


def grid_kernel(order_ref, cor_ref, weight_ref, syn_ref, ana_ref, *refs, scale):
    sources = order_ref.shape[0]
    in_refs, out_refs, (modes, force) = refs[:sources], refs[sources:-2], refs[-2:]
    fields, rows, lanes = in_refs[0].shape
    longitudes = syn_ref.shape[0]
    for n in range(sources):
        at = pl.multiple_of(order_ref[n] * rows, 16)
        for f in range(fields):
            modes[pl.ds(at, rows), f * lanes : (f + 1) * lanes] = in_refs[n][f]
    cor = cor_ref[...]
    weight = weight_ref[...]
    span = 128

    def synth(b, carry):
        at = pl.multiple_of(b * span, span)
        g = (
            jnp.dot(syn_ref[pl.ds(at, span), :], modes[...], preferred_element_type=jnp.float32)
            * scale
        )
        field = [g[:, f * lanes : (f + 1) * lanes] for f in range(fields)]
        mean = 0.5 * (field[4] + field[5])
        out = [None] * fields
        for a in range(2):
            spin = field[a] + cor
            div = field[2 + a]
            out[a] = -spin * div
            out[2 + a] = spin * field[a] - 0.5 * div * div
            out[4 + a] = -(field[4 + a] + mean) * div
        for f in range(fields):
            force[pl.ds(at, span), f * lanes : (f + 1) * lanes] = out[f].astype(jnp.bfloat16)
        return carry

    lax.fori_loop(0, longitudes // span, synth, 0)

    def analyse(d, carry):
        at = pl.multiple_of(d * rows, 16)
        w = jnp.dot(ana_ref[pl.ds(at, rows), :], force[...], preferred_element_type=jnp.float32)
        for f in range(fields):
            lane = slice(f * lanes, (f + 1) * lanes)
            modes[pl.ds(at, rows), lane] = (w[:, lane] * weight).astype(jnp.bfloat16)
        return carry

    lax.fori_loop(0, sources, analyse, 0)
    for n in range(sources):
        at = pl.multiple_of(order_ref[n] * rows, 16)
        for f in range(fields):
            out_refs[n][f] = modes[pl.ds(at, rows), f * lanes : (f + 1) * lanes]


def step_terms(degree, gm, hm, truncation):
    eig = wave_scale * (degree * (degree + 1)).astype(jnp.float32) / float(truncation * truncation)
    damping = 1.0 / (1.0 + diffusion * eig * eig)
    coupling = time_step * time_step * eig
    pm = [[gm[a][0] * hm[0][b] + gm[a][1] * hm[1][b] for b in range(2)] for a in range(2)]
    diag = [1.0 + coupling * pm[a][a] for a in range(2)]
    cross = [coupling * pm[0][1], coupling * pm[1][0]]
    inverse = 1.0 / (diag[0] * diag[1] - cross[0] * cross[1])
    solve = [
        [diag[1] * inverse, -cross[0] * inverse],
        [-cross[1] * inverse, diag[0] * inverse],
    ]
    push = [[time_step * eig * gm[a][b] for b in range(2)] for a in range(2)]
    return damping, solve, push


def semi_implicit_slabs(old, tend, terms, hm):
    damping, solve, push = terms
    out = [None] * 12
    for r in range(2):
        star = [old[c * 2 + r] + time_step * tend[c * 2 + r] for c in range(6)]
        right = [star[2 + a] + push[a][0] * star[4] + push[a][1] * star[5] for a in range(2)]
        div = [solve[a][0] * right[0] + solve[a][1] * right[1] for a in range(2)]
        for a in range(2):
            heat = (time_step * hm[a][0]) * div[0] + (time_step * hm[a][1]) * div[1]
            out[a * 2 + r] = damping * star[a]
            out[(2 + a) * 2 + r] = damping * div[a]
            out[(4 + a) * 2 + r] = damping * (star[4 + a] - heat)
    return out


def inverse_kernel(
    slot_ref,
    gravity_ref,
    stability_ref,
    *refs,
    truncation,
    pairs,
    real_pairs,
    chunks,
    last,
    stored,
    slots,
    count,
    patches,
    direct,
):
    w_refs, refs = refs[: chunks * slots], refs[chunks * slots :]
    leg_refs, refs = refs[:chunks], refs[chunks:]
    spec_ref, refs = refs[0], refs[1:]
    mended = count if stored else 0
    fresh_refs, refs = refs[: 2 * patches], refs[2 * patches :]
    mend_refs, refs = refs[:mended], refs[mended:]
    out_ref, ws, ten = refs[:3]
    if stored:
        wide = refs[3]
    step = pl.program_id(0)
    row_length = truncation + 1
    trajectories, comps, block, _ = out_ref.shape
    rows = trajectories * comps
    tiles = ten.shape[0]
    padded = tiles * LANES

    @pl.when(step == 0)
    def _():
        if stored:
            for k in range(chunks):
                wide[k, row_length * block :, :] = jnp.zeros(
                    (wide.shape[1] - row_length * block, LANES), jnp.float32
                )

        def fill(k, t, s, source):
            base = pl.multiple_of((s * (2 * rows) + t * comps) * pairs, SUB)
            for f in range(comps // 2):
                got = source(f).astype(jnp.float32)
                for r in range(2):
                    for h in range(2):
                        at = (r * 2 + h) * pairs
                        ws[k, pl.ds(base + (h * rows + 2 * f + r) * pairs, pairs), :] = got[
                            at : at + pairs, :
                        ]

        for k in range(chunks):
            for n in range(slots):
                place = slot_place(n, direct)
                fill(k, lax.div(place, 2), lax.rem(place, 2), lambda f: w_refs[k * slots + n][f])
        for i in range(mended):

            @pl.when(slot_ref[i] >= 0)
            def _():
                for s in range(2):
                    fill(0, slot_ref[i], s, lambda f: mend_refs[i][s, f])

    if stored:
        for k in range(chunks):
            wide[k, : row_length * block, :] = (
                leg_refs[k][...].astype(jnp.float32).reshape(row_length * block, LANES)
            )
    first_pair = lax.axis_index("space") * real_pairs + step * block

    def one(q, carry):
        at = pl.ds(step * block + q, 4 * rows, stride=pairs)
        lhs = jnp.concatenate([ws[k, at, :].astype(jnp.bfloat16) for k in range(chunks)], axis=1)
        if not stored:
            rhs = jnp.concatenate([leg_refs[k][q] for k in range(chunks)], axis=1)
        else:
            at = pl.ds(q, padded, stride=block)
            rhs = jnp.concatenate(
                [wide[k, at, :].astype(jnp.bfloat16) for k in range(chunks)], axis=1
            )
        got = lax.dot_general(
            lhs, rhs, (((1,), (1,)), ((), ())), preferred_element_type=jnp.float32
        )
        leading, odd, _ = layout_terms(first_pair + q, 1, 0, padded, truncation)
        north = jnp.where(leading, got[:rows], got[rows : 2 * rows])
        south = jnp.where(leading, got[2 * rows : 3 * rows], got[3 * rows :])
        total = north + jnp.where(odd, -south, south)
        for k in range(tiles):
            ten[k, pl.ds(q, rows, stride=block), :] = total[:, k * LANES : (k + 1) * LANES]
        return carry

    lax.fori_loop(0, block, one, 0, unroll=UNROLL_INVERSE)

    if last:
        gm = [[gravity_ref[a, b] for b in range(2)] for a in range(2)]
        hm = [[stability_ref[a, b] for b in range(2)] for a in range(2)]
    for k in range(tiles):
        width = min(LANES, row_length - k * LANES)
        lanes = slice(k * LANES, k * LANES + width)
        if last:
            _, _, degree = layout_terms(first_pair, block, k * LANES, width, truncation)
            terms = step_terms(degree, gm, hm, truncation)

        def body(t, carry):
            tend = []
            for c in range(comps):
                at = pl.multiple_of((t * comps + c) * block, SUB)
                value = ten[k, pl.ds(at, block), :][:, :width]
                tend.append(value)
            old = [spec_ref[t, c, :, lanes] for c in range(comps)]
            for i in range(mended):
                mine = slot_ref[i] == t
                old = [jnp.where(mine, 0.0, old[c]) for c in range(comps)]
            if last:
                tend = semi_implicit_slabs(old, tend, terms, hm)
            else:
                tend = [old[c] + time_step * tend[c] for c in range(comps)]
            for c in range(comps):
                out_ref[t, c, :, lanes] = tend[c]
            return carry

        lax.fori_loop(0, trajectories, body, 0, unroll=True)

    for i in range(patches):
        for there in range(2):
            mine = jnp.logical_and(slot_ref[i] >= 0, (slot_ref[count + i] != 0) == bool(there))

            @pl.when(mine)
            def _():
                for c in range(comps):
                    out_ref[slot_ref[i], c] += fresh_refs[2 * i + there][c]


def fourier_tables(pair_count, groups, truncation, longitudes):
    half_turn = longitudes // 2
    order = jnp.arange(pair_count + 1, dtype=jnp.int32)[None, :, None]
    column = jnp.arange(half_turn, dtype=jnp.int32)[None, None, :]
    quarter = jnp.arange(2, dtype=jnp.int32)[:, None, None] * (longitudes // 4)
    phase = (order * column + quarter) % longitudes
    angle = phase.astype(jnp.float32) * (2.0 * math.pi / longitudes)
    base = lax.optimization_barrier(jnp.cos(angle).astype(jnp.bfloat16))
    low = base[:, :pair_count]
    flip = (1 - 2 * (column % 2)) * (1 - 2 * jnp.arange(2, dtype=jnp.int32)[:, None, None])
    high = base[:, 1:] * flip.astype(jnp.bfloat16)
    pair = jnp.arange(pair_count, dtype=jnp.int32)[None, :, None]
    low_sign = (1 - 2 * (pair % 2)).astype(jnp.bfloat16)
    high_sign = (1 - 2 * ((truncation - 1 - pair) % 2)).astype(jnp.bfloat16)
    low = jnp.concatenate([low, low * low_sign], axis=2)
    high = jnp.concatenate([high, high * high_sign], axis=2)
    table = jnp.stack([low, high], axis=1)
    table = table.reshape(2, 2, groups, pair_count // groups, longitudes)
    return jnp.transpose(table, (2, 0, 1, 3, 4)).reshape(4 * pair_count, longitudes)


def far_members(members):
    return [(a, b) for a in range(members) for b in range(a + 1, members) if a ^ b != 1]


def pick_kernel(clones_ref, spec_ref, row_ref, slot_ref, *route_refs, local):
    row_ref[...] = spec_ref[...].astype(jnp.bfloat16)
    members, member = lax.axis_size("member"), lax.axis_index("member")
    for i, route_ref in enumerate(route_refs):
        source = lax.div(clones_ref[i, 1], local)
        target = lax.div(clones_ref[i, 0], local)
        route = jnp.where(source == target, 0, 1)
        low, high = jnp.minimum(source, target), jnp.maximum(source, target)
        for k, (a, b) in enumerate(far_members(members)):
            route = jnp.where(jnp.logical_and(low == a, high == b), 2 + k, route)
        route_ref[0] = route
        slot_ref[i] = jnp.where(target == member, clones_ref[i, 0] - target * local, -1)
        slot_ref[len(route_refs) + i] = jnp.bitwise_and(
            jnp.bitwise_xor(source, member), members // 2
        )


def pick_clones(spectra, clones):
    local, comps, pairs, row_length = spectra.shape
    count = clones.shape[0]
    smem = pl.BlockSpec(memory_space=pltpu.SMEM)
    block = (1, comps, pairs, row_length)
    got = pl.pallas_call(
        functools.partial(pick_kernel, local=local),
        out_shape=[
            jax.ShapeDtypeStruct((count,) + block[1:], jnp.bfloat16),
            jax.ShapeDtypeStruct((2 * count,), jnp.int32),
        ]
        + [jax.ShapeDtypeStruct((1,), jnp.int32)] * count,
        grid_spec=pltpu.PrefetchScalarGridSpec(
            num_scalar_prefetch=1,
            grid=(count,),
            in_specs=[pl.BlockSpec(block, lambda i, c: (lax.rem(c[i, 1], local), 0, 0, 0))],
            out_specs=[pl.BlockSpec(block, lambda i, c: (i, 0, 0, 0))] + [smem] * (1 + count),
        ),
        cost_estimate=pl.CostEstimate(
            flops=0, bytes_accessed=6 * 1024 * 1024, transcendentals=0
        ),
        name="pick",
    )(clones, spectra)
    return got[0], got[1], [r.reshape(()) for r in got[2:]]


def choose_kernel(clones_ref, *refs, local, slots, direct):
    in_refs, out_refs = refs[:slots], refs[slots:]
    for i, out_ref in enumerate(out_refs):
        t = lax.rem(clones_ref[i, 1], local)
        for n in range(slots):
            place = slot_place(n, direct)

            @pl.when(lax.div(place, 2) == t)
            def _():
                out_ref[lax.rem(place, 2)] = in_refs[n][...]


def choose_rows(parts, clones, local, direct):
    vmem = pl.BlockSpec(memory_space=pltpu.VMEM)
    return pl.pallas_call(
        functools.partial(choose_kernel, local=local, slots=len(parts), direct=direct),
        out_shape=[jax.ShapeDtypeStruct((2,) + parts[0].shape, parts[0].dtype)] * clones.shape[0],
        in_specs=[pl.BlockSpec(memory_space=pltpu.SMEM)] + [vmem] * len(parts),
        out_specs=[vmem] * clones.shape[0],
        cost_estimate=pl.CostEstimate(
            flops=0, bytes_accessed=4 * 1024 * 1024, transcendentals=0
        ),
        name="choose",
    )(clones, *parts)


def send_clone(row, route):
    members = lax.axis_size("member")

    def swap(pairs):
        both = pairs + [(b, a) for a, b in pairs]
        return lambda v: lax.ppermute(v, "member", both)

    branches = [lambda v: v, swap([(a, a + 1) for a in range(0, members, 2)])]
    branches += [swap([pair]) for pair in far_members(members)]
    return lax.switch(route, branches, row)


def share_row(row, owner):
    members = lax.axis_size("member")
    differs = jnp.bitwise_xor(owner, lax.axis_index("member").astype(jnp.int32))
    bit = 1
    while True:
        other = lax.ppermute(row, "member", [(m, m ^ bit) for m in range(members)])
        if 2 * bit >= members:
            return [row, other]
        row = jnp.where(jnp.bitwise_and(differs, bit) != 0, other, row)
        bit *= 2


def shards(spectra, legendre, sin_lat, gravity, stability, clones):
    trajectories, comps, pairs, row_length = spectra.shape
    truncation = row_length - 1
    half_lat = legendre.shape[2]
    longitudes = LONGITUDES_PER_WAVE * truncation
    space = lax.axis_size("space")
    position = lax.axis_index("space")
    fields = comps // 2
    split = space // (2 * trajectories)
    lane_count = LANES // split
    chunk_count = half_lat // LANES
    assert chunk_count > 2
    padded_pairs = -(-pairs // SUB) * SUB
    steps = padded_pairs // SUB
    tiles = -(-row_length // LANES)
    extra = padded_pairs - pairs
    rows = trajectories * comps

    count = clones.shape[0]
    slots = 2 * trajectories
    direct = split == 1
    state = spectra
    if extra:
        state = jnp.pad(state, ((0, 0), (0, 0), (0, extra), (0, 0)))
    order = jnp.arange(space, dtype=jnp.int32)
    if direct:
        order = jnp.bitwise_xor(position.astype(jnp.int32), order)
    columns = jnp.transpose(legendre, (1, 0, 2))
    if extra:
        columns = jnp.pad(columns, ((0, 0), (0, extra), (0, 0)))

    smem = pl.BlockSpec(memory_space=pltpu.SMEM)
    state_spec = pl.BlockSpec((trajectories, comps, SUB, row_length), lambda i: (0, 0, i, 0))
    fresh_spec = pl.BlockSpec((comps, SUB, row_length), lambda i: (0, i, 0))
    kept_spec = pl.BlockSpec((SUB, tiles * LANES, LANES), lambda i: (i, 0, 0))
    part_shape = (fields, 4 * padded_pairs, LANES)
    part_spec = pl.BlockSpec(part_shape, lambda i: (0, 0, 0))
    mend_spec = pl.BlockSpec((2,) + part_shape, lambda i: (0, 0, 0, 0))

    def leg_spec(k):
        return pl.BlockSpec((row_length, SUB, LANES), lambda i: (0, i, k))

    mib = 1024 * 1024

    def forward(k, made, span, clone_slot, patches):
        keep = k > 0
        kept_shape = jax.ShapeDtypeStruct((padded_pairs, tiles * LANES, LANES), jnp.bfloat16)
        return pl.pallas_call(
            functools.partial(
                forward_kernel, truncation=truncation, pairs=padded_pairs, keep=keep,
                real_pairs=pairs, count=len(patches), made=made, span=span, direct=direct,
            ),
            out_shape=[jax.ShapeDtypeStruct(part_shape, jnp.bfloat16)] * len(made)
            + [kept_shape] * keep,
            grid=(steps,),
            in_specs=[smem] * bool(patches)
            + [state_spec, leg_spec(k)]
            + [fresh_spec] * len(patches),
            out_specs=[part_spec] * len(made) + [kept_spec] * keep,
            scratch_shapes=[
                pltpu.VMEM((tiles * LANES * SUB, LANES), jnp.float32),
                pltpu.VMEM((tiles, span * comps * SUB, LANES), jnp.float32),
                pltpu.VMEM((4 * span * comps * padded_pairs, LANES), jnp.float32),
            ],
            compiler_params=pltpu.CompilerParams(vmem_limit_bytes=60 * mib),
            cost_estimate=pl.CostEstimate(
                flops=8 * span * comps * padded_pairs * row_length * LANES,
                bytes_accessed=16 * 1024 * 1024,
                transcendentals=0,
            ),
            name="forward",
        )(*([clone_slot] if patches else []), state, columns, *patches)

    def to_wire(x):
        if extra:
            x = x.reshape(slots, fields, 4, padded_pairs, LANES)[:, :, :, :pairs]
        x = x.reshape(slots, fields, 4 * pairs, split, lane_count)
        return jnp.transpose(x, (0, 3, 1, 2, 4)).reshape(space, fields, 4 * pairs, lane_count)

    def from_wire(x):
        x = x.reshape(slots, split, fields, 4, pairs, lane_count)
        x = jnp.transpose(x, (0, 2, 3, 4, 1, 5)).reshape(slots, fields, 4, pairs, LANES)
        if extra:
            x = jnp.pad(x, ((0, 0), (0, 0), (0, 0), (0, extra), (0, 0)))
        return x.reshape((slots,) + part_shape)

    def exchange(x):
        return lax.all_to_all(x, "space", split_axis=0, concat_axis=0, tiled=True)

    def swap(parts):
        got = list(parts)
        for n in reversed(range(1, space)):
            got[n] = lax.ppermute(parts[n], "space", [(d, d ^ n) for d in range(space)])
        return got

    def spread(parts):
        if direct:
            return swap(parts)
        x = exchange(to_wire(jnp.stack(parts)))
        x = jnp.pad(x, ((0, 0), (0, 0), (0, 0), (0, LANES - lane_count)))
        return [x[d] for d in range(space)]

    def collect(parts):
        if direct:
            return swap(parts)
        x = from_wire(exchange(jnp.stack(parts)[..., :lane_count]))
        return [x[n] for n in range(slots)]

    analysis = lax.optimization_barrier(
        fourier_tables(pairs * space, space, truncation, longitudes)
    )
    synthesis = analysis.T
    south = position // split % 2
    hemisphere = jnp.where(south == 0, sin_lat, -sin_lat)
    weights_all = math.pi * jnp.sqrt(1.0 - hemisphere * hemisphere) / (2 * half_lat)
    vmem = pl.BlockSpec(memory_space=pltpu.VMEM)
    modes = 4 * pairs * space

    def grid(k, parts):
        first = k * LANES + position % split * lane_count
        mu = lax.dynamic_slice_in_dim(hemisphere, first, lane_count)
        weight = lax.dynamic_slice_in_dim(weights_all, first, lane_count)
        short = LANES - lane_count
        if short:
            mu = jnp.pad(mu, (0, short))
            weight = jnp.pad(weight, (0, short))
        return pl.pallas_call(
            functools.partial(grid_kernel, scale=1.0 / truncation),
            out_shape=[jax.ShapeDtypeStruct(x.shape, jnp.bfloat16) for x in parts],
            in_specs=[smem] + [vmem] * (4 + space),
            out_specs=[vmem] * space,
            scratch_shapes=[
                pltpu.VMEM((modes, fields * LANES), jnp.bfloat16),
                pltpu.VMEM((longitudes, fields * LANES), jnp.bfloat16),
            ],
            compiler_params=pltpu.CompilerParams(vmem_limit_bytes=60 * mib),
            cost_estimate=pl.CostEstimate(
                flops=4 * modes * longitudes * fields * LANES,
                bytes_accessed=12 * 1024 * 1024,
                transcendentals=0,
            ),
            name="grid",
        )(order, (2.0 * mu)[None], weight[None], synthesis, analysis, *parts)

    def inverse(ws, legs, start, patches, mends, last):
        chunks = len(ws)
        stored = bool(mends)
        wide_scratch = pltpu.VMEM((chunks, tiles * LANES * SUB, LANES), jnp.float32)
        return pl.pallas_call(
            functools.partial(
                inverse_kernel,
                truncation=truncation,
                pairs=padded_pairs,
                chunks=chunks,
                last=last,
                stored=stored,
                slots=slots,
                count=count,
                patches=len(patches) // 2,
                real_pairs=pairs,
                direct=direct,
            ),
            out_shape=jax.ShapeDtypeStruct(state.shape, jnp.float32),
            grid=(steps,),
            in_specs=[smem] * 3
            + [part_spec] * (chunks * slots)
            + ([leg_spec(k) for k in range(chunks)] if stored else [kept_spec] * chunks)
            + [state_spec]
            + [fresh_spec] * len(patches)
            + [mend_spec] * len(mends),
            out_specs=state_spec,
            scratch_shapes=[
                pltpu.VMEM((chunks, 4 * rows * padded_pairs, LANES), jnp.float32),
                pltpu.VMEM((tiles, rows * SUB, LANES), jnp.float32),
            ]
            + ([wide_scratch] if stored else []),
            compiler_params=pltpu.CompilerParams(vmem_limit_bytes=60 * mib),
            cost_estimate=pl.CostEstimate(
                flops=8 * rows * padded_pairs * row_length * LANES * chunks,
                bytes_accessed=20 * 1024 * 1024,
                transcendentals=0,
            ),
            name="inverse",
        )(slot, gravity, stability, *[x for w in ws for x in w], *legs, start, *patches, *mends)

    everything = tuple(range(slots))
    halved = direct and trajectories % 2 == 0
    near, far = everything[: slots // 2], everything[slots // 2 :]
    if halved:
        first = list(forward(0, far, trajectories // 2, None, []))
        second = list(forward(0, near, trajectories // 2, None, []))
    else:
        first = list(forward(0, everything, trajectories, None, []))

    turn, first[0] = lax.optimization_barrier((clones, first[0]))
    made = [second + first if halved else first]
    picked, slot, route = pick_clones(spectra, turn)
    narrow = [send_clone(picked[i], route[i]) for i in range(count)]
    if extra:
        narrow = [jnp.pad(x, ((0, 0), (0, extra), (0, 0))) for x in narrow]
    turn = slot
    for k in range(1, chunk_count):
        made.append(list(forward(k, everything, trajectories, turn, narrow)))
        turn, made[k][0] = lax.optimization_barrier((slot, made[k][0]))
    later, made[-1][0] = lax.optimization_barrier((clones[:, 1], made[-1][0]))
    kept = [x[-1] for x in made[1:]]
    sent = []
    for x in made:
        sent.append(spread(x[:slots]))
    back = []
    for k in range(chunk_count):
        got = grid(k, sent[k])
        back.append(collect(got))
    fresh = [
        share_row(
            lax.dynamic_index_in_dim(spectra, lax.rem(later[i], trajectories), 0, keepdims=False),
            lax.div(later[i], trajectories),
        )
        for i in range(count)
    ]
    fresh = [x for pair in fresh for x in pair]
    if extra:
        fresh = [jnp.pad(x, ((0, 0), (0, extra), (0, 0))) for x in fresh]
    chosen = choose_rows(back[0], clones, trajectories, direct)
    mends = [send_clone(chosen[i], route[i]) for i in range(count)]
    start = inverse(back[:1], [columns], state, [], mends, False)
    for k in range(1, chunk_count - 1):
        start = inverse(back[k : k + 1], kept[k - 1 : k], start, fresh, [], False)
        fresh = []
    out = inverse(back[-1:], kept[-1:], start, fresh, [], True)
    return out[:, :, :pairs] if extra else out


def solution(mesh):
    placed = (P("member", None, "space", None), P("space", None, None), P(), P(), P(), P())
    return jax.shard_map(
        shards,
        mesh=mesh,
        in_specs=placed,
        out_specs=P("member", None, "space", None),
        check_vma=False,
    )
```

```python
import functools
import math

import jax
import jax.numpy as jnp
from jax import lax
from jax.experimental import pallas as pl
from jax.experimental.pallas import tpu as pltpu
from jax.sharding import PartitionSpec as P


LANES = 128
SUB = 8
PACKED = 16
DEEP = 256
UNROLL_FORWARD = 8
UNROLL_INVERSE = 8
LONGITUDES_PER_WAVE = 2

time_step = 0.25
wave_scale = 16.0
diffusion = 0.02


def layout_terms(first_pair, count, lane0, lanes, truncation):
    pair = first_pair + lax.broadcasted_iota(jnp.int32, (count, lanes), 0)
    column = lane0 + lax.broadcasted_iota(jnp.int32, (count, lanes), 1)
    leading = column < truncation - pair
    offset = jnp.where(leading, column, column - (truncation - pair))
    order = jnp.where(leading, pair, truncation - 1 - pair)
    return leading, (offset & 1) == 1, order + offset


def slot_place(n, direct):
    return jnp.bitwise_xor(lax.axis_index("space"), n) if direct else jnp.int32(n)


def forward_kernel(
    *refs, truncation, pairs, real_pairs, keep, count, made, span, direct
):
    if count:
        slot_ref, refs = refs[0], refs[1:]
    spec_ref, leg_ref, refs = refs[0], refs[1], refs[2:]
    step = pl.program_id(0)
    row_length = truncation + 1
    _, comps, block, _ = spec_ref.shape
    rows = span * comps
    fresh_refs, refs = refs[:count], refs[count:]
    out_refs, refs = refs[: len(made)], refs[len(made) :]
    if keep:
        keep_ref, refs = refs[0], refs[1:]
    wide, xs, res = refs
    tiles = xs.shape[0]
    padded = tiles * LANES
    first_place = lax.div(slot_place(made[0], direct), 2)
    t0 = lax.div(first_place, span) * span

    @pl.when(step == 0)
    def _():
        wide[row_length * block :, :] = jnp.zeros(
            (wide.shape[0] - row_length * block, LANES), jnp.float32
        )

    wide[: row_length * block, :] = (
        leg_ref[...].astype(jnp.float32).reshape(row_length * block, LANES)
    )
    for k in range(tiles):
        width = min(LANES, row_length - k * LANES)
        lanes = slice(k * LANES, k * LANES + width)
        if width < LANES:
            xs[k] = jnp.zeros((rows * block, LANES), jnp.float32)
        xs[k, :, :width] = spec_ref[pl.ds(t0, span), :, :, lanes].reshape(rows * block, width)

    for i in range(count):
        slot = slot_ref[i] - t0

        @pl.when(jnp.logical_and(slot >= 0, slot < span))
        def _():
            at = pl.multiple_of(slot * comps * block, SUB)
            for k in range(tiles):
                width = min(LANES, row_length - k * LANES)
                fresh = fresh_refs[i][:, :, k * LANES : k * LANES + width].astype(jnp.float32)
                xs[k, pl.ds(at, comps * block), :width] = fresh.reshape(comps * block, width)

    first_pair = lax.axis_index("space") * real_pairs + step * block

    def one(q, carry):
        x = jnp.concatenate(
            [xs[k, pl.ds(q, rows, stride=block), :] for k in range(tiles)], axis=1
        )
        edge = truncation - first_pair - q
        group = PACKED if rows % PACKED == 0 else SUB
        column = lax.broadcasted_iota(jnp.int32, (group, padded), 1)
        leading = column < edge
        odd = (jnp.where(leading, column, column - edge) & 1) == 1
        sign = jnp.where(odd, -1.0, 1.0)
        kind = jnp.bfloat16 if group == PACKED else jnp.float32
        factors = [
            jnp.where(leading, 1.0, 0.0),
            jnp.where(leading, 0.0, 1.0),
            jnp.where(leading, sign, 0.0),
            jnp.where(leading, 0.0, sign),
        ]
        x = x.astype(kind)
        lhs = []
        for factor in factors:
            factor = factor.astype(kind)
            for at in range(0, rows, group):
                lhs.append(x[at : at + group] * factor)
        lhs = jnp.concatenate(lhs, axis=0).astype(jnp.bfloat16)
        rhs = wide[pl.ds(q, padded, stride=block), :].astype(jnp.bfloat16)
        if keep:
            keep_ref[q] = rhs
        got = jnp.dot(lhs, rhs, preferred_element_type=jnp.float32)
        res[pl.ds(step * block + q, 4 * rows, stride=pairs), :] = got
        return carry

    lax.fori_loop(0, block, one, 0, unroll=UNROLL_FORWARD)

    @pl.when(step == pl.num_programs(0) - 1)
    def _():
        for n, slot in enumerate(made):
            place = slot_place(slot, direct)
            t, s = lax.div(place, 2) - t0, lax.rem(place, 2)
            base = pl.multiple_of((s * (2 * rows) + t * comps) * pairs, SUB)
            for f in range(comps // 2):
                parts = []
                for r in range(2):
                    for h in range(2):
                        parts.append(res[pl.ds(base + (h * rows + 2 * f + r) * pairs, pairs), :])
                out_refs[n][f] = jnp.concatenate(parts, axis=0).astype(jnp.bfloat16)


def grid_kernel(order_ref, cor_ref, weight_ref, syn_ref, ana_ref, *refs, scale):
    sources = order_ref.shape[0]
    in_refs, out_refs, (modes, force) = refs[:sources], refs[sources:-2], refs[-2:]
    fields, rows, lanes = in_refs[0].shape
    longitudes = syn_ref.shape[0]
    for n in range(sources):
        at = pl.multiple_of(order_ref[n] * rows, 16)
        for f in range(fields):
            modes[pl.ds(at, rows), f * lanes : (f + 1) * lanes] = in_refs[n][f]
    cor = cor_ref[...]
    weight = weight_ref[...]
    span = 128

    def synth(b, carry):
        at = pl.multiple_of(b * span, span)
        g = (
            jnp.dot(syn_ref[pl.ds(at, span), :], modes[...], preferred_element_type=jnp.float32)
            * scale
        )
        field = [g[:, f * lanes : (f + 1) * lanes] for f in range(fields)]
        mean = 0.5 * (field[4] + field[5])
        out = [None] * fields
        for a in range(2):
            spin = field[a] + cor
            div = field[2 + a]
            out[a] = -spin * div
            out[2 + a] = spin * field[a] - 0.5 * div * div
            out[4 + a] = -(field[4 + a] + mean) * div
        for f in range(fields):
            force[pl.ds(at, span), f * lanes : (f + 1) * lanes] = out[f].astype(jnp.bfloat16)
        return carry

    lax.fori_loop(0, longitudes // span, synth, 0)

    def analyse(d, carry):
        at = pl.multiple_of(d * rows, 16)
        w = jnp.dot(ana_ref[pl.ds(at, rows), :], force[...], preferred_element_type=jnp.float32)
        for f in range(fields):
            lane = slice(f * lanes, (f + 1) * lanes)
            modes[pl.ds(at, rows), lane] = (w[:, lane] * weight).astype(jnp.bfloat16)
        return carry

    lax.fori_loop(0, sources, analyse, 0)
    for n in range(sources):
        at = pl.multiple_of(order_ref[n] * rows, 16)
        for f in range(fields):
            out_refs[n][f] = modes[pl.ds(at, rows), f * lanes : (f + 1) * lanes]


def step_terms(degree, gm, hm, truncation):
    eig = wave_scale * (degree * (degree + 1)).astype(jnp.float32) / float(truncation * truncation)
    damping = 1.0 / (1.0 + diffusion * eig * eig)
    coupling = time_step * time_step * eig
    pm = [[gm[a][0] * hm[0][b] + gm[a][1] * hm[1][b] for b in range(2)] for a in range(2)]
    diag = [1.0 + coupling * pm[a][a] for a in range(2)]
    cross = [coupling * pm[0][1], coupling * pm[1][0]]
    inverse = 1.0 / (diag[0] * diag[1] - cross[0] * cross[1])
    solve = [
        [diag[1] * inverse, -cross[0] * inverse],
        [-cross[1] * inverse, diag[0] * inverse],
    ]
    push = [[time_step * eig * gm[a][b] for b in range(2)] for a in range(2)]
    return damping, solve, push


def semi_implicit_slabs(old, tend, terms, hm):
    damping, solve, push = terms
    out = [None] * 12
    for r in range(2):
        star = [old[c * 2 + r] + time_step * tend[c * 2 + r] for c in range(6)]
        right = [star[2 + a] + push[a][0] * star[4] + push[a][1] * star[5] for a in range(2)]
        div = [solve[a][0] * right[0] + solve[a][1] * right[1] for a in range(2)]
        for a in range(2):
            heat = (time_step * hm[a][0]) * div[0] + (time_step * hm[a][1]) * div[1]
            out[a * 2 + r] = damping * star[a]
            out[(2 + a) * 2 + r] = damping * div[a]
            out[(4 + a) * 2 + r] = damping * (star[4 + a] - heat)
    return out


def inverse_kernel(
    slot_ref,
    gravity_ref,
    stability_ref,
    *refs,
    truncation,
    pairs,
    real_pairs,
    chunks,
    last,
    stored,
    slots,
    count,
    patches,
    direct,
):
    w_refs, refs = refs[: chunks * slots], refs[chunks * slots :]
    leg_refs, refs = refs[:chunks], refs[chunks:]
    spec_ref, refs = refs[0], refs[1:]
    mended = count if stored else 0
    fresh_refs, refs = refs[: 2 * patches], refs[2 * patches :]
    mend_refs, refs = refs[:mended], refs[mended:]
    out_ref, ws, ten = refs[:3]
    if stored:
        wide = refs[3]
    step = pl.program_id(0)
    row_length = truncation + 1
    trajectories, comps, block, _ = out_ref.shape
    rows = trajectories * comps
    tiles = ten.shape[0]
    padded = tiles * LANES

    @pl.when(step == 0)
    def _():
        if stored:
            for k in range(chunks):
                wide[k, row_length * block :, :] = jnp.zeros(
                    (wide.shape[1] - row_length * block, LANES), jnp.float32
                )

        def fill(k, t, s, source):
            base = pl.multiple_of((s * (2 * rows) + t * comps) * pairs, SUB)
            for f in range(comps // 2):
                got = source(f).astype(jnp.float32)
                for r in range(2):
                    for h in range(2):
                        at = (r * 2 + h) * pairs
                        ws[k, pl.ds(base + (h * rows + 2 * f + r) * pairs, pairs), :] = got[
                            at : at + pairs, :
                        ]

        for k in range(chunks):
            for n in range(slots):
                place = slot_place(n, direct)
                fill(k, lax.div(place, 2), lax.rem(place, 2), lambda f: w_refs[k * slots + n][f])
        for i in range(mended):

            @pl.when(slot_ref[i] >= 0)
            def _():
                for s in range(2):
                    fill(0, slot_ref[i], s, lambda f: mend_refs[i][s, f])

    if stored:
        for k in range(chunks):
            wide[k, : row_length * block, :] = (
                leg_refs[k][...].astype(jnp.float32).reshape(row_length * block, LANES)
            )
    first_pair = lax.axis_index("space") * real_pairs + step * block

    def split_product(q):
        edge = truncation - first_pair - q
        late = edge > 2 * DEEP
        border = jnp.where(late, 2, 1)

        def half(h):
            got = []
            for s in range(2):
                start = (2 * s + h) * (rows * pairs) + step * block + q
                got.append(ws[0, pl.ds(start, rows, stride=pairs), :].astype(jnp.bfloat16))
            return jnp.concatenate(got, axis=0)

        def product(rows_of, first, width, shift):
            got = lax.dot_general(
                rows_of,
                leg_refs[0][q, pl.ds(first, width), :],
                (((1,), (1,)), ((), ())),
                preferred_element_type=jnp.float32,
            )
            column = first + lax.broadcasted_iota(jnp.int32, (1, width), 1) - shift
            south = got[rows:]
            return got[:rows] + jnp.where((column & 1) == 1, -south, south)

        lead = product(half(0), 0, 2 * DEEP, 0)
        trail = product(half(1), 2 * DEEP, DEEP, edge)
        other = product(
            half(jnp.where(late, 0, 1)),
            pl.multiple_of(border * DEEP, DEEP),
            DEEP,
            jnp.where(late, 0, edge),
        )
        column = lax.broadcasted_iota(jnp.int32, (1, DEEP), 1)
        middle = jnp.where(column < edge - DEEP, lead[:, DEEP:], other)
        tail = jnp.where(column < edge - 2 * DEEP, other, trail)
        return jnp.concatenate([lead[:, :DEEP], middle, tail], axis=1)

    def one(q, carry):
        if last and tiles * LANES == 3 * DEEP:
            total = split_product(q)
        else:
            at = pl.ds(step * block + q, 4 * rows, stride=pairs)
            lhs = jnp.concatenate([ws[k, at, :].astype(jnp.bfloat16) for k in range(chunks)], axis=1)
            if not stored:
                rhs = jnp.concatenate([leg_refs[k][q] for k in range(chunks)], axis=1)
            else:
                at = pl.ds(q, padded, stride=block)
                rhs = jnp.concatenate(
                    [wide[k, at, :].astype(jnp.bfloat16) for k in range(chunks)], axis=1
                )
            got = lax.dot_general(
                lhs, rhs, (((1,), (1,)), ((), ())), preferred_element_type=jnp.float32
            )
            leading, odd, _ = layout_terms(first_pair + q, 1, 0, padded, truncation)
            north = jnp.where(leading, got[:rows], got[rows : 2 * rows])
            south = jnp.where(leading, got[2 * rows : 3 * rows], got[3 * rows :])
            total = north + jnp.where(odd, -south, south)
        for k in range(tiles):
            ten[k, pl.ds(q, rows, stride=block), :] = total[:, k * LANES : (k + 1) * LANES]
        return carry

    lax.fori_loop(0, block, one, 0, unroll=UNROLL_INVERSE)

    if last:
        gm = [[gravity_ref[a, b] for b in range(2)] for a in range(2)]
        hm = [[stability_ref[a, b] for b in range(2)] for a in range(2)]
    for k in range(tiles):
        width = min(LANES, row_length - k * LANES)
        lanes = slice(k * LANES, k * LANES + width)
        if last:
            _, _, degree = layout_terms(first_pair, block, k * LANES, width, truncation)
            terms = step_terms(degree, gm, hm, truncation)

        def body(t, carry):
            tend = []
            for c in range(comps):
                at = pl.multiple_of((t * comps + c) * block, SUB)
                value = ten[k, pl.ds(at, block), :][:, :width]
                tend.append(value)
            old = [spec_ref[t, c, :, lanes] for c in range(comps)]
            if mended:
                killed = slot_ref[0] == t
                for i in range(1, mended):
                    killed = jnp.logical_or(killed, slot_ref[i] == t)
                old = [jnp.where(killed, 0.0, old[c]) for c in range(comps)]
            if last:
                tend = semi_implicit_slabs(old, tend, terms, hm)
            else:
                tend = [old[c] + time_step * tend[c] for c in range(comps)]
            for c in range(comps):
                out_ref[t, c, :, lanes] = tend[c]
            return carry

        lax.fori_loop(0, trajectories, body, 0, unroll=True)

    for i in range(patches):
        for there in range(2):
            mine = jnp.logical_and(slot_ref[i] >= 0, (slot_ref[count + i] != 0) == bool(there))

            @pl.when(mine)
            def _():
                for c in range(comps):
                    out_ref[slot_ref[i], c] += fresh_refs[2 * i + there][c]


def fourier_tables(pair_count, groups, truncation, longitudes):
    half_turn = longitudes // 2
    order = jnp.arange(pair_count + 1, dtype=jnp.int32)[None, :, None]
    column = jnp.arange(half_turn, dtype=jnp.int32)[None, None, :]
    quarter = jnp.arange(2, dtype=jnp.int32)[:, None, None] * (longitudes // 4)
    phase = (order * column + quarter) % longitudes
    angle = phase.astype(jnp.float32) * (2.0 * math.pi / longitudes)
    base = lax.optimization_barrier(jnp.cos(angle).astype(jnp.bfloat16))
    low = base[:, :pair_count]
    flip = (1 - 2 * (column % 2)) * (1 - 2 * jnp.arange(2, dtype=jnp.int32)[:, None, None])
    high = base[:, 1:] * flip.astype(jnp.bfloat16)
    pair = jnp.arange(pair_count, dtype=jnp.int32)[None, :, None]
    low_sign = (1 - 2 * (pair % 2)).astype(jnp.bfloat16)
    high_sign = (1 - 2 * ((truncation - 1 - pair) % 2)).astype(jnp.bfloat16)
    low = jnp.concatenate([low, low * low_sign], axis=2)
    high = jnp.concatenate([high, high * high_sign], axis=2)
    table = jnp.stack([low, high], axis=1)
    table = table.reshape(2, 2, groups, pair_count // groups, longitudes)
    return jnp.transpose(table, (2, 0, 1, 3, 4)).reshape(4 * pair_count, longitudes)


def far_members(members):
    return [(a, b) for a in range(members) for b in range(a + 1, members) if a ^ b != 1]


def pick_kernel(clones_ref, spec_ref, row_ref, slot_ref, *route_refs, local):
    row_ref[...] = spec_ref[...].astype(jnp.bfloat16)
    members, member = lax.axis_size("member"), lax.axis_index("member")
    for i, route_ref in enumerate(route_refs):
        source = lax.div(clones_ref[i, 1], local)
        target = lax.div(clones_ref[i, 0], local)
        route = jnp.where(source == target, 0, 1)
        low, high = jnp.minimum(source, target), jnp.maximum(source, target)
        for k, (a, b) in enumerate(far_members(members)):
            route = jnp.where(jnp.logical_and(low == a, high == b), 2 + k, route)
        route_ref[0] = route
        slot_ref[i] = jnp.where(target == member, clones_ref[i, 0] - target * local, -1)
        slot_ref[len(route_refs) + i] = jnp.bitwise_and(
            jnp.bitwise_xor(source, member), members // 2
        )


def pick_clones(spectra, clones):
    local, comps, pairs, row_length = spectra.shape
    count = clones.shape[0]
    smem = pl.BlockSpec(memory_space=pltpu.SMEM)
    block = (1, comps, pairs, row_length)
    got = pl.pallas_call(
        functools.partial(pick_kernel, local=local),
        out_shape=[
            jax.ShapeDtypeStruct((count,) + block[1:], jnp.bfloat16),
            jax.ShapeDtypeStruct((2 * count,), jnp.int32),
        ]
        + [jax.ShapeDtypeStruct((1,), jnp.int32)] * count,
        grid_spec=pltpu.PrefetchScalarGridSpec(
            num_scalar_prefetch=1,
            grid=(count,),
            in_specs=[pl.BlockSpec(block, lambda i, c: (lax.rem(c[i, 1], local), 0, 0, 0))],
            out_specs=[pl.BlockSpec(block, lambda i, c: (i, 0, 0, 0))] + [smem] * (1 + count),
        ),
        cost_estimate=pl.CostEstimate(
            flops=0, bytes_accessed=6 * 1024 * 1024, transcendentals=0
        ),
        name="pick",
    )(clones, spectra)
    return got[0], got[1], [r.reshape(()) for r in got[2:]]


def choose_kernel(clones_ref, *refs, local, slots, direct):
    in_refs, out_refs = refs[:slots], refs[slots:]
    for i, out_ref in enumerate(out_refs):
        t = lax.rem(clones_ref[i, 1], local)
        for n in range(slots):
            place = slot_place(n, direct)

            @pl.when(lax.div(place, 2) == t)
            def _():
                out_ref[lax.rem(place, 2)] = in_refs[n][...]


def choose_rows(parts, clones, local, direct):
    vmem = pl.BlockSpec(memory_space=pltpu.VMEM)
    return pl.pallas_call(
        functools.partial(choose_kernel, local=local, slots=len(parts), direct=direct),
        out_shape=[jax.ShapeDtypeStruct((2,) + parts[0].shape, parts[0].dtype)] * clones.shape[0],
        in_specs=[pl.BlockSpec(memory_space=pltpu.SMEM)] + [vmem] * len(parts),
        out_specs=[vmem] * clones.shape[0],
        cost_estimate=pl.CostEstimate(
            flops=0, bytes_accessed=4 * 1024 * 1024, transcendentals=0
        ),
        name="choose",
    )(clones, *parts)


def send_clone(row, route):
    members = lax.axis_size("member")

    def swap(pairs):
        both = pairs + [(b, a) for a, b in pairs]
        return lambda v: lax.ppermute(v, "member", both)

    branches = [lambda v: v, swap([(a, a + 1) for a in range(0, members, 2)])]
    branches += [swap([pair]) for pair in far_members(members)]
    return lax.switch(route, branches, row)


def share_row(row, owner):
    members = lax.axis_size("member")
    differs = jnp.bitwise_xor(owner, lax.axis_index("member").astype(jnp.int32))
    bit = 1
    while True:
        other = lax.ppermute(row, "member", [(m, m ^ bit) for m in range(members)])
        if 2 * bit >= members:
            return [row, other]
        row = jnp.where(jnp.bitwise_and(differs, bit) != 0, other, row)
        bit *= 2


def shards(spectra, legendre, sin_lat, gravity, stability, clones):
    trajectories, comps, pairs, row_length = spectra.shape
    truncation = row_length - 1
    half_lat = legendre.shape[2]
    longitudes = LONGITUDES_PER_WAVE * truncation
    space = lax.axis_size("space")
    position = lax.axis_index("space")
    fields = comps // 2
    split = space // (2 * trajectories)
    lane_count = LANES // split
    chunk_count = half_lat // LANES
    assert chunk_count > 2
    padded_pairs = -(-pairs // SUB) * SUB
    steps = padded_pairs // SUB
    tiles = -(-row_length // LANES)
    extra = padded_pairs - pairs
    rows = trajectories * comps

    count = clones.shape[0]
    slots = 2 * trajectories
    direct = split == 1
    state = spectra
    if extra:
        state = jnp.pad(state, ((0, 0), (0, 0), (0, extra), (0, 0)))
    order = jnp.arange(space, dtype=jnp.int32)
    if direct:
        order = jnp.bitwise_xor(position.astype(jnp.int32), order)
    columns = jnp.transpose(legendre, (1, 0, 2))
    if extra:
        columns = jnp.pad(columns, ((0, 0), (0, extra), (0, 0)))

    smem = pl.BlockSpec(memory_space=pltpu.SMEM)
    state_spec = pl.BlockSpec((trajectories, comps, SUB, row_length), lambda i: (0, 0, i, 0))
    fresh_spec = pl.BlockSpec((comps, SUB, row_length), lambda i: (0, i, 0))
    kept_spec = pl.BlockSpec((SUB, tiles * LANES, LANES), lambda i: (i, 0, 0))
    part_shape = (fields, 4 * padded_pairs, LANES)
    part_spec = pl.BlockSpec(part_shape, lambda i: (0, 0, 0))
    mend_spec = pl.BlockSpec((2,) + part_shape, lambda i: (0, 0, 0, 0))

    def leg_spec(k):
        return pl.BlockSpec((row_length, SUB, LANES), lambda i: (0, i, k))

    mib = 1024 * 1024

    def forward(k, made, span, clone_slot, patches):
        keep = k > 0
        kept_shape = jax.ShapeDtypeStruct((padded_pairs, tiles * LANES, LANES), jnp.bfloat16)
        return pl.pallas_call(
            functools.partial(
                forward_kernel, truncation=truncation, pairs=padded_pairs, keep=keep,
                real_pairs=pairs, count=len(patches), made=made, span=span, direct=direct,
            ),
            out_shape=[jax.ShapeDtypeStruct(part_shape, jnp.bfloat16)] * len(made)
            + [kept_shape] * keep,
            grid=(steps,),
            in_specs=[smem] * bool(patches)
            + [state_spec, leg_spec(k)]
            + [fresh_spec] * len(patches),
            out_specs=[part_spec] * len(made) + [kept_spec] * keep,
            scratch_shapes=[
                pltpu.VMEM((tiles * LANES * SUB, LANES), jnp.float32),
                pltpu.VMEM((tiles, span * comps * SUB, LANES), jnp.float32),
                pltpu.VMEM((4 * span * comps * padded_pairs, LANES), jnp.float32),
            ],
            compiler_params=pltpu.CompilerParams(vmem_limit_bytes=60 * mib),
            cost_estimate=pl.CostEstimate(
                flops=8 * span * comps * padded_pairs * row_length * LANES,
                bytes_accessed=16 * 1024 * 1024,
                transcendentals=0,
            ),
            name="forward",
        )(*([clone_slot] if patches else []), state, columns, *patches)

    def to_wire(x):
        if extra:
            x = x.reshape(slots, fields, 4, padded_pairs, LANES)[:, :, :, :pairs]
        x = x.reshape(slots, fields, 4 * pairs, split, lane_count)
        return jnp.transpose(x, (0, 3, 1, 2, 4)).reshape(space, fields, 4 * pairs, lane_count)

    def from_wire(x):
        x = x.reshape(slots, split, fields, 4, pairs, lane_count)
        x = jnp.transpose(x, (0, 2, 3, 4, 1, 5)).reshape(slots, fields, 4, pairs, LANES)
        if extra:
            x = jnp.pad(x, ((0, 0), (0, 0), (0, 0), (0, extra), (0, 0)))
        return x.reshape((slots,) + part_shape)

    def exchange(x):
        return lax.all_to_all(x, "space", split_axis=0, concat_axis=0, tiled=True)

    def swap(parts):
        got = list(parts)
        for n in reversed(range(1, space)):
            got[n] = lax.ppermute(parts[n], "space", [(d, d ^ n) for d in range(space)])
        return got

    def spread(parts):
        if direct:
            return swap(parts)
        x = exchange(to_wire(jnp.stack(parts)))
        x = jnp.pad(x, ((0, 0), (0, 0), (0, 0), (0, LANES - lane_count)))
        return [x[d] for d in range(space)]

    def collect(parts):
        if direct:
            return swap(parts)
        x = from_wire(exchange(jnp.stack(parts)[..., :lane_count]))
        return [x[n] for n in range(slots)]

    analysis = lax.optimization_barrier(
        fourier_tables(pairs * space, space, truncation, longitudes)
    )
    synthesis = analysis.T
    south = position // split % 2
    hemisphere = jnp.where(south == 0, sin_lat, -sin_lat)
    weights_all = math.pi * jnp.sqrt(1.0 - hemisphere * hemisphere) / (2 * half_lat)
    vmem = pl.BlockSpec(memory_space=pltpu.VMEM)
    modes = 4 * pairs * space

    def grid(k, parts):
        first = k * LANES + position % split * lane_count
        mu = lax.dynamic_slice_in_dim(hemisphere, first, lane_count)
        weight = lax.dynamic_slice_in_dim(weights_all, first, lane_count)
        short = LANES - lane_count
        if short:
            mu = jnp.pad(mu, (0, short))
            weight = jnp.pad(weight, (0, short))
        return pl.pallas_call(
            functools.partial(grid_kernel, scale=1.0 / truncation),
            out_shape=[jax.ShapeDtypeStruct(x.shape, jnp.bfloat16) for x in parts],
            in_specs=[smem] + [vmem] * (4 + space),
            out_specs=[vmem] * space,
            scratch_shapes=[
                pltpu.VMEM((modes, fields * LANES), jnp.bfloat16),
                pltpu.VMEM((longitudes, fields * LANES), jnp.bfloat16),
            ],
            compiler_params=pltpu.CompilerParams(vmem_limit_bytes=60 * mib),
            cost_estimate=pl.CostEstimate(
                flops=4 * modes * longitudes * fields * LANES,
                bytes_accessed=12 * 1024 * 1024,
                transcendentals=0,
            ),
            name="grid",
        )(order, (2.0 * mu)[None], weight[None], synthesis, analysis, *parts)

    def inverse(ws, legs, start, patches, mends, last):
        chunks = len(ws)
        stored = bool(mends)
        wide_scratch = pltpu.VMEM((chunks, tiles * LANES * SUB, LANES), jnp.float32)
        return pl.pallas_call(
            functools.partial(
                inverse_kernel,
                truncation=truncation,
                pairs=padded_pairs,
                chunks=chunks,
                last=last,
                stored=stored,
                slots=slots,
                count=count,
                patches=len(patches) // 2,
                real_pairs=pairs,
                direct=direct,
            ),
            out_shape=jax.ShapeDtypeStruct(state.shape, jnp.float32),
            grid=(steps,),
            in_specs=[smem] * 3
            + [part_spec] * (chunks * slots)
            + ([leg_spec(k) for k in range(chunks)] if stored else [kept_spec] * chunks)
            + [state_spec]
            + [fresh_spec] * len(patches)
            + [mend_spec] * len(mends),
            out_specs=state_spec,
            scratch_shapes=[
                pltpu.VMEM((chunks, 4 * rows * padded_pairs, LANES), jnp.float32),
                pltpu.VMEM((tiles, rows * SUB, LANES), jnp.float32),
            ]
            + ([wide_scratch] if stored else []),
            compiler_params=pltpu.CompilerParams(vmem_limit_bytes=60 * mib),
            cost_estimate=pl.CostEstimate(
                flops=8 * rows * padded_pairs * row_length * LANES * chunks,
                bytes_accessed=20 * 1024 * 1024,
                transcendentals=0,
            ),
            name="inverse",
        )(slot, gravity, stability, *[x for w in ws for x in w], *legs, start, *patches, *mends)

    everything = tuple(range(slots))
    halved = direct and trajectories % 2 == 0
    near, far = everything[: slots // 2], everything[slots // 2 :]
    if halved:
        first = list(forward(0, far, trajectories // 2, None, []))
        second = list(forward(0, near, trajectories // 2, None, []))
    else:
        first = list(forward(0, everything, trajectories, None, []))

    turn, first[0] = lax.optimization_barrier((clones, first[0]))
    made = [second + first if halved else first]
    picked, slot, route = pick_clones(spectra, turn)
    narrow = [send_clone(picked[i], route[i]) for i in range(count)]
    if extra:
        narrow = [jnp.pad(x, ((0, 0), (0, extra), (0, 0))) for x in narrow]
    turn = slot
    for k in range(1, chunk_count):
        made.append(list(forward(k, everything, trajectories, turn, narrow)))
        turn, made[k][0] = lax.optimization_barrier((slot, made[k][0]))
    later, made[-1][0] = lax.optimization_barrier((clones[:, 1], made[-1][0]))
    kept = [x[-1] for x in made[1:]]
    sent = []
    for x in made:
        sent.append(spread(x[:slots]))
    back = []
    for k in range(chunk_count):
        got = grid(k, sent[k])
        back.append(collect(got))
    fresh = [
        share_row(
            lax.dynamic_index_in_dim(spectra, lax.rem(later[i], trajectories), 0, keepdims=False),
            lax.div(later[i], trajectories),
        )
        for i in range(count)
    ]
    fresh = [x for pair in fresh for x in pair]
    if extra:
        fresh = [jnp.pad(x, ((0, 0), (0, extra), (0, 0))) for x in fresh]
    chosen = choose_rows(back[0], clones, trajectories, direct)
    mends = [send_clone(chosen[i], route[i]) for i in range(count)]
    start = inverse(back[:1], [columns], state, [], mends, False)
    for k in range(1, chunk_count - 1):
        start = inverse(back[k : k + 1], kept[k - 1 : k], start, fresh, [], False)
        fresh = []
    out = inverse(back[-1:], kept[-1:], start, fresh, [], True)
    return out[:, :, :pairs] if extra else out


def solution(mesh):
    placed = (P("member", None, "space", None), P("space", None, None), P(), P(), P(), P())
    return jax.shard_map(
        shards,
        mesh=mesh,
        in_specs=placed,
        out_specs=P("member", None, "space", None),
        check_vma=False,
    )
```
